32 devices in a mesh: dp: 4 (over y, x), row: 4 (over z), col: 2 (over core).
Axes of the slice: x: 2, y: 2, z: 4, core: 2. Of those that a mesh axis runs over, the one named last changes fastest.
Arguments:
- tokens: bfloat16 [32768, 1024], P(('dp', 'row'), 'col')
- cotangent: bfloat16 [32768, 1024], P(('dp', 'row'), 'col'), may hold values from -6 to 6
- seq_lens: int32 [4, 2], replicated, may hold values from 2200 to 4096, as said below
- norm1_gain: bfloat16 [1024], P('col'), may hold values from 0.25 to 1.75
- in_weight: bfloat16 [3, 1024, 1024], P(None, 'col', 'row'), may hold values from -0.1875 to 0.1875
- conv_weight: bfloat16 [3, 1024], P(None, 'row'), may hold values from -3.5 to 3.5
- out_weight: bfloat16 [1024, 1024], P('row', 'col'), may hold values from -0.1875 to 0.1875
- norm2_gain: bfloat16 [1024], P('col'), may hold values from 0.25 to 1.75
- gate_up_weight: bfloat16 [2, 1024, 4608], P(None, 'col', 'row'), may hold values from -0.1875 to 0.1875
- down_weight: bfloat16 [4608, 1024], P('row', 'col'), may hold values from -0.09375 to 0.09375
Outputs:
- output: bfloat16 [32768, 1024], P(('dp', 'row'), 'col')
- input_grad: bfloat16 [32768, 1024], P(('dp', 'row'), 'col')
- norm1_gain_grad: float32 [1024], P('col')
- in_weight_grad: float32 [3, 1024, 1024], P(None, 'col', 'row')
- conv_weight_grad: float32 [3, 1024], P(None, 'row')
- out_weight_grad: float32 [1024, 1024], P('row', 'col')
- norm2_gain_grad: float32 [1024], P('col')
- gate_up_weight_grad: float32 [2, 1024, 4608], P(None, 'col', 'row')
- down_weight_grad: float32 [4608, 1024], P('row', 'col')
The draws below stay inside these ranges and needn't reach their ends.
Inputs may be any that keep to these rules, and one draw needn't show every extreme that they name: Each packed row of 8192 slots holds two sequences back to back from its first slot, of lengths seq_lens[q, 0] and seq_lens[q, 1], then padding; some row holds a sequence of 4096 tokens.
All inputs are finite; a program needn't handle non-finite values.
Results may differ from the reference program's by a relative error of at most 0.0085.
Values may be sent and summed in bfloat16 or wider, within the bound.
No kernel may reach another device: no remote copies, remote signals or barrier semaphores. Data moves between devices by JAX's collectives and lax.ppermute only.
A program may use at most 320 MiB of HBM per device.

```python
import jax
import jax.numpy as jnp
from jax import lax

D = 1024
FF = 4608
KCONV = 3
ROW_LEN = 8192
MIN_SEQ = 2200
TOKENS = 32768
PACKED = 4


def draw_tokens(key, part):
    key_base, key_rows, key_cols = jax.random.split(key, 3)
    row_scale = jnp.exp(jax.random.uniform(key_rows, (TOKENS, 1), jnp.float32, -1.15, 1.15))
    col_scale = jnp.exp(jax.random.uniform(key_cols, (1, D), jnp.float32, -1.15, 1.15))
    base = jax.random.normal(key_base, (TOKENS, D), jnp.float32)
    return (base * row_scale * col_scale).astype(jnp.bfloat16)


def draw_seq_lens(key, part):
    key_lens, key_which, key_slot = jax.random.split(key, 3)
    lengths = jax.random.randint(key_lens, (PACKED, 2), MIN_SEQ, ROW_LEN // 2 + 1)
    which = jax.random.randint(key_which, (), 0, PACKED)
    chosen = jax.random.randint(key_slot, (), 0, 2)
    hit = (jnp.arange(PACKED)[:, None] == which) & (jnp.arange(2)[None, :] == chosen)
    return jnp.where(hit, ROW_LEN // 2, lengths).astype(jnp.int32)


def steps_of(stream_key, dims, pieces, least, top_value):
    loudness = 1.0
    for position, blocks in pieces:
        steps = jax.random.uniform(jax.random.fold_in(jax.random.fold_in(stream_key, 6), position), (blocks,), jnp.float32, least / len(pieces), top_value / len(pieces))
        loudness = loudness * jnp.repeat(jnp.exp(steps), dims[position] // blocks).reshape((-1,) + (1,) * (len(dims) - 1 - position))
    return loudness


def gaussian(key, shape, width, reach, shards=(), kind=jnp.bfloat16):
    array = jax.random.normal(key, shape, jnp.float32) * width
    if len(shards) > 0:
        array = steps_of(key, shape, shards, -0.22, 0.18) * array
    return jnp.clip(array, min=-reach, max=reach).astype(kind)


def setup_inputs(seed: int = 0) -> dict:
    arg_keys = jax.random.split(jax.random.key(seed), 11)
    tokens = draw_tokens(jax.random.fold_in(arg_keys[10], 71), 0)
    cotangent = gaussian(arg_keys[1], (TOKENS, D), 1.0, 6.0, ((0, 16), (1, 2)))
    seq_lens = draw_seq_lens(jax.random.fold_in(arg_keys[10], 71), 0)
    norm1_gain = jnp.clip(1.0 + 0.15 * jax.random.normal(arg_keys[3], (D,), jnp.float32), 0.25, 1.75).astype(jnp.bfloat16)
    in_weight = gaussian(arg_keys[4], (3, D, D), D ** -0.5, 0.1875, ((1, 2), (2, 4)))
    conv_weight = gaussian(arg_keys[5], (KCONV, D), KCONV ** -0.5, 3.5, ((1, 4),))
    out_weight = gaussian(arg_keys[6], (D, D), D ** -0.5, 0.1875, ((0, 4), (1, 2)))
    norm2_gain = jnp.clip(1.0 + 0.15 * jax.random.normal(arg_keys[7], (D,), jnp.float32), 0.25, 1.75).astype(jnp.bfloat16)
    gate_up_weight = gaussian(arg_keys[8], (2, D, FF), D ** -0.5, 0.1875, ((1, 2), (2, 4)))
    down_weight = gaussian(arg_keys[9], (FF, D), FF ** -0.5, 0.09375, ((0, 4), (1, 2)))
    return {"tokens": tokens, "cotangent": cotangent, "seq_lens": seq_lens, "norm1_gain": norm1_gain, "in_weight": in_weight, "conv_weight": conv_weight, "out_weight": out_weight, "norm2_gain": norm2_gain, "gate_up_weight": gate_up_weight, "down_weight": down_weight}


eps = 1e-05

@jax.custom_vjp
def low(v):
    return lax.optimization_barrier(v.astype(jnp.bfloat16)).astype(jnp.float32)

@jax.custom_vjp
def low_back(v):
    return v

def low_keep(v):
    return (low(v), None)

def low_pass(kept, grad):
    return (grad,)

def back_keep(v):
    return (v, None)

def back_low(kept, grad):
    return (low(grad),)
low.defvjp(low_keep, low_pass)
low_back.defvjp(back_keep, back_low)

def matmul(left, right):
    return jnp.dot(left, right, precision=lax.Precision.HIGHEST, preferred_element_type=jnp.float32)

def rms_norm(values, gain):
    return values * lax.rsqrt(lax.optimization_barrier(jnp.mean(values * values, axis=1, keepdims=True)) + eps) * gain

def slot_masks(lengths):
    place = jnp.arange(ROW_LEN, dtype=jnp.int32)
    first = lengths[0].astype(jnp.int32)
    second = lengths[1].astype(jnp.int32)
    start = jnp.where(place < first, 0, first)
    valid_slot = (place < first + second).astype(jnp.float32)
    keep_masks = jnp.stack([(place - lag >= start).astype(jnp.float32) for lag in range(KCONV)])
    return (valid_slot, keep_masks)

def delayed(values, lag):
    if lag == 0:
        return values
    padding = jnp.zeros((lag, values.shape[1]), jnp.float32)
    return jnp.concatenate([padding, values[:ROW_LEN - lag]], axis=0)

def block_forward(row_inputs, params, keep_masks):
    gain_first, in_weight, conv_weight, out_weight, gain_second, gate_up_weight, down_weight = params
    normed = low(rms_norm(row_inputs, gain_first))
    gate_b = low_back(matmul(normed, in_weight[0]))
    gate_c = low_back(matmul(normed, in_weight[1]))
    value_part = low_back(matmul(normed, in_weight[2]))
    product = gate_b * value_part
    conv = conv_weight[0] * keep_masks[0][:, None] * product
    for lag in range(1, KCONV):
        conv = conv + conv_weight[lag] * keep_masks[lag][:, None] * delayed(product, lag)
    carried = low(gate_c * conv)
    hidden = row_inputs + low_back(matmul(carried, out_weight))
    normed_two = low(rms_norm(hidden, gain_second))
    gate = low_back(matmul(normed_two, gate_up_weight[0]))
    up_part = low_back(matmul(normed_two, gate_up_weight[1]))
    active = low(jax.nn.silu(gate) * up_part)
    return hidden + low_back(matmul(active, down_weight))

def reference(tokens, cotangent, seq_lens, norm1_gain, in_weight, conv_weight, out_weight, norm2_gain, gate_up_weight, down_weight):
    params = tuple((item.astype(jnp.float32) for item in (norm1_gain, in_weight, conv_weight, out_weight, norm2_gain, gate_up_weight, down_weight)))
    rows_in = tokens.astype(jnp.float32).reshape(PACKED, ROW_LEN, D)
    rows_grad = cotangent.astype(jnp.float32).reshape(PACKED, ROW_LEN, D)

    def one_row(totals, inputs):
        row_inputs, row_grad, lengths = inputs
        valid_slot, keep_masks = slot_masks(lengths)

        def apply_block(values, weights):
            return block_forward(values, weights, keep_masks)
        result, pull = jax.vjp(apply_block, row_inputs, params)
        grad_inputs, grad_params = pull(row_grad * valid_slot[:, None])
        totals = jax.tree.map(lambda left, right: left + right, totals, grad_params)
        return (totals, (result.astype(jnp.bfloat16), grad_inputs.astype(jnp.bfloat16)))
    zeros = tuple((jnp.zeros_like(item) for item in params))
    totals, (results, grads) = lax.scan(one_row, zeros, (rows_in, rows_grad, seq_lens))
    return (results.reshape(TOKENS, D), grads.reshape(TOKENS, D), totals[0], totals[1], totals[2], totals[3], totals[4], totals[5], totals[6])
```

```python
import jax
import jax.numpy as jnp
from jax import lax
from jax.sharding import PartitionSpec as P

KCONV = 3
ROW_LEN = 8192
BLOCKS = 4


eps = 1e-05
bf16 = jnp.bfloat16
f32 = jnp.float32


def dot(left, right):
    return jnp.dot(left, right, preferred_element_type=f32)


def dot_nt(left, right):
    return lax.dot_general(left, right, (((1,), (1,)), ((), ())), preferred_element_type=f32)


def dot_tn(left, right):
    return lax.dot_general(left, right, (((0,), (0,)), ((), ())), preferred_element_type=f32)


def swap_cores(value):
    return lax.ppermute(value, "col", [(0, 1), (1, 0)])


def slot_masks(seq_lens, count):
    flat_rank = (
        lax.axis_index("dp") * lax.axis_size("row") + lax.axis_index("row")
    ) * lax.axis_size("col") + lax.axis_index("col")
    position = flat_rank * count + jnp.arange(count + KCONV - 1, dtype=jnp.int32)
    packed = position // ROW_LEN
    place = position - packed * ROW_LEN
    table = (packed[:, None] == jnp.arange(seq_lens.shape[0], dtype=jnp.int32)[None, :]).astype(
        jnp.int32
    )
    first = jnp.sum(table * seq_lens[None, :, 0], axis=1)
    second = jnp.sum(table * seq_lens[None, :, 1], axis=1)
    start = jnp.where(place < first, 0, first)
    valid_slot = (place < first + second).astype(f32)
    keep_masks = jnp.stack([(place - lag >= start).astype(f32) for lag in range(KCONV)])
    return (valid_slot[:count], keep_masks)


class RingPlan:
    def __init__(self):
        dp, self.row, col = lax.axis_index("dp"), lax.axis_index("row"), lax.axis_index("col")
        low, high = dp % 2, dp // 2
        self.bit_first = jnp.where(col == 0, low, high)
        self.bit_second = jnp.where(col == 0, high, low)
        self.quarter = 2 * self.bit_second + self.bit_first

    def first(self, value):
        return lax.ppermute(
            value, ("dp", "col"), [(2 * p + c, 2 * (p ^ (1 << c)) + c) for p in range(4) for c in range(2)]
        )

    def second(self, value):
        return lax.ppermute(
            value, ("dp", "col"), [(2 * p + c, 2 * (p ^ (2 >> c)) + c) for p in range(4) for c in range(2)]
        )

    def onward(self, value):
        return lax.ppermute(value, "row", [(i, (i + 1) % BLOCKS) for i in range(BLOCKS)])

    def reorder(self, value, axis):
        width = value.shape[axis] // 4
        return jnp.concatenate(
            [
                lax.dynamic_slice_in_dim(value, (self.quarter ^ j) * width, width, axis)
                for j in range(4)
            ],
            axis,
        )

    def gather(self, own):
        own = self.reorder(own, 1)
        moving = own[:, : own.shape[1] // 4]
        halves = []
        for _ in range(BLOCKS - 1):
            moving = self.onward(moving)
            pair = jnp.concatenate([moving, self.first(moving)], axis=1)
            halves.append(jnp.concatenate([pair, self.second(pair)], axis=1))
        halves.append(own)
        return [jnp.concatenate([half, swap_cores(half)], axis=1) for half in halves]

    def reduce(self, block, running):
        half = block.shape[1] // 2
        total = block[:, :half].astype(f32) + swap_cores(block[:, half:]).astype(f32)
        total = total.astype(bf16)
        half //= 2
        total = (total[:, :half].astype(f32) + self.second(total[:, half:]).astype(f32)).astype(bf16)
        half //= 2
        total = total[:, :half].astype(f32) + self.first(total[:, half:]).astype(f32)
        if running is not None:
            total = total + self.onward(running).astype(f32)
        return total.astype(bf16)

    def spread(self, part):
        pair = jnp.concatenate([part, self.first(part)], axis=1)
        half = jnp.concatenate([pair, self.second(pair)], axis=1)
        return self.reorder(half, 1).astype(f32)

    def reduce_blocks(self, blocks):
        running = None
        for block in blocks:
            running = self.reduce(block, running)
        return self.spread(running)

    def ring_order(self, value, axis):
        width = value.shape[axis] // BLOCKS
        return jnp.concatenate(
            [
                lax.dynamic_slice_in_dim(value, (self.row - 1 - j) % BLOCKS * width, width, axis)
                for j in range(BLOCKS)
            ],
            axis,
        )

    def own_block(self, value, axis):
        width = value.shape[axis] // BLOCKS
        return lax.slice_in_dim(value, (BLOCKS - 1) * width, None, axis=axis)

    def shifted(self, value, steps):
        count = lax.axis_size("row") * lax.axis_size("col")
        pairs = [(i, i + steps) for i in range(count) if 0 <= i + steps < count]
        value = lax.ppermute(value, ("row", "col"), pairs)
        width = value.shape[1] // BLOCKS
        crossing = lax.axis_index("col") == (0 if steps > 0 else 1)
        return jnp.where(crossing, jnp.roll(value, steps * width, axis=1), value)


class FlatPlan:
    def reorder(self, value, axis):
        return value

    def gather(self, own):
        half = lax.all_gather(own, "row", axis=2, tiled=True)
        return jnp.split(jnp.concatenate([half, swap_cores(half)], axis=1), BLOCKS, axis=2)

    def reduce_blocks(self, blocks):
        block = jnp.concatenate(blocks, axis=2)
        half = block.shape[1] // 2
        total = block[:, :half].astype(f32) + swap_cores(block[:, half:]).astype(f32)
        total = lax.psum_scatter(total, "row", scatter_dimension=2, tiled=True)
        return lax.psum(total, "dp")

    def ring_order(self, value, axis):
        return value

    def own_block(self, value, axis):
        width = value.shape[axis] // lax.axis_size("row")
        return lax.dynamic_slice_in_dim(value, lax.axis_index("row") * width, width, axis)

    def shifted(self, value, steps):
        count = lax.axis_size("row") * lax.axis_size("col")
        pairs = [(i, i + steps) for i in range(count) if 0 <= i + steps < count]
        return lax.ppermute(value, ("row", "col"), pairs)


def norm_backward(values, rstd, gain, grad_normed):
    scaled = grad_normed * gain
    gain_grad = jnp.sum(grad_normed * values * rstd, axis=0)
    grad_values = rstd * scaled - values * (rstd * rstd * rstd) * jnp.mean(
        scaled * values, axis=1, keepdims=True
    )
    return (grad_values, gain_grad)


def shards(
    plan_of,
    tokens,
    cotangent,
    seq_lens,
    norm1_gain,
    in_weight,
    conv_weight,
    out_weight,
    norm2_gain,
    gate_up_weight,
    down_weight,
):
    plan = plan_of()
    core = lax.axis_index("col")
    count, half_width = tokens.shape[0] // 2, tokens.shape[1]
    reach = KCONV - 1

    def take_tokens(value):
        value = plan.reorder(value, 1)
        own = lax.dynamic_slice_in_dim(value, core * count, count, 0)
        other = lax.dynamic_slice_in_dim(value, (1 - core) * count, count, 0)
        return jnp.concatenate([own, swap_cores(other)], axis=1)

    def give_tokens(value):
        own, other = value[:, :half_width], swap_cores(value[:, half_width:])
        both = jnp.where(
            core == 0, jnp.concatenate([own, other], axis=0), jnp.concatenate([other, own], axis=0)
        )
        return plan.reorder(both, 1)

    def take_gain(gain):
        gain = plan.reorder(gain.astype(f32), 0)
        return jnp.concatenate([gain, swap_cores(gain)], axis=0)

    own_tokens = take_tokens(tokens)
    mix_weights = jnp.concatenate([in_weight, out_weight.T[None]], axis=0)
    feed_weights = jnp.concatenate([gate_up_weight, down_weight.T[None]], axis=0)
    mix_blocks = plan.gather(mix_weights)
    feed_blocks = plan.gather(feed_weights)
    own_cotangent = take_tokens(cotangent)
    gain_one, gain_two = take_gain(norm1_gain), take_gain(norm2_gain)
    taps = plan.ring_order(lax.all_gather(conv_weight.astype(f32), "row", axis=1, tiled=True), 1)
    valid_slot, keep_masks = slot_masks(seq_lens, count)

    inputs = own_tokens.astype(f32)
    rstd_first = lax.rsqrt(jnp.mean(inputs * inputs, axis=1, keepdims=True) + eps)
    normed = (inputs * rstd_first * gain_one).astype(bf16)
    mix = jnp.concatenate(mix_blocks, axis=2)
    gate_b, gate_c, value_part = dot(normed, mix[0]), dot(normed, mix[1]), dot(normed, mix[2])
    product = gate_b * value_part
    extended = jnp.concatenate([plan.shifted(product[count - reach :], 1), product], axis=0)
    conv = jnp.zeros_like(product)
    for lag in range(KCONV):
        conv = (
            conv
            + taps[lag]
            * keep_masks[lag, :count, None]
            * extended[reach - lag : reach - lag + count]
        )
    carried = (gate_c * conv).astype(bf16)
    hidden = inputs + dot_nt(carried, mix[3])
    rstd_second = lax.rsqrt(jnp.mean(hidden * hidden, axis=1, keepdims=True) + eps)
    normed_two = (hidden * rstd_second * gain_two).astype(bf16)

    grad_out = own_cotangent.astype(f32) * valid_slot[:, None]
    grad_low = grad_out.astype(bf16)
    output, grad_normed_two = hidden, jnp.zeros_like(hidden)
    feed_grads = []
    for block in feed_blocks:
        gate, up_part, grad_active = (
            dot(normed_two, block[0]),
            dot(normed_two, block[1]),
            dot(grad_low, block[2]),
        )
        sigmoid_gate = jax.nn.sigmoid(gate)
        silu_gate = gate * sigmoid_gate
        active = (silu_gate * up_part).astype(bf16)
        grad_gate = (
            grad_active * up_part * sigmoid_gate * (1.0 + gate * (1.0 - sigmoid_gate))
        ).astype(bf16)
        grad_up = (grad_active * silu_gate).astype(bf16)
        output = output + dot_nt(active, block[2])
        grad_normed_two = grad_normed_two + dot_nt(grad_gate, block[0]) + dot_nt(grad_up, block[1])
        feed_grads.append(
            jnp.stack(
                [dot_tn(normed_two, grad_gate), dot_tn(normed_two, grad_up), dot_tn(grad_low, active)]
            ).astype(bf16)
        )
    feed_sum = plan.reduce_blocks(feed_grads)
    grad_second, gain_second_part = norm_backward(hidden, rstd_second, gain_two, grad_normed_two)
    grad_hidden = grad_out + grad_second
    grad_o = grad_hidden.astype(bf16)
    grad_carried = dot(grad_o, mix[3])
    grad_gate_c = (grad_carried * conv).astype(bf16)
    grad_conv = grad_carried * gate_c
    grad_extended = jnp.concatenate([grad_conv, plan.shifted(grad_conv[:reach], -1)], axis=0)
    grad_product = jnp.zeros_like(product)
    conv_rows = []
    for lag in range(KCONV):
        masked = keep_masks[lag, :, None] * grad_extended
        grad_product = grad_product + taps[lag] * masked[lag : lag + count]
        conv_rows.append(
            jnp.sum(masked[:count] * extended[reach - lag : reach - lag + count], axis=0)
        )
    grad_gate_b = (grad_product * value_part).astype(bf16)
    grad_value = (grad_product * gate_b).astype(bf16)
    mix_grad = jnp.stack(
        [
            dot_tn(normed, grad_gate_b),
            dot_tn(normed, grad_gate_c),
            dot_tn(normed, grad_value),
            dot_tn(grad_o, carried),
        ]
    ).astype(bf16)
    mix_sum = plan.reduce_blocks(jnp.split(mix_grad, BLOCKS, axis=2))
    grad_normed = (
        dot_nt(grad_gate_b, mix[0]) + dot_nt(grad_gate_c, mix[1]) + dot_nt(grad_value, mix[2])
    )
    grad_first, gain_first_part = norm_backward(inputs, rstd_first, gain_one, grad_normed)
    input_grad = (grad_hidden + grad_first).astype(bf16)
    output_back, input_back = give_tokens(output.astype(bf16)), give_tokens(input_grad)

    def whole_gain(part):
        own = part[:half_width] + swap_cores(part[half_width:])
        return plan.reorder(own, 0)

    gain_one_sum, gain_two_sum = lax.psum(
        (whole_gain(gain_first_part), whole_gain(gain_second_part)), ("dp", "row")
    )
    conv_sum = plan.ring_order(jnp.stack(conv_rows), 1)
    conv_sum = lax.psum(conv_sum, ("dp", "row", "col"))
    block_width = conv_weight.shape[1]
    conv_grad = lax.dynamic_slice_in_dim(
        conv_sum, lax.axis_index("row") * block_width, block_width, axis=1
    )
    return (
        output_back,
        input_back,
        gain_one_sum,
        mix_sum[:3],
        conv_grad,
        mix_sum[3].T,
        gain_two_sum,
        feed_sum[:2],
        feed_sum[2].T,
    )


def solution(mesh):
    ring = mesh.shape["dp"] == 4 and mesh.shape["row"] == BLOCKS and mesh.shape["col"] == 2
    plan_of = RingPlan if ring else FlatPlan

    def local(*arrays):
        return shards(plan_of, *arrays)

    return jax.shard_map(
        local,
        mesh=mesh,
        in_specs=(
            P(("dp", "row"), "col"),
            P(("dp", "row"), "col"),
            P(),
            P("col"),
            P(None, "col", "row"),
            P(None, "row"),
            P("row", "col"),
            P("col"),
            P(None, "col", "row"),
            P("row", "col"),
        ),
        out_specs=(
            P(("dp", "row"), "col"),
            P(("dp", "row"), "col"),
            P("col"),
            P(None, "col", "row"),
            P(None, "row"),
            P("row", "col"),
            P("col"),
            P(None, "col", "row"),
            P("row", "col"),
        ),
        check_vma=False,
    )
```

```python
import functools

import jax
import jax.numpy as jnp
from jax import lax
from jax.experimental import pallas as pl
from jax.experimental.pallas import tpu as pltpu
from jax.sharding import PartitionSpec as P

KCONV = 3
ROW_LEN = 8192
BLOCKS = 4
OFFSETS = (0, -1, 1, 2)
HALO = 16
STEP = 256


eps = 1e-05
bf16 = jnp.bfloat16
f32 = jnp.float32
VMEM_LIMIT = 64000 * 1024
HERE = pl.BlockSpec(memory_space=pl.ANY)
SCALARS = pl.BlockSpec(memory_space=pltpu.SMEM)


def dot(left, right):
    return jnp.dot(left, right, preferred_element_type=f32)


def dot_nt(left, right):
    return lax.dot_general(left, right, (((1,), (1,)), ((), ())), preferred_element_type=f32)


def shape_of(*dims, dtype=bf16):
    return jax.ShapeDtypeStruct(dims, dtype)


def call(body, name, out_shape, flops=0, moved=0, tie=(), n_in=None, **kwargs):
    if tie:
        inner, at = body, n_in

        def body(*refs):
            inner(*refs[:at], *refs[at + len(tie) :])

        if "grid_spec" in kwargs:
            spec = kwargs["grid_spec"]
            kwargs["grid_spec"] = pltpu.PrefetchScalarGridSpec(
                num_scalar_prefetch=1,
                grid=spec.grid,
                in_specs=list(spec.in_specs) + [HERE] * len(tie),
                out_specs=spec.out_specs,
                scratch_shapes=spec.scratch_shapes,
            )
        else:
            kwargs["in_specs"] = list(kwargs["in_specs"]) + [HERE] * len(tie)
    return pl.pallas_call(
        body,
        out_shape=out_shape,
        name=name,
        compiler_params=pltpu.CompilerParams(vmem_limit_bytes=VMEM_LIMIT),
        cost_estimate=pl.CostEstimate(flops=flops, bytes_accessed=moved, transcendentals=0),
        **kwargs,
    )


def scalar_grid(grid, in_specs, out_specs, scratch_shapes=()):
    return pltpu.PrefetchScalarGridSpec(
        num_scalar_prefetch=1,
        grid=grid,
        in_specs=in_specs,
        out_specs=out_specs,
        scratch_shapes=scratch_shapes,
    )


def quarter_of(place, j):
    dp, core = place[0], place[1]
    low, high = j % 2, j // 2
    mask = jnp.where(core == 0, 2 * high + low, 2 * low + high)
    return jnp.bitwise_xor(dp, mask)


def join_tokens(mine, theirs, place):
    count, half = mine.shape

    def body(place, mine, theirs, out):
        own = pl.program_id(0) == place[1]

        @pl.when(own)
        def _():
            out[...] = mine[...]

        @pl.when(jnp.logical_not(own))
        def _():
            out[...] = theirs[...]

    kept = pl.BlockSpec((count, half), lambda h, place: (0, 0))
    return call(
        body,
        "join_tokens",
        shape_of(2 * count, half),
        grid_spec=scalar_grid(
            (2,), [kept, kept], pl.BlockSpec((count, half), lambda h, place: (h, 0))
        ),
    )(place, mine, theirs)


def outgoing(place, tokens, cotangent, before, gains):
    count, half = tokens.shape[0] // 2, tokens.shape[1]
    rows = 2 * count + 2 * HALO

    def body(place, tokens, cotangent, between, before, gains, out):
        out[:count] = tokens[...]
        out[count : 2 * count] = cotangent[...]

        @pl.when(place[1] == 0)
        def _():
            out[2 * count : 2 * count + HALO] = between[...]

        @pl.when(place[1] == 1)
        def _():
            out[2 * count : 2 * count + HALO] = before[...]

        out[2 * count + HALO :] = gains[...]

    theirs = pl.BlockSpec((count, half), lambda i, place: (1 - place[1], 0))
    few = pl.BlockSpec((HALO, half), lambda i, place: (0, 0))
    return call(
        body,
        "outgoing",
        shape_of(rows, half),
        grid_spec=scalar_grid(
            (1,),
            [theirs, theirs, pl.BlockSpec((HALO, half), lambda i, place: (count // HALO - 1, 0)), few, few],
            pl.BlockSpec((rows, half), lambda i, place: (0, 0)),
        ),
    )(place, tokens, cotangent, tokens, before, gains)


def pack(stack, turned, place, quarters, rows=None, tie=()):
    k, half, n = stack.shape
    width = half // 4
    lanes = (k + 1) * n
    below = [] if rows is None else [rows]

    def body(place, stack, turned, *refs):
        out = refs[-1]
        for i in range(k):
            out[:width, i * n : (i + 1) * n] = stack[i]
        out[:width, k * n :] = turned[...].astype(f32).T.astype(out.dtype)
        if below:
            out[width:, :] = jnp.zeros((HALO, lanes), out.dtype)
            out[width : width + KCONV, :n] = refs[0][...]

    def source(j, place):
        return place[0] if quarters == 1 else j

    return call(
        body,
        "pack",
        shape_of(quarters * width + HALO * len(below), lanes),
        tie=tie,
        n_in=3 + len(below),
        grid_spec=scalar_grid(
            (quarters,),
            [
                pl.BlockSpec((k, width, n), lambda j, place: (0, source(j, place), 0)),
                pl.BlockSpec((n, width), lambda j, place: (0, source(j, place))),
            ]
            + [pl.BlockSpec((KCONV, n), lambda j, place: (0, 0))] * len(below),
            pl.BlockSpec((width + HALO * len(below), lanes), lambda j, place: (j, 0)),
        ),
    )(place, stack, turned, *below, *tie)


def join_rows(parts, tie):
    rows, lanes = parts[0].shape

    def body(*refs):
        for i in range(len(parts)):
            refs[-1][i * rows : (i + 1) * rows] = refs[i][...]

    whole = pl.BlockSpec(memory_space=pltpu.VMEM)
    return call(
        body,
        "join_rows",
        shape_of(len(parts) * rows, lanes),
        tie=tie,
        n_in=len(parts),
        in_specs=[whole] * len(parts),
        out_specs=whole,
    )(*parts, *tie)


def mix_assemble(own, pieces, place, tie):
    half, lanes = own.shape
    width = half // 4
    stride = width + HALO

    def body(place, own, *refs):
        out = refs[-1]
        out[0] = own[...]
        for s in range(1, BLOCKS):
            for j in range(4):
                rows = pl.ds(pl.multiple_of(quarter_of(place, j) * width, width), width)
                out[s, rows, :] = refs[j][(s - 1) * stride : (s - 1) * stride + width, :]

    whole = pl.BlockSpec(memory_space=pltpu.VMEM)
    return call(
        body,
        "mix_assemble",
        shape_of(BLOCKS, half, lanes),
        tie=tie,
        n_in=6,
        in_specs=[SCALARS] + [whole] * 5,
        out_specs=whole,
    )(place, own, *pieces, *tie)


def unpack(pieces, k, place):
    width, lanes = pieces[0].shape
    half, n = 4 * width, lanes // (k + 1)

    def body(place, *refs):
        stack, turned = refs[4:]
        for j in range(4):

            @pl.when(pl.program_id(0) == j)
            def _(piece=refs[j]):
                for i in range(k):
                    stack[i] = piece[:, i * n : (i + 1) * n].astype(f32)
                turned[...] = piece[:, k * n :].astype(f32).T

    whole = pl.BlockSpec((width, lanes), lambda j, place: (0, 0))
    return call(
        body,
        "unpack",
        (shape_of(k, half, n, dtype=f32), shape_of(n, half, dtype=f32)),
        grid_spec=scalar_grid(
            (4,),
            [whole] * 4,
            [
                pl.BlockSpec((k, width, n), lambda j, place: (0, quarter_of(place, j), 0)),
                pl.BlockSpec((n, width), lambda j, place: (0, quarter_of(place, j))),
            ],
        ),
    )(place, *pieces)


def rows_of(i, step=STEP):
    return pl.ds(pl.multiple_of(i * step, step), step)


def slots(place, start, count):
    slot = place[2] + start + lax.broadcasted_iota(jnp.int32, (count, 1), 0)
    return slot, jnp.where(slot < place[3], 0, place[3])


def inverse_rms(*parts):
    width = sum(part.shape[1] for part in parts)
    total = sum(jnp.sum(part * part, axis=1, keepdims=True) for part in parts)
    return lax.rsqrt(total / width + eps)


def prepare(place, tokens, theirs, before, cotangent, gain, tie):
    count, half = tokens.shape[0] // 2, tokens.shape[1]
    width = 2 * half

    def body(
        place, own, other, before, between, halo_other, cot, cot_other, gain, normed, normed_t, low, low_t
    ):
        def norm(left, right):
            left, right = left.astype(f32), right.astype(f32)
            rstd = inverse_rms(left, right)
            return (
                (left * rstd * gain[:, :half]).astype(bf16),
                (right * rstd * gain[:, half:]).astype(bf16),
            )

        halo = jnp.where(place[1] == 0, before[...].astype(f32), between[...].astype(f32))

        @pl.when(pl.program_id(0) == 0)
        def _():
            left, right = norm(halo, halo_other[...])
            normed[:HALO, :half] = left
            normed[:HALO, half:] = right

        tile = pl.program_id(0)
        here = pl.ds(pl.multiple_of(HALO + tile * STEP, HALO), STEP)
        for i, value in enumerate(norm(own[...], other[...])):
            lanes = slice(i * half, (i + 1) * half)
            normed[here, lanes] = value
            normed_t[lanes, :] = value.astype(f32).T.astype(bf16)
        slot, _ = slots(place, tile * STEP, STEP)
        valid = (slot < place[4]).astype(f32)
        for i, value in enumerate((cot[...], cot_other[...])):
            lanes = slice(i * half, (i + 1) * half)
            value = value.astype(f32) * valid
            low[:, lanes] = value.astype(bf16)
            low_t[lanes, :] = value.T.astype(bf16)

    tiles = count // STEP
    mine = pl.BlockSpec((STEP, half), lambda m, place: (place[1] * tiles + m, 0))

    def received(first):
        return pl.BlockSpec((STEP, half), lambda m, place: (first + m, 0))

    def few(block):
        return pl.BlockSpec((HALO, half), lambda m, place: (block, 0))

    turned = pl.BlockSpec((width, STEP), lambda m, place: (0, m))
    return call(
        body,
        "prepare",
        (
            shape_of(HALO + count, width),
            shape_of(width, count),
            shape_of(count, width),
            shape_of(width, count),
        ),
        moved=16 * count * width,
        tie=tie,
        n_in=9,
        grid_spec=scalar_grid(
            (tiles,),
            [
                mine,
                received(0),
                few(0),
                few(count // HALO - 1),
                few(2 * count // HALO),
                mine,
                received(tiles),
                pl.BlockSpec((1, width), lambda m, place: (0, 0)),
            ],
            [
                pl.BlockSpec((HALO + count, width), lambda m, place: (0, 0)),
                turned,
                pl.BlockSpec((STEP, width), lambda m, place: (m, 0)),
                turned,
            ],
        ),
    )(place, tokens, theirs, before, tokens, theirs, cotangent, theirs, gain, *tie)


def mix_copies(sources, inward, outward, sems):
    copies = []
    for s in range(BLOCKS):
        for side in range(2):
            source = sources[side].at[s]
            half, lanes = source.shape
            n = lanes // 4
            rows = pl.ds(side * half, half)
            at = 4 * s + 2 * side
            copies.append(
                pltpu.make_async_copy(
                    source.at[:, pl.ds(0, 3 * n)],
                    inward.at[rows, pl.ds(s * 3 * n, 3 * n)],
                    sems.at[at],
                )
            )
            copies.append(
                pltpu.make_async_copy(
                    source.at[:, pl.ds(3 * n, n)],
                    outward.at[rows, pl.ds(s * n, n)],
                    sems.at[at + 1],
                )
            )
    return copies


def mix_forward(place, normed, halves, tokens, theirs, taps, gain, tie):
    count, half = tokens.shape[0] // 2, tokens.shape[1]
    width = 2 * half
    n = width // BLOCKS
    part = (HALO + count) // 5
    kept = 4

    def body(place, *refs):
        normed_hbm, sources, refs = refs[0], refs[1:3], refs[3:]
        tokens_hbm, theirs_hbm, taps, gain = refs[:4]
        results, hidden_hbm, carried_hbm, normed2_hbm, turned_hbm = (
            refs[4:8],
            refs[8],
            refs[9],
            refs[10],
            refs[11],
        )
        normed, inward, outward, mine, other, mixed, product, carried, hidden, normed2, turned = refs[
            12:23
        ]
        saved = refs[23:27]
        in_sems, weight_sems, saved_sems, out_sems = refs[27:]
        loads = [
            pltpu.make_async_copy(normed_hbm, normed, in_sems.at[0]),
            pltpu.make_async_copy(
                tokens_hbm.at[pl.ds(pl.multiple_of(place[1] * count, count), count)],
                mine,
                in_sems.at[1],
            ),
            pltpu.make_async_copy(theirs_hbm.at[pl.ds(0, count)], other, in_sems.at[2]),
        ]
        weights = mix_copies(sources, inward, outward, weight_sems)
        loads[0].start()
        for copy in weights:
            copy.start()
        loads[1].start()
        loads[2].start()
        loads[0].wait()
        pending = []
        for s in range(BLOCKS):
            for copy in weights[4 * s : 4 * s + 4]:
                copy.wait()

            def project(i, carry, s=s):
                rows = rows_of(i, part)
                value = dot(normed[rows, :], inward[:, s * 3 * n : (s + 1) * 3 * n])
                mixed[rows, :] = value
                product[rows, :] = value[:, :n] * value[:, 2 * n :]
                return carry

            lax.fori_loop(0, 5, project, 0)
            lanes = slice(s * n, (s + 1) * n)
            for m in range(count // STEP):
                first = HALO + m * STEP
                rows = slice(m * STEP, (m + 1) * STEP)
                slot, start = slots(place, m * STEP, STEP)
                conv = jnp.zeros((STEP, n), f32)
                for lag in range(KCONV):
                    keep = (slot - lag >= start).astype(f32)
                    conv = conv + taps[lag : lag + 1, lanes] * (
                        keep * product[first - lag : first - lag + STEP, :]
                    )
                inside = mixed[first : first + STEP, :]
                carried[rows, lanes] = (inside[:, n : 2 * n] * conv).astype(bf16)
                for i, value in enumerate((inside[:, :n], inside[:, n : 2 * n], inside[:, 2 * n :], conv)):
                    saved[i][rows, lanes] = value.astype(bf16)
            for i in range(kept):
                copy = pltpu.make_async_copy(
                    saved[i].at[:, pl.ds(s * n, n)],
                    results[i].at[:, pl.ds(s * n, n)],
                    saved_sems.at[kept * s + i],
                )
                copy.start()
                pending.append(copy)
        copy = pltpu.make_async_copy(carried, carried_hbm, in_sems.at[3])
        copy.start()
        pending.append(copy)
        loads[1].wait()
        loads[2].wait()
        for m in range(count // STEP):
            rows = slice(m * STEP, (m + 1) * STEP)
            term = dot_nt(carried[rows, :], outward[...])
            left = mine[rows, :].astype(f32) + term[:, :half]
            right = other[rows, :].astype(f32) + term[:, half:]
            rstd = inverse_rms(left, right)
            for i, value in enumerate((left, right)):
                lanes = slice(i * half, (i + 1) * half)
                hidden[rows, lanes] = value
                value = value * rstd * gain[:, lanes]
                normed2[rows, lanes] = value.astype(bf16)
                turned[lanes, rows] = value.T.astype(bf16)
            for i, (source, target, by) in enumerate(
                (
                    (hidden, hidden_hbm, 0),
                    (normed2, normed2_hbm, 0),
                    (turned, turned_hbm, 1),
                )
            ):
                here = pl.ds(m * STEP, STEP)
                source, target = (
                    (source.at[:, here], target.at[:, here])
                    if by
                    else (source.at[here], target.at[here])
                )
                copy = pltpu.make_async_copy(source, target, out_sems.at[3 * m + i])
                copy.start()
                pending.append(copy)
        for copy in pending:
            copy.wait()

    tiles = count // STEP
    wide = shape_of(count, width, dtype=f32)
    flat = shape_of(count, width)
    whole = pl.BlockSpec(memory_space=pltpu.VMEM)
    return call(
        body,
        "mix_forward",
        (flat, flat, flat, flat, wide, flat, flat, shape_of(width, count)),
        flops=8 * count * width * width,
        moved=30 * count * width + 8 * width * width,
        tie=tie,
        n_in=8,
        in_specs=[SCALARS] + [HERE] * 5 + [whole] * 2,
        out_specs=(HERE,) * 8,
        scratch_shapes=[
            pltpu.VMEM((HALO + count, width), bf16),
            pltpu.VMEM((width, 3 * width), bf16),
            pltpu.VMEM((width, width), bf16),
            pltpu.VMEM((count, half), bf16),
            pltpu.VMEM((count, half), bf16),
            pltpu.VMEM((HALO + count, 3 * n), f32),
            pltpu.VMEM((HALO + count, n), f32),
            pltpu.VMEM((count, width), bf16),
            pltpu.VMEM((count, width), f32),
            pltpu.VMEM((count, width), bf16),
            pltpu.VMEM((width, count), bf16),
        ]
        + [pltpu.VMEM((count, width), bf16)] * kept
        + [
            pltpu.SemaphoreType.DMA((4,)),
            pltpu.SemaphoreType.DMA((4 * BLOCKS,)),
            pltpu.SemaphoreType.DMA((kept * BLOCKS,)),
            pltpu.SemaphoreType.DMA((3 * tiles,)),
        ],
    )(place, normed, *halves, tokens, theirs, taps, gain, *tie)


def feed_body(
    lanes,
    started,
    normed_hbm,
    low_hbm,
    normed_t_hbm,
    low_t_hbm,
    own_hbm,
    other_hbm,
    grad_in,
    grad_hbm,
    acts_hbm,
    theirs_hbm,
    normed,
    low,
    normed_t,
    low_t,
    weights,
    grad,
    acts,
    theirs,
    in_sems,
    grad_sems,
    acts_sems,
    their_sems,
):
    f = lanes // 3
    count, width = normed.shape
    half = width // 2
    loads = [
        pltpu.make_async_copy(source, target, in_sems.at[i])
        for i, (source, target) in enumerate(
            (
                (normed_hbm, normed),
                (own_hbm, weights.at[pl.ds(0, half)]),
                (other_hbm, weights.at[pl.ds(half, half)]),
                (low_hbm, low),
                (normed_t_hbm.at[pl.ds(half, half)], normed_t),
                (low_t_hbm.at[pl.ds(half, half)], low_t),
            )
        )
    ]
    if started:
        loads.append(pltpu.make_async_copy(grad_in, grad, in_sems.at[6]))
    for load in loads[:4]:
        load.start()
    for load in loads[:4]:
        load.wait()
    for load in loads[4:]:
        load.start()

    def acts_copy(i):
        rows = rows_of(i)
        return pltpu.make_async_copy(acts.at[rows], acts_hbm.at[rows], acts_sems.at[i])

    def activations(i, carry):
        rows = rows_of(i)
        for start in range(0, f, 256):
            stop = min(start + 256, f)
            gate_lanes = slice(start, stop)
            up_lanes = slice(f + start, f + stop)
            down_lanes = slice(2 * f + start, 2 * f + stop)
            gate = dot(normed[rows, :], weights[:, gate_lanes])
            up_part = dot(normed[rows, :], weights[:, up_lanes])
            grad_active = dot(low[rows, :], weights[:, down_lanes])
            sigmoid_gate = jax.nn.sigmoid(gate)
            silu_gate = gate * sigmoid_gate
            acts[rows, gate_lanes] = (
                grad_active * up_part * sigmoid_gate * (1.0 + gate * (1.0 - sigmoid_gate))
            ).astype(bf16)
            acts[rows, up_lanes] = (grad_active * silu_gate).astype(bf16)
            acts[rows, down_lanes] = (silu_gate * up_part).astype(bf16)
        acts_copy(i).start()
        return carry

    lax.fori_loop(0, count // STEP, activations, 0)
    loads[4].wait()
    loads[5].wait()

    def their_copy(i):
        rows = rows_of(i)
        return pltpu.make_async_copy(theirs.at[rows], theirs_hbm.at[rows], their_sems.at[i])

    def outer(i, carry):
        rows = rows_of(i)
        theirs[rows, : 2 * f] = dot(normed_t[rows, :], acts[:, : 2 * f]).astype(bf16)
        theirs[rows, 2 * f :] = dot(low_t[rows, :], acts[:, 2 * f :]).astype(bf16)
        their_copy(i).start()
        return carry

    lax.fori_loop(0, half // STEP, outer, 0)
    if started:
        loads[6].wait()

    def grad_copy(i):
        rows = rows_of(i)
        return pltpu.make_async_copy(grad.at[rows], grad_hbm.at[rows], grad_sems.at[i])

    def inner(i, carry):
        rows = rows_of(i)
        term = dot_nt(acts[rows, : 2 * f], weights[:, : 2 * f])
        grad[rows, :] = grad[rows, :] + term if started else term
        grad_copy(i).start()
        return carry

    lax.fori_loop(0, count // STEP, inner, 0)
    for i in range(half // STEP):
        their_copy(i).wait()
    for i in range(count // STEP):
        acts_copy(i).wait()
        grad_copy(i).wait()


def feed(normed, low, normed_t, low_t, own, other, grad, tie):
    count, width = normed.shape
    half, lanes = own.shape
    f = lanes // 3
    started = grad is not None
    tiles = count // STEP
    before = [grad] if started else []
    body = functools.partial(feed_body, lanes, started)
    if not started:
        inner = body

        def body(*refs):
            inner(*refs[:6], None, *refs[6:])

    return call(
        body,
        "feed",
        (shape_of(count, width, dtype=f32), shape_of(count, lanes), shape_of(half, lanes)),
        flops=13 * count * width * f,
        moved=2 * (4 * count * width + 3 * half * lanes + count * lanes) + 8 * count * width,
        tie=tie,
        n_in=6 + len(before),
        in_specs=[HERE] * (6 + len(before)),
        out_specs=(HERE,) * 3,
        scratch_shapes=[
            pltpu.VMEM((count, width), bf16),
            pltpu.VMEM((count, width), bf16),
            pltpu.VMEM((half, count), bf16),
            pltpu.VMEM((half, count), bf16),
            pltpu.VMEM((width, lanes), bf16),
            pltpu.VMEM((count, width), f32),
            pltpu.VMEM((count, lanes), bf16),
            pltpu.VMEM((half, lanes), bf16),
            pltpu.SemaphoreType.DMA((7,)),
            pltpu.SemaphoreType.DMA((tiles,)),
            pltpu.SemaphoreType.DMA((tiles,)),
            pltpu.SemaphoreType.DMA((half // STEP,)),
        ],
    )(normed, low, normed_t, low_t, own, other, *before, *tie)


def feed_output(hidden, acts, owns, others, tie):
    count, width = hidden.shape
    half, lanes = owns[0].shape
    f = lanes // 3

    def body(hidden, *refs):
        acts, owns, others, outs = refs[:4], refs[4:8], refs[8:12], refs[12:]
        for side, weights in enumerate((owns, others)):
            total = hidden[:, side * half : (side + 1) * half]
            for k in range(BLOCKS):
                total = total + dot_nt(acts[k][...], weights[k][...])
            outs[side][...] = total.astype(bf16)

    rows = pl.BlockSpec((STEP, f), lambda m: (m, 2))
    whole = pl.BlockSpec((half, f), lambda m: (0, 2))
    part = pl.BlockSpec((STEP, half), lambda m: (m, 0))
    return call(
        body,
        "feed_output",
        (shape_of(count, half),) * 2,
        flops=2 * BLOCKS * count * width * f,
        moved=2 * BLOCKS * (count + width) * f + 6 * count * width,
        tie=tie,
        n_in=13,
        grid=(count // STEP,),
        in_specs=[pl.BlockSpec((STEP, width), lambda m: (m, 0))] + [rows] * 4 + [whole] * 8,
        out_specs=(part, part),
    )(hidden, *acts, *owns, *others, *tie)


def keep_and_send(place, total, keep, send):
    width = keep.shape[0] // 2
    for j in range(4):
        target = keep if j < 2 else send
        rows = pl.ds(pl.multiple_of(quarter_of(place, j) * width, width), width)
        target[(j % 2) * width : (j % 2 + 1) * width, :] = total[rows, :].astype(bf16)


def feed_weights(place, normed_t, low_t, acts, received, tie):
    width, count = normed_t.shape
    half, lanes = received.shape
    f = lanes // 3
    step = f

    def body(place, normed_t, low_t, acts, received, keep, send, total):
        def put(left):
            total[...] = dot(left[...], acts[...]) + received[...].astype(f32)

        is_down = pl.program_id(0) >= 2 * f // step

        @pl.when(jnp.logical_not(is_down))
        def _():
            put(normed_t)

        @pl.when(is_down)
        def _():
            put(low_t)

        keep_and_send(place, total, keep, send)

    left = pl.BlockSpec((half, count), lambda j, place: (0, 0))
    part = pl.BlockSpec((half // 2, step), lambda j, place: (0, j))
    return call(
        body,
        "feed_weights",
        (shape_of(half // 2, lanes),) * 2,
        flops=6 * count * half * f,
        moved=2 * (2 * half * count + count * lanes + 2 * half * lanes),
        tie=tie,
        n_in=5,
        grid_spec=scalar_grid(
            (lanes // step,),
            [
                left,
                left,
                pl.BlockSpec((count, step), lambda j, place: (0, j)),
                pl.BlockSpec((half, step), lambda j, place: (0, j)),
            ],
            [part, part],
            [pltpu.VMEM((half, step), f32)],
        ),
    )(place, normed_t, low_t, acts, received, *tie)


def hidden_backward(hidden, grad_normed, grad_out, gain):
    width = hidden.shape[1]
    rstd = lax.rsqrt(jnp.sum(hidden * hidden, axis=1, keepdims=True) / width + eps)
    scaled = grad_normed * gain
    mean = jnp.sum(scaled * hidden, axis=1, keepdims=True) / width
    grad = grad_out + (rstd * scaled - hidden * (rstd * rstd * rstd) * mean)
    return grad, grad_normed * hidden * rstd


def first_rows(hidden, grad_normed, low, gate_c, gain, halves):
    width = hidden.shape[1]
    n = width // BLOCKS
    half = width // 2

    def body(hidden, grad_normed, low, gate_c, gain, *refs):
        grad, _ = hidden_backward(hidden[...], grad_normed[...], low[...].astype(f32), gain[...])
        grad_o = grad.astype(bf16)
        for s in range(BLOCKS):
            value = dot(grad_o[:, :half], refs[0][s]) + dot(grad_o[:, half:], refs[1][s])
            lanes = slice(s * n, (s + 1) * n)
            refs[-1][:, lanes] = (value * gate_c[:, lanes].astype(f32))[:8]

    few = pl.BlockSpec((HALO, width), lambda i: (0, 0))
    return call(
        body,
        "first_rows",
        shape_of(8, width, dtype=f32),
        grid=(1,),
        in_specs=[few] * 4
        + [pl.BlockSpec((1, width), lambda i: (0, 0))]
        + [pl.BlockSpec((BLOCKS, half, n), lambda i: (0, 0, 3))] * 2,
        out_specs=pl.BlockSpec((8, width), lambda i: (0, 0)),
    )(hidden, grad_normed, low, gate_c, gain, *halves)


def mix_backward(
    place, hidden, grad_normed, low, tokens, theirs, saved, later, taps, gain_one, gain_two, halves, tie
):
    count, width = hidden.shape
    half = width // 2
    n = width // BLOCKS
    tiles = count // STEP

    def body(place, *refs):
        hidden, grad_normed, low, mine, other = refs[:5]
        gate_b, gate_c, value_part, conv, later, taps, gain_one, gain_two = refs[5:13]
        sources = refs[13:15]
        grad_own, grad_other, grads, turned, sums = refs[15:20]
        inward, outward, extended, sems = refs[20:]
        step = pl.program_id(0)
        tile = tiles - 1 - step

        @pl.when(step == 0)
        def _():
            copies = mix_copies(sources, inward, outward, sems)
            for copy in copies:
                copy.start()
            sums[...] = jnp.zeros_like(sums)
            extended[STEP:, :] = later[...]
            for copy in copies:
                copy.wait()

        @pl.when(step > 0)
        def _():
            extended[STEP:, :] = extended[:8, :]

        grad, gain_terms = hidden_backward(
            hidden[...], grad_normed[...], low[...].astype(f32), gain_two[...]
        )
        sums[1:2, :] += jnp.sum(gain_terms, axis=0, keepdims=True)
        grad_o = grad.astype(bf16)
        turned[...] = grad.T.astype(bf16)
        grad_carried = dot(grad_o, outward[...])
        extended[:STEP, :] = grad_carried * gate_c[...].astype(f32)
        grad_c = (grad_carried * conv[...].astype(f32)).astype(bf16)
        left_gate, right_gate = gate_b[...].astype(f32), value_part[...].astype(f32)
        product = left_gate * right_gate
        grad_product = jnp.zeros((STEP, width), f32)
        for lag in range(KCONV):
            slot, start = slots(place, tile * STEP + lag, STEP)
            keep = (slot - lag >= start).astype(f32)
            masked = keep * extended[lag : lag + STEP, :]
            grad_product = grad_product + taps[lag : lag + 1, :] * masked
            sums[2 + lag : 3 + lag, :] += jnp.sum(masked * product, axis=0, keepdims=True)
        grad_b = (grad_product * right_gate).astype(bf16)
        grad_v = (grad_product * left_gate).astype(bf16)
        for s in range(BLOCKS):
            lanes = slice(s * n, (s + 1) * n)
            at = s * 3 * n
            grads[:, at : at + n] = grad_b[:, lanes]
            grads[:, at + n : at + 2 * n] = grad_c[:, lanes]
            grads[:, at + 2 * n : at + 3 * n] = grad_v[:, lanes]
        grad_first = dot_nt(grads[...], inward[...])
        left, right = mine[...].astype(f32), other[...].astype(f32)
        rstd = inverse_rms(left, right)
        scaled = grad_first * gain_one[...]
        mean = (
            jnp.sum(scaled[:, :half] * left, axis=1, keepdims=True)
            + jnp.sum(scaled[:, half:] * right, axis=1, keepdims=True)
        ) / width
        for i, (value, target) in enumerate(((left, grad_own), (right, grad_other))):
            lanes = slice(i * half, (i + 1) * half)
            sums[0:1, lanes] += jnp.sum(grad_first[:, lanes] * value * rstd, axis=0, keepdims=True)
            target[...] = (
                grad[:, lanes] + (rstd * scaled[:, lanes] - value * (rstd * rstd * rstd) * mean)
            ).astype(bf16)

    def tile_of(m):
        return tiles - 1 - m

    rows = pl.BlockSpec((STEP, width), lambda m, place: (tile_of(m), 0))
    one = pl.BlockSpec((1, width), lambda m, place: (0, 0))
    eight = pl.BlockSpec((8, width), lambda m, place: (0, 0))
    narrow = pl.BlockSpec((STEP, half), lambda m, place: (tile_of(m), 0))
    return call(
        body,
        "mix_backward",
        (
            shape_of(count, half),
            shape_of(count, half),
            shape_of(count, 3 * width),
            shape_of(width, count),
            shape_of(8, width, dtype=f32),
        ),
        flops=8 * count * width * width,
        moved=44 * count * width,
        tie=tie,
        n_in=16,
        grid_spec=scalar_grid(
            (tiles,),
            [
                rows,
                rows,
                rows,
                pl.BlockSpec(
                    (STEP, half), lambda m, place: (place[1] * tiles + tile_of(m), 0)
                ),
                narrow,
                rows,
                rows,
                rows,
                rows,
                eight,
                pl.BlockSpec((KCONV, width), lambda m, place: (0, 0)),
                one,
                one,
            ]
            + [HERE] * 2,
            [
                narrow,
                narrow,
                pl.BlockSpec((STEP, 3 * width), lambda m, place: (tile_of(m), 0)),
                pl.BlockSpec((width, STEP), lambda m, place: (0, tile_of(m))),
                eight,
            ],
            [
                pltpu.VMEM((width, 3 * width), bf16),
                pltpu.VMEM((width, width), bf16),
                pltpu.VMEM((STEP + 8, width), f32),
                pltpu.SemaphoreType.DMA((4 * BLOCKS,)),
            ],
        ),
    )(
        place,
        hidden,
        grad_normed,
        low,
        tokens,
        theirs,
        *saved,
        later,
        taps,
        gain_one,
        gain_two,
        *halves,
        *tie,
    )


def mix_weights(place, normed_t, grad_t, grads, carried, received, tie):
    width, count = normed_t.shape
    half = width // 2
    n = width // BLOCKS
    side = 1 if received is None else 0

    def body(place, normed_t, grad_t, grads, carried, *refs):
        inward = dot(normed_t[...], grads[...])
        outward = dot(grad_t[...], carried[...])
        if received is None:
            out = refs[0]
            out[:, : 3 * n] = inward.astype(bf16)
            out[:, 3 * n :] = outward.astype(bf16)
        else:
            received_part, keep, send, total = refs
            total[:, : 3 * n] = inward + received_part[:, : 3 * n].astype(f32)
            total[:, 3 * n :] = outward + received_part[:, 3 * n :].astype(f32)
            keep_and_send(place, total, keep, send)

    left = pl.BlockSpec((half, count), lambda s, place: (side, 0))
    part = pl.BlockSpec((half, 4 * n), lambda s, place: (0, s))
    small = pl.BlockSpec((half // 2, 4 * n), lambda s, place: (0, s))
    more = [] if received is None else [received]
    return call(
        body,
        "mix_weights",
        (shape_of(half // 2, 4 * width),) * 2 if more else shape_of(half, 4 * width),
        flops=8 * count * half * width,
        moved=2 * (2 * half * count + (count + half) * 4 * width),
        tie=tie,
        n_in=5 + len(more),
        grid_spec=scalar_grid(
            (BLOCKS,),
            [
                left,
                left,
                pl.BlockSpec((count, 3 * n), lambda s, place: (0, s)),
                pl.BlockSpec((count, n), lambda s, place: (0, s)),
            ]
            + [part] * len(more),
            [small, small] if more else part,
            [pltpu.VMEM((half, 4 * n), f32)] if more else [],
        ),
    )(place, normed_t, grad_t, grads, carried, *more, *tie)


def after(value, *earlier):
    return lax.optimization_barrier((value, *earlier))[0]


def swap_cores(value):
    return lax.ppermute(value, "col", [(0, 1), (1, 0)])


def across_first(value):
    return lax.ppermute(
        value, ("dp", "col"), [(2 * p + c, 2 * (p ^ (1 << c)) + c) for p in range(4) for c in range(2)]
    )


def across_second(value):
    return lax.ppermute(
        value, ("dp", "col"), [(2 * p + c, 2 * (p ^ (2 >> c)) + c) for p in range(4) for c in range(2)]
    )


def along_row(value, steps):
    return lax.ppermute(value, "row", [(i, (i + steps) % BLOCKS) for i in range(BLOCKS)])


def quarters(part):
    across = across_first(part)
    return (part, across, across_second(part), across_second(across))


def add(*parts):
    return sum(part.astype(f32) for part in parts).astype(bf16)


def upper(value):
    return value[: value.shape[0] // 2]


def lower(value):
    return value[value.shape[0] // 2 :]


def block_of(value, b, axis=0):
    width = value.shape[axis] // BLOCKS
    return lax.dynamic_slice_in_dim(value, b * width, width, axis)


def later_rows(value):
    pairs = [(i, i - 1) for i in range(1, 2 * BLOCKS)]
    value = lax.ppermute(value, ("row", "col"), pairs)
    parts = jnp.split(value, BLOCKS, axis=1)
    order = [OFFSETS.index(offset % BLOCKS - 1) for offset in OFFSETS]
    moved = jnp.concatenate([parts[i] for i in order], axis=1)
    return jnp.where(lax.axis_index("col") == 1, moved, value)


def shards(
    tokens,
    cotangent,
    seq_lens,
    norm1_gain,
    in_weight,
    conv_weight,
    out_weight,
    norm2_gain,
    gate_up_weight,
    down_weight,
):
    dp, row, core = lax.axis_index("dp"), lax.axis_index("row"), lax.axis_index("col")
    count, half = tokens.shape[0] // 2, tokens.shape[1]
    position = ((dp * BLOCKS + row) * 2 + core) * count
    lengths = lax.dynamic_slice_in_dim(seq_lens, position // ROW_LEN, 1, 0)[0]
    place = jnp.stack(
        [dp, core, position % ROW_LEN, lengths[0], lengths[0] + lengths[1]]
    ).astype(jnp.int32)

    def of_the_other(value):
        return lax.dynamic_slice_in_dim(value, (1 - core) * count, count, 0)

    mix_first = pack(in_weight, out_weight, place, 1, conv_weight)
    mix_quarters = [along_row(mix_first, -offset) for offset in OFFSETS[1:]]
    before = lax.ppermute(
        after(tokens[2 * count - HALO :], mix_first),
        "row",
        [(i, i + 1) for i in range(BLOCKS - 1)],
    )
    own_gains = jnp.pad(jnp.stack([norm1_gain, norm2_gain]), ((0, HALO - 2), (0, 0)))
    mix_own = pack(in_weight, out_weight, place, 4, tie=[mix_first])
    feed_own = pack(gate_up_weight, down_weight, place, 4, tie=[mix_own])
    sent = outgoing(place, tokens, cotangent, before, own_gains)
    theirs = swap_cores(sent)
    joined = join_rows(mix_quarters, [mix_own, feed_own, sent])
    feed_first = pack(gate_up_weight, down_weight, place, 1, tie=[joined])
    gains = jnp.concatenate([own_gains[:2], theirs[2 * count + HALO :][:2]], axis=1).astype(f32)
    gain_one, gain_two = gains[:1], gains[1:]
    normed, normed_t, low, low_t = prepare(
        place, tokens, theirs, before, cotangent, gain_one, [joined]
    )
    width = half // 4
    taps = jnp.concatenate(
        [conv_weight] + [part[width : width + KCONV, : conv_weight.shape[1]] for part in mix_quarters],
        axis=1,
    ).astype(f32)
    quarter_one = along_row(feed_first, -OFFSETS[1])
    mix_half = mix_assemble(mix_own, quarters(joined), place, [normed, quarter_one])
    mix_halves = [mix_half, swap_cores(mix_half)]
    half_one = lax.all_gather(after(quarter_one, mix_half), "dp", axis=0, tiled=True)

    *saved, hidden, carried, normed_two, normed_two_t = mix_forward(
        place, normed, mix_halves, tokens, theirs, taps, gain_two, []
    )
    feed_halves, others = [feed_own], [swap_cores(feed_own)]
    activations, from_them = [], []

    def gathered(k, last, here):
        part = along_row(after(feed_first, last), -OFFSETS[k])
        return lax.all_gather(after(part, here), "dp", axis=0, tiled=True)

    def have(half):
        feed_halves.append(half)
        others.append(swap_cores(half))

    def activate(grad, tie):
        k = len(activations)
        grad, acts, for_them = feed(
            normed_two, low, normed_two_t, low_t, feed_halves[k], others[k], grad, tie
        )
        activations.append(acts)
        from_them.append(swap_cores(for_them))
        return grad, for_them

    def weights_of(k, tie):
        keep, send = feed_weights(place, normed_two_t, low_t, activations[k], from_them[k], tie)
        return keep, across_second(send)

    grad_normed_two, done = activate(None, [])
    half_two = gathered(2, hidden, done)
    have(after(half_one, done))
    last = done
    grad_normed_two, done = activate(grad_normed_two, [])
    half_three = gathered(3, last, done)
    keep, send = weights_of(0, [done])
    have(after(half_two, keep))
    grad_normed_two, done = activate(grad_normed_two, [keep])
    zero = (keep, send)
    keep, send = weights_of(1, [done, send])
    have(after(half_three, keep))
    grad_normed_two, done = activate(grad_normed_two, [keep])
    one = add(keep, send)
    keep, send = weights_of(2, [done, send])
    one_across = across_first(lower(after(one, keep)))
    first = first_rows(hidden, grad_normed_two, low, saved[1], gain_two, mix_halves)
    later = later_rows(first)
    one = add(upper(one), one_across)
    two = add(keep, send)
    keep, send = weights_of(3, [keep, first, one])
    one = along_row(one, OFFSETS[1])
    zero_across = across_first(after(add(*map(lower, zero)), keep))

    grad_own, grad_other, grads, grad_t, sums = mix_backward(
        place,
        hidden,
        grad_normed_two,
        low,
        tokens,
        theirs,
        saved,
        later,
        taps,
        gain_one,
        gain_two,
        mix_halves,
        [keep, two],
    )
    two = add(upper(two), across_first(lower(after(two, keep))))
    three = add(keep, send)
    where = jnp.array([OFFSETS.index(offset) for offset in (0, 1, 2, -1)], jnp.int32)
    own_taps = jnp.concatenate(
        [block_of(sums[2:], where[(b - row) % BLOCKS], 1) for b in range(BLOCKS)], axis=1
    )
    packed_sums = jnp.concatenate([sums[:2], own_taps], axis=0)
    every = lax.all_gather(packed_sums, ("dp", "row", "col"), axis=0)
    sums = jnp.sum(every.reshape(16, 2, *packed_sums.shape), axis=0)
    mine, other = sums[core], sums[1 - core]
    gain_grads = mine[:2, :half] + other[:2, half:]
    taps_grad = block_of(mine[2 : 2 + KCONV] + other[2 : 2 + KCONV], row, 1)

    for_them = mix_weights(place, normed_t, grad_t, grads, carried, None, [one, two, three, packed_sums])
    received = swap_cores(for_them)
    three = add(upper(three), across_first(lower(three)))
    two = along_row(two, OFFSETS[2])
    grad_theirs = swap_cores(grad_other)
    keep, send = mix_weights(
        place, normed_t, grad_t, grads, carried, received, [three, grad_theirs, two]
    )
    send = across_second(send)
    three = along_row(three, OFFSETS[3])
    own_out, other_out = feed_output(hidden, activations, feed_halves, others, [keep])
    three, send = lax.optimization_barrier((three, send, own_out))[:2]
    other_out = swap_cores(other_out)
    feed_sum = add(*map(upper, zero), zero_across, one, two, three)
    feed_sum = quarters(feed_sum)
    go = across_first(add(lower(keep), lower(send)))
    mix_quarters = jnp.split(add(upper(keep), upper(send), go), BLOCKS, axis=1)
    mix_quarters = [along_row(part, OFFSETS[k]) if k else part for k, part in enumerate(mix_quarters)]
    mix_sum = quarters(add(*mix_quarters))
    output_back = join_tokens(own_out, other_out, place)
    input_back = join_tokens(grad_own, grad_theirs, place)
    gate_up_grad, down_grad = unpack(feed_sum, 2, place)
    in_grad, out_grad = unpack(mix_sum, 3, place)
    return (
        output_back,
        input_back,
        gain_grads[0],
        in_grad,
        taps_grad,
        out_grad,
        gain_grads[1],
        gate_up_grad,
        down_grad,
    )


def from_behind(value, axis, steps):
    count = lax.axis_size(axis)
    leading, last = (max(0, -steps), min(count, count - steps))
    return lax.ppermute(value, axis, [(source, source + steps) for source in range(leading, last)])


def token_index(count, extra):
    flat_rank = (
        lax.axis_index("dp") * lax.axis_size("row") + lax.axis_index("row")
    ) * lax.axis_size("col") + lax.axis_index("col")
    return flat_rank * count + jnp.arange(count + extra, dtype=jnp.int32)


def flat_slot_masks(seq_lens, count, extra):
    position = token_index(count, extra)
    packed = position // ROW_LEN
    place = position - packed * ROW_LEN
    table = (packed[:, None] == jnp.arange(seq_lens.shape[0], dtype=jnp.int32)[None, :]).astype(
        jnp.int32
    )
    first = jnp.sum(table * seq_lens[None, :, 0], axis=1)
    second = jnp.sum(table * seq_lens[None, :, 1], axis=1)
    start = jnp.where(place < first, 0, first)
    valid_slot = (place < first + second).astype(jnp.float32)
    keep_masks = jnp.stack([(place - lag >= start).astype(jnp.float32) for lag in range(KCONV)])
    return (valid_slot[:count], keep_masks)


def collect(
    norm1_gain, in_weight, conv_weight, out_weight, norm2_gain, gate_up_weight, down_weight
):
    in_rows, conv_full, out_rows, gate_rows, down_rows = (
        lax.all_gather(in_weight, "row", axis=2, tiled=True),
        lax.all_gather(conv_weight, "row", axis=1, tiled=True),
        lax.all_gather(out_weight, "row", axis=0, tiled=True),
        lax.all_gather(gate_up_weight, "row", axis=2, tiled=True),
        lax.all_gather(down_weight, "row", axis=0, tiled=True),
    )
    gain_first, in_full, out_full, gain_second, gate_full, down_full = (
        lax.all_gather(norm1_gain, "col", axis=0, tiled=True),
        lax.all_gather(in_rows, "col", axis=1, tiled=True),
        lax.all_gather(out_rows, "col", axis=1, tiled=True),
        lax.all_gather(norm2_gain, "col", axis=0, tiled=True),
        lax.all_gather(gate_rows, "col", axis=1, tiled=True),
        lax.all_gather(down_rows, "col", axis=1, tiled=True),
    )
    return (gain_first, in_full, conv_full, out_full, gain_second, gate_full, down_full)


def flat_norm_backward(values, rstd, gain, grad_normed):
    scaled = grad_normed * gain
    gain_grad = jnp.sum(grad_normed * values * rstd, axis=0)
    grad_values = rstd * scaled - values * (rstd * rstd * rstd) * jnp.mean(
        scaled * values, axis=1, keepdims=True
    )
    return (grad_values, gain_grad)


def project(left, right):
    return jnp.dot(left, right, preferred_element_type=jnp.float32)


def weight_grad(left, right):
    return jnp.einsum("td,te->de", left, right, preferred_element_type=jnp.float32)


def back_project(grad, matrix):
    return jnp.einsum("te,de->td", grad, matrix, preferred_element_type=jnp.float32)


def flat_shards(
    tokens,
    cotangent,
    seq_lens,
    norm1_gain,
    in_weight,
    conv_weight,
    out_weight,
    norm2_gain,
    gate_up_weight,
    down_weight,
):
    own_tokens, own_cotangent = (
        lax.all_to_all(tokens, "col", split_axis=0, concat_axis=1, tiled=True),
        lax.all_to_all(cotangent, "col", split_axis=0, concat_axis=1, tiled=True),
    )
    gain_first, in_full, conv_full, out_full, gain_second, gate_full, down_full = collect(
        norm1_gain, in_weight, conv_weight, out_weight, norm2_gain, gate_up_weight, down_weight
    )
    count, width = own_tokens.shape
    reach = KCONV - 1
    valid_slot, keep_masks = flat_slot_masks(seq_lens, count, reach)
    conv_taps = conv_full.astype(jnp.float32)
    gain_one_f = gain_first.astype(jnp.float32)
    gain_two_f = gain_second.astype(jnp.float32)
    inputs = own_tokens.astype(jnp.float32)
    rstd_first = lax.rsqrt(jnp.mean(inputs * inputs, axis=1, keepdims=True) + eps)
    normed = (inputs * rstd_first * gain_one_f).astype(jnp.bfloat16)
    gate_b = project(normed, in_full[0])
    gate_c = project(normed, in_full[1])
    value_part = project(normed, in_full[2])
    product = gate_b * value_part
    earlier = from_behind(product[count - reach :], ("row", "col"), 1)
    extended = jnp.concatenate([earlier, product], axis=0)
    conv = jnp.zeros((count, width), jnp.float32)
    for lag in range(KCONV):
        conv = (
            conv
            + conv_taps[lag]
            * keep_masks[lag, :count, None]
            * extended[reach - lag : reach - lag + count]
        )
    carried = (gate_c * conv).astype(jnp.bfloat16)
    hidden = inputs + project(carried, out_full)
    rstd_second = lax.rsqrt(jnp.mean(hidden * hidden, axis=1, keepdims=True) + eps)
    normed_two = (hidden * rstd_second * gain_two_f).astype(jnp.bfloat16)
    gate = project(normed_two, gate_full[0])
    up_part = project(normed_two, gate_full[1])
    sigmoid_gate = jax.nn.sigmoid(gate)
    silu_gate = gate * sigmoid_gate
    active = (silu_gate * up_part).astype(jnp.bfloat16)
    output = hidden + project(active, down_full)
    grad_out = own_cotangent.astype(jnp.float32) * valid_slot[:, None]
    grad_low = grad_out.astype(jnp.bfloat16)
    down_grad = weight_grad(active, grad_low)
    grad_active = back_project(grad_low, down_full)
    grad_gate = (grad_active * up_part * sigmoid_gate * (1.0 + gate * (1.0 - sigmoid_gate))).astype(
        jnp.bfloat16
    )
    grad_up = (grad_active * silu_gate).astype(jnp.bfloat16)
    gate_grad = jnp.stack([weight_grad(normed_two, grad_gate), weight_grad(normed_two, grad_up)])
    grad_normed_two = back_project(grad_gate, gate_full[0]) + back_project(grad_up, gate_full[1])
    grad_second, gain_second_part = flat_norm_backward(hidden, rstd_second, gain_two_f, grad_normed_two)
    grad_hidden = grad_out + grad_second
    grad_o = grad_hidden.astype(jnp.bfloat16)
    out_grad = weight_grad(carried, grad_o)
    grad_carried = back_project(grad_o, out_full)
    grad_gate_c = (grad_carried * conv).astype(jnp.bfloat16)
    grad_conv = grad_carried * gate_c
    later = from_behind(grad_conv[:reach], ("row", "col"), -1)
    grad_extended = jnp.concatenate([grad_conv, later], axis=0)
    grad_product = jnp.zeros((count, width), jnp.float32)
    conv_rows = []
    for lag in range(KCONV):
        masked = keep_masks[lag, :, None] * grad_extended
        grad_product = grad_product + conv_taps[lag] * masked[lag : lag + count]
        conv_rows.append(
            jnp.sum(masked[:count] * extended[reach - lag : reach - lag + count], axis=0)
        )
    conv_grad = jnp.stack(conv_rows)
    grad_gate_b = (grad_product * value_part).astype(jnp.bfloat16)
    grad_value = (grad_product * gate_b).astype(jnp.bfloat16)
    in_grad = jnp.stack(
        [
            weight_grad(normed, grad_gate_b),
            weight_grad(normed, grad_gate_c),
            weight_grad(normed, grad_value),
        ]
    )
    grad_normed = (
        back_project(grad_gate_b, in_full[0])
        + back_project(grad_gate_c, in_full[1])
        + back_project(grad_value, in_full[2])
    )
    grad_first, gain_first_part = flat_norm_backward(inputs, rstd_first, gain_one_f, grad_normed)
    input_grad = (grad_hidden + grad_first).astype(jnp.bfloat16)
    output_back, input_back = (
        lax.all_to_all(output.astype(jnp.bfloat16), "col", split_axis=1, concat_axis=0, tiled=True),
        lax.all_to_all(input_grad, "col", split_axis=1, concat_axis=0, tiled=True),
    )
    in_cols, out_cols, gate_cols, down_cols = (
        lax.psum_scatter(in_grad, "col", scatter_dimension=1, tiled=True),
        lax.psum_scatter(out_grad, "col", scatter_dimension=1, tiled=True),
        lax.psum_scatter(gate_grad, "col", scatter_dimension=1, tiled=True),
        lax.psum_scatter(down_grad, "col", scatter_dimension=1, tiled=True),
    )
    in_part, out_part, gate_part, down_part = (
        lax.psum_scatter(in_cols, "row", scatter_dimension=2, tiled=True),
        lax.psum_scatter(out_cols, "row", scatter_dimension=0, tiled=True),
        lax.psum_scatter(gate_cols, "row", scatter_dimension=2, tiled=True),
        lax.psum_scatter(down_cols, "row", scatter_dimension=0, tiled=True),
    )
    in_sum, out_sum, gate_sum, down_sum = lax.psum((in_part, out_part, gate_part, down_part), "dp")
    gain_one_sum, gain_two_sum, conv_sum = lax.psum(
        (gain_first_part, gain_second_part, conv_grad), ("dp", "row", "col")
    )
    col_width = width // lax.axis_size("col")
    row_width = width // lax.axis_size("row")
    gain_first_grad = lax.dynamic_slice_in_dim(
        gain_one_sum, lax.axis_index("col") * col_width, col_width
    )
    gain_second_grad = lax.dynamic_slice_in_dim(
        gain_two_sum, lax.axis_index("col") * col_width, col_width
    )
    conv_weight_grad = lax.dynamic_slice_in_dim(
        conv_sum, lax.axis_index("row") * row_width, row_width, axis=1
    )
    return (
        output_back,
        input_back,
        gain_first_grad,
        in_sum,
        conv_weight_grad,
        out_sum,
        gain_second_grad,
        gate_sum,
        down_sum,
    )


def solution(mesh):
    ring = mesh.shape["dp"] == 4 and mesh.shape["row"] == BLOCKS and mesh.shape["col"] == 2
    return jax.shard_map(
        shards if ring else flat_shards,
        mesh=mesh,
        in_specs=(
            P(("dp", "row"), "col"),
            P(("dp", "row"), "col"),
            P(),
            P("col"),
            P(None, "col", "row"),
            P(None, "row"),
            P("row", "col"),
            P("col"),
            P(None, "col", "row"),
            P("row", "col"),
        ),
        out_specs=(
            P(("dp", "row"), "col"),
            P(("dp", "row"), "col"),
            P("col"),
            P(None, "col", "row"),
            P(None, "row"),
            P("row", "col"),
            P("col"),
            P(None, "col", "row"),
            P("row", "col"),
        ),
        check_vma=False,
    )
```

```python
import functools

import jax
import jax.numpy as jnp
from jax import lax
from jax.experimental import pallas as pl
from jax.experimental.pallas import tpu as pltpu
from jax.sharding import PartitionSpec as P

KCONV = 3
ROW_LEN = 8192
BLOCKS = 4
OFFSETS = (0, -1, 1, 2)
HALO = 16
STEP = 256


eps = 1e-05
bf16 = jnp.bfloat16
f32 = jnp.float32
VMEM_LIMIT = 64000 * 1024
HERE = pl.BlockSpec(memory_space=pl.ANY)
SCALARS = pl.BlockSpec(memory_space=pltpu.SMEM)


def dot(left, right):
    return jnp.dot(left, right, preferred_element_type=f32)


def dot_nt(left, right):
    return lax.dot_general(left, right, (((1,), (1,)), ((), ())), preferred_element_type=f32)


def shape_of(*dims, dtype=bf16):
    return jax.ShapeDtypeStruct(dims, dtype)


def call(body, name, out_shape, flops=0, moved=0, tie=(), n_in=None, **kwargs):
    if tie:
        inner, at = body, n_in

        def body(*refs):
            inner(*refs[:at], *refs[at + len(tie) :])

        if "grid_spec" in kwargs:
            spec = kwargs["grid_spec"]
            kwargs["grid_spec"] = pltpu.PrefetchScalarGridSpec(
                num_scalar_prefetch=1,
                grid=spec.grid,
                in_specs=list(spec.in_specs) + [HERE] * len(tie),
                out_specs=spec.out_specs,
                scratch_shapes=spec.scratch_shapes,
            )
        else:
            kwargs["in_specs"] = list(kwargs["in_specs"]) + [HERE] * len(tie)
    return pl.pallas_call(
        body,
        out_shape=out_shape,
        name=name,
        compiler_params=pltpu.CompilerParams(vmem_limit_bytes=VMEM_LIMIT),
        cost_estimate=pl.CostEstimate(flops=flops, bytes_accessed=moved, transcendentals=0),
        **kwargs,
    )


def scalar_grid(grid, in_specs, out_specs, scratch_shapes=()):
    return pltpu.PrefetchScalarGridSpec(
        num_scalar_prefetch=1,
        grid=grid,
        in_specs=in_specs,
        out_specs=out_specs,
        scratch_shapes=scratch_shapes,
    )


def quarter_of(place, j):
    dp, core = place[0], place[1]
    low, high = j % 2, j // 2
    mask = jnp.where(core == 0, 2 * high + low, 2 * low + high)
    return jnp.bitwise_xor(dp, mask)


def join_tokens(mine, theirs, place):
    count, half = mine.shape

    def body(place, mine, theirs, out):
        own = pl.program_id(0) == place[1]

        @pl.when(own)
        def _():
            out[...] = mine[...]

        @pl.when(jnp.logical_not(own))
        def _():
            out[...] = theirs[...]

    kept = pl.BlockSpec((count, half), lambda h, place: (0, 0))
    return call(
        body,
        "join_tokens",
        shape_of(2 * count, half),
        grid_spec=scalar_grid(
            (2,), [kept, kept], pl.BlockSpec((count, half), lambda h, place: (h, 0))
        ),
    )(place, mine, theirs)


def outgoing(place, tokens, cotangent, before, gains, tie):
    count, half = tokens.shape[0] // 2, tokens.shape[1]
    rows = 2 * count + 2 * HALO

    def body(place, tokens, cotangent, between, before, gains, out):
        out[:count] = tokens[...]
        out[count : 2 * count] = cotangent[...]

        @pl.when(place[1] == 0)
        def _():
            out[2 * count : 2 * count + HALO] = between[...]

        @pl.when(place[1] == 1)
        def _():
            out[2 * count : 2 * count + HALO] = before[...]

        out[2 * count + HALO :] = gains[...]

    theirs = pl.BlockSpec((count, half), lambda i, place: (1 - place[1], 0))
    few = pl.BlockSpec((HALO, half), lambda i, place: (0, 0))
    return call(
        body,
        "outgoing",
        shape_of(rows, half),
        tie=tie,
        n_in=6,
        grid_spec=scalar_grid(
            (1,),
            [theirs, theirs, pl.BlockSpec((HALO, half), lambda i, place: (count // HALO - 1, 0)), few, few],
            pl.BlockSpec((rows, half), lambda i, place: (0, 0)),
        ),
    )(place, tokens, cotangent, tokens, before, gains, *tie)


def pack(stack, turned, place, quarters, rows=None, tie=()):
    k, half, n = stack.shape
    width = half // 4
    lanes = (k + 1) * n
    below = [] if rows is None else [rows]

    def body(place, stack, turned, *refs):
        out = refs[-1]
        for i in range(k):
            out[:width, i * n : (i + 1) * n] = stack[i]
        out[:width, k * n :] = turned[...].astype(f32).T.astype(out.dtype)
        if below:
            out[width:, :] = jnp.zeros((HALO, lanes), out.dtype)
            out[width : width + KCONV, :n] = refs[0][...]

    def source(j, place):
        return place[0] if quarters == 1 else j

    return call(
        body,
        "pack",
        shape_of(quarters * width + HALO * len(below), lanes),
        tie=tie,
        n_in=3 + len(below),
        grid_spec=scalar_grid(
            (quarters,),
            [
                pl.BlockSpec((k, width, n), lambda j, place: (0, source(j, place), 0)),
                pl.BlockSpec((n, width), lambda j, place: (0, source(j, place))),
            ]
            + [pl.BlockSpec((KCONV, n), lambda j, place: (0, 0))] * len(below),
            pl.BlockSpec((width + HALO * len(below), lanes), lambda j, place: (j, 0)),
        ),
    )(place, stack, turned, *below, *tie)


def join_rows(parts, tie):
    rows, lanes = parts[0].shape

    def body(*refs):
        for i in range(len(parts)):
            refs[-1][i * rows : (i + 1) * rows] = refs[i][...]

    whole = pl.BlockSpec(memory_space=pltpu.VMEM)
    return call(
        body,
        "join_rows",
        shape_of(len(parts) * rows, lanes),
        tie=tie,
        n_in=len(parts),
        in_specs=[whole] * len(parts),
        out_specs=whole,
    )(*parts, *tie)


def mix_assemble(own, pieces, place, tie):
    half, lanes = own.shape
    width = half // 4
    stride = width + HALO

    def body(place, own, *refs):
        out = refs[-1]
        out[0] = own[...]
        for s in range(1, BLOCKS):
            for j in range(4):
                rows = pl.ds(pl.multiple_of(quarter_of(place, j) * width, width), width)
                out[s, rows, :] = refs[j][(s - 1) * stride : (s - 1) * stride + width, :]

    whole = pl.BlockSpec(memory_space=pltpu.VMEM)
    return call(
        body,
        "mix_assemble",
        shape_of(BLOCKS, half, lanes),
        tie=tie,
        n_in=6,
        in_specs=[SCALARS] + [whole] * 5,
        out_specs=whole,
    )(place, own, *pieces, *tie)


def unpack(pieces, k, place):
    width, lanes = pieces[0].shape
    half, n = 4 * width, lanes // (k + 1)

    def body(place, *refs):
        stack, turned = refs[4:]
        for j in range(4):

            @pl.when(pl.program_id(0) == j)
            def _(piece=refs[j]):
                for i in range(k):
                    stack[i] = piece[:, i * n : (i + 1) * n].astype(f32)
                turned[...] = piece[:, k * n :].astype(f32).T

    whole = pl.BlockSpec((width, lanes), lambda j, place: (0, 0))
    return call(
        body,
        "unpack",
        (shape_of(k, half, n, dtype=f32), shape_of(n, half, dtype=f32)),
        grid_spec=scalar_grid(
            (4,),
            [whole] * 4,
            [
                pl.BlockSpec((k, width, n), lambda j, place: (0, quarter_of(place, j), 0)),
                pl.BlockSpec((n, width), lambda j, place: (0, quarter_of(place, j))),
            ],
        ),
    )(place, *pieces)


def rows_of(i, step=STEP):
    return pl.ds(pl.multiple_of(i * step, step), step)


def slots(place, start, count):
    slot = place[2] + start + lax.broadcasted_iota(jnp.int32, (count, 1), 0)
    return slot, jnp.where(slot < place[3], 0, place[3])


def inverse_rms(*parts):
    width = sum(part.shape[1] for part in parts)
    total = sum(jnp.sum(part * part, axis=1, keepdims=True) for part in parts)
    return lax.rsqrt(total / width + eps)


def prepare(place, tokens, theirs, before, cotangent, gain, tie):
    count, half = tokens.shape[0] // 2, tokens.shape[1]
    width = 2 * half

    def body(
        place, own, other, before, between, halo_other, cot, cot_other, gain, normed, normed_t, low, low_t
    ):
        def norm(left, right):
            left, right = left.astype(f32), right.astype(f32)
            rstd = inverse_rms(left, right)
            return (
                (left * rstd * gain[:, :half]).astype(bf16),
                (right * rstd * gain[:, half:]).astype(bf16),
            )

        halo = jnp.where(place[1] == 0, before[...].astype(f32), between[...].astype(f32))

        @pl.when(pl.program_id(0) == 0)
        def _():
            left, right = norm(halo, halo_other[...])
            normed[:HALO, :half] = left
            normed[:HALO, half:] = right

        tile = pl.program_id(0)
        here = pl.ds(pl.multiple_of(HALO + tile * STEP, HALO), STEP)
        for i, value in enumerate(norm(own[...], other[...])):
            lanes = slice(i * half, (i + 1) * half)
            normed[here, lanes] = value
            normed_t[lanes, :] = value.astype(f32).T.astype(bf16)
        slot, _ = slots(place, tile * STEP, STEP)
        valid = (slot < place[4]).astype(f32)
        for i, value in enumerate((cot[...], cot_other[...])):
            lanes = slice(i * half, (i + 1) * half)
            value = value.astype(f32) * valid
            low[:, lanes] = value.astype(bf16)
            low_t[lanes, :] = value.T.astype(bf16)

    tiles = count // STEP
    mine = pl.BlockSpec((STEP, half), lambda m, place: (place[1] * tiles + m, 0))

    def received(first):
        return pl.BlockSpec((STEP, half), lambda m, place: (first + m, 0))

    def few(block):
        return pl.BlockSpec((HALO, half), lambda m, place: (block, 0))

    turned = pl.BlockSpec((width, STEP), lambda m, place: (0, m))
    return call(
        body,
        "prepare",
        (
            shape_of(HALO + count, width),
            shape_of(width, count),
            shape_of(count, width),
            shape_of(width, count),
        ),
        moved=16 * count * width,
        tie=tie,
        n_in=9,
        grid_spec=scalar_grid(
            (tiles,),
            [
                mine,
                received(0),
                few(0),
                few(count // HALO - 1),
                few(2 * count // HALO),
                mine,
                received(tiles),
                pl.BlockSpec((1, width), lambda m, place: (0, 0)),
            ],
            [
                pl.BlockSpec((HALO + count, width), lambda m, place: (0, 0)),
                turned,
                pl.BlockSpec((STEP, width), lambda m, place: (m, 0)),
                turned,
            ],
        ),
    )(place, tokens, theirs, before, tokens, theirs, cotangent, theirs, gain, *tie)


def mix_copies(sources, inward, outward, sems):
    copies = []
    for s in range(BLOCKS):
        for side in range(2):
            source = sources[side].at[s]
            half, lanes = source.shape
            n = lanes // 4
            rows = pl.ds(side * half, half)
            at = 4 * s + 2 * side
            copies.append(
                pltpu.make_async_copy(
                    source.at[:, pl.ds(0, 3 * n)],
                    inward.at[rows, pl.ds(s * 3 * n, 3 * n)],
                    sems.at[at],
                )
            )
            copies.append(
                pltpu.make_async_copy(
                    source.at[:, pl.ds(3 * n, n)],
                    outward.at[rows, pl.ds(s * n, n)],
                    sems.at[at + 1],
                )
            )
    return copies


def mix_forward(place, normed, halves, tokens, theirs, taps, gain, tie):
    count, half = tokens.shape[0] // 2, tokens.shape[1]
    width = 2 * half
    n = width // BLOCKS
    part = (HALO + count) // 5
    kept = 4

    def body(place, *refs):
        normed_hbm, sources, refs = refs[0], refs[1:3], refs[3:]
        tokens_hbm, theirs_hbm, taps, gain = refs[:4]
        results, hidden_hbm, carried_hbm, normed2_hbm, turned_hbm = (
            refs[4:8],
            refs[8],
            refs[9],
            refs[10],
            refs[11],
        )
        normed, inward, outward, mine, other, mixed, product, carried, hidden, normed2, turned = refs[
            12:23
        ]
        saved = refs[23:27]
        in_sems, weight_sems, saved_sems, out_sems = refs[27:]
        loads = [
            pltpu.make_async_copy(normed_hbm, normed, in_sems.at[0]),
            pltpu.make_async_copy(
                tokens_hbm.at[pl.ds(pl.multiple_of(place[1] * count, count), count)],
                mine,
                in_sems.at[1],
            ),
            pltpu.make_async_copy(theirs_hbm.at[pl.ds(0, count)], other, in_sems.at[2]),
        ]
        weights = mix_copies(sources, inward, outward, weight_sems)
        loads[0].start()
        for copy in weights:
            copy.start()
        loads[1].start()
        loads[2].start()
        loads[0].wait()
        pending = []
        for s in range(BLOCKS):
            for copy in weights[4 * s : 4 * s + 4]:
                copy.wait()

            def project(i, carry, s=s):
                rows = rows_of(i, part)
                value = dot(normed[rows, :], inward[:, s * 3 * n : (s + 1) * 3 * n])
                mixed[rows, :] = value
                product[rows, :] = value[:, :n] * value[:, 2 * n :]
                return carry

            lax.fori_loop(0, 5, project, 0)
            lanes = slice(s * n, (s + 1) * n)
            for m in range(count // STEP):
                first = HALO + m * STEP
                rows = slice(m * STEP, (m + 1) * STEP)
                slot, start = slots(place, m * STEP, STEP)
                conv = jnp.zeros((STEP, n), f32)
                for lag in range(KCONV):
                    keep = (slot - lag >= start).astype(f32)
                    conv = conv + taps[lag : lag + 1, lanes] * (
                        keep * product[first - lag : first - lag + STEP, :]
                    )
                inside = mixed[first : first + STEP, :]
                carried[rows, lanes] = (inside[:, n : 2 * n] * conv).astype(bf16)
                for i, value in enumerate((inside[:, :n], inside[:, n : 2 * n], inside[:, 2 * n :], conv)):
                    saved[i][rows, lanes] = value.astype(bf16)
            for i in range(kept):
                copy = pltpu.make_async_copy(
                    saved[i].at[:, pl.ds(s * n, n)],
                    results[i].at[:, pl.ds(s * n, n)],
                    saved_sems.at[kept * s + i],
                )
                copy.start()
                pending.append(copy)
        copy = pltpu.make_async_copy(carried, carried_hbm, in_sems.at[3])
        copy.start()
        pending.append(copy)
        loads[1].wait()
        loads[2].wait()
        for m in range(count // STEP):
            rows = slice(m * STEP, (m + 1) * STEP)
            term = dot_nt(carried[rows, :], outward[...])
            left = mine[rows, :].astype(f32) + term[:, :half]
            right = other[rows, :].astype(f32) + term[:, half:]
            rstd = inverse_rms(left, right)
            for i, value in enumerate((left, right)):
                lanes = slice(i * half, (i + 1) * half)
                hidden[rows, lanes] = value
                value = value * rstd * gain[:, lanes]
                normed2[rows, lanes] = value.astype(bf16)
                turned[lanes, rows] = value.T.astype(bf16)
            for i, (source, target, by) in enumerate(
                (
                    (hidden, hidden_hbm, 0),
                    (normed2, normed2_hbm, 0),
                    (turned, turned_hbm, 1),
                )
            ):
                here = pl.ds(m * STEP, STEP)
                source, target = (
                    (source.at[:, here], target.at[:, here])
                    if by
                    else (source.at[here], target.at[here])
                )
                copy = pltpu.make_async_copy(source, target, out_sems.at[3 * m + i])
                copy.start()
                pending.append(copy)
        for copy in pending:
            copy.wait()

    tiles = count // STEP
    wide = shape_of(count, width, dtype=f32)
    flat = shape_of(count, width)
    whole = pl.BlockSpec(memory_space=pltpu.VMEM)
    return call(
        body,
        "mix_forward",
        (flat, flat, flat, flat, wide, flat, flat, shape_of(width, count)),
        flops=8 * count * width * width,
        moved=30 * count * width + 8 * width * width,
        tie=tie,
        n_in=8,
        in_specs=[SCALARS] + [HERE] * 5 + [whole] * 2,
        out_specs=(HERE,) * 8,
        scratch_shapes=[
            pltpu.VMEM((HALO + count, width), bf16),
            pltpu.VMEM((width, 3 * width), bf16),
            pltpu.VMEM((width, width), bf16),
            pltpu.VMEM((count, half), bf16),
            pltpu.VMEM((count, half), bf16),
            pltpu.VMEM((HALO + count, 3 * n), f32),
            pltpu.VMEM((HALO + count, n), f32),
            pltpu.VMEM((count, width), bf16),
            pltpu.VMEM((count, width), f32),
            pltpu.VMEM((count, width), bf16),
            pltpu.VMEM((width, count), bf16),
        ]
        + [pltpu.VMEM((count, width), bf16)] * kept
        + [
            pltpu.SemaphoreType.DMA((4,)),
            pltpu.SemaphoreType.DMA((4 * BLOCKS,)),
            pltpu.SemaphoreType.DMA((kept * BLOCKS,)),
            pltpu.SemaphoreType.DMA((3 * tiles,)),
        ],
    )(place, normed, *halves, tokens, theirs, taps, gain, *tie)


def feed_body(
    lanes,
    started,
    normed_hbm,
    low_hbm,
    normed_t_hbm,
    low_t_hbm,
    own_hbm,
    other_hbm,
    grad_in,
    grad_hbm,
    acts_hbm,
    theirs_hbm,
    normed,
    low,
    normed_t,
    low_t,
    weights,
    grad,
    acts,
    theirs,
    in_sems,
    grad_sems,
    acts_sems,
    their_sems,
):
    f = lanes // 3
    count, width = normed.shape
    half = width // 2
    loads = [
        pltpu.make_async_copy(source, target, in_sems.at[i])
        for i, (source, target) in enumerate(
            (
                (normed_hbm, normed),
                (own_hbm, weights.at[pl.ds(0, half)]),
                (other_hbm, weights.at[pl.ds(half, half)]),
                (low_hbm, low),
                (normed_t_hbm.at[pl.ds(half, half)], normed_t),
                (low_t_hbm.at[pl.ds(half, half)], low_t),
            )
        )
    ]
    if started:
        loads.append(pltpu.make_async_copy(grad_in, grad, in_sems.at[6]))
    for load in loads[:4]:
        load.start()
    for load in loads[:4]:
        load.wait()
    for load in loads[4:]:
        load.start()

    def acts_copy(i):
        rows = rows_of(i)
        return pltpu.make_async_copy(acts.at[rows], acts_hbm.at[rows], acts_sems.at[i])

    def activations(i, carry):
        rows = rows_of(i)
        for start in range(0, f, 256):
            stop = min(start + 256, f)
            gate_lanes = slice(start, stop)
            up_lanes = slice(f + start, f + stop)
            down_lanes = slice(2 * f + start, 2 * f + stop)
            gate = dot(normed[rows, :], weights[:, gate_lanes])
            up_part = dot(normed[rows, :], weights[:, up_lanes])
            grad_active = dot(low[rows, :], weights[:, down_lanes])
            sigmoid_gate = jax.nn.sigmoid(gate)
            silu_gate = gate * sigmoid_gate
            acts[rows, gate_lanes] = (
                grad_active * up_part * sigmoid_gate * (1.0 + gate * (1.0 - sigmoid_gate))
            ).astype(bf16)
            acts[rows, up_lanes] = (grad_active * silu_gate).astype(bf16)
            acts[rows, down_lanes] = (silu_gate * up_part).astype(bf16)
        acts_copy(i).start()
        return carry

    lax.fori_loop(0, count // STEP, activations, 0)
    loads[4].wait()
    loads[5].wait()

    def their_copy(i):
        rows = rows_of(i)
        return pltpu.make_async_copy(theirs.at[rows], theirs_hbm.at[rows], their_sems.at[i])

    def outer(i, carry):
        rows = rows_of(i)
        theirs[rows, : 2 * f] = dot(normed_t[rows, :], acts[:, : 2 * f]).astype(bf16)
        theirs[rows, 2 * f :] = dot(low_t[rows, :], acts[:, 2 * f :]).astype(bf16)
        their_copy(i).start()
        return carry

    lax.fori_loop(0, half // STEP, outer, 0)
    if started:
        loads[6].wait()

    def grad_copy(i):
        rows = rows_of(i)
        return pltpu.make_async_copy(grad.at[rows], grad_hbm.at[rows], grad_sems.at[i])

    def inner(i, carry):
        rows = rows_of(i)
        term = dot_nt(acts[rows, : 2 * f], weights[:, : 2 * f])
        grad[rows, :] = grad[rows, :] + term if started else term
        grad_copy(i).start()
        return carry

    lax.fori_loop(0, count // STEP, inner, 0)
    for i in range(half // STEP):
        their_copy(i).wait()
    for i in range(count // STEP):
        acts_copy(i).wait()
        grad_copy(i).wait()


def feed(normed, low, normed_t, low_t, own, other, grad, tie):
    count, width = normed.shape
    half, lanes = own.shape
    f = lanes // 3
    started = grad is not None
    tiles = count // STEP
    before = [grad] if started else []
    body = functools.partial(feed_body, lanes, started)
    if not started:
        inner = body

        def body(*refs):
            inner(*refs[:6], None, *refs[6:])

    return call(
        body,
        "feed",
        (shape_of(count, width, dtype=f32), shape_of(count, lanes), shape_of(half, lanes)),
        flops=13 * count * width * f,
        moved=2 * (4 * count * width + 3 * half * lanes + count * lanes) + 8 * count * width,
        tie=tie,
        n_in=6 + len(before),
        in_specs=[HERE] * (6 + len(before)),
        out_specs=(HERE,) * 3,
        scratch_shapes=[
            pltpu.VMEM((count, width), bf16),
            pltpu.VMEM((count, width), bf16),
            pltpu.VMEM((half, count), bf16),
            pltpu.VMEM((half, count), bf16),
            pltpu.VMEM((width, lanes), bf16),
            pltpu.VMEM((count, width), f32),
            pltpu.VMEM((count, lanes), bf16),
            pltpu.VMEM((half, lanes), bf16),
            pltpu.SemaphoreType.DMA((7,)),
            pltpu.SemaphoreType.DMA((tiles,)),
            pltpu.SemaphoreType.DMA((tiles,)),
            pltpu.SemaphoreType.DMA((half // STEP,)),
        ],
    )(normed, low, normed_t, low_t, own, other, *before, *tie)


def feed_output(hidden, acts, owns, others, tie):
    count, width = hidden.shape
    half, lanes = owns[0].shape
    f = lanes // 3

    def body(hidden, *refs):
        acts, owns, others, outs = refs[:4], refs[4:8], refs[8:12], refs[12:]
        for side, weights in enumerate((owns, others)):
            total = hidden[:, side * half : (side + 1) * half]
            for k in range(BLOCKS):
                total = total + dot_nt(acts[k][...], weights[k][...])
            outs[side][...] = total.astype(bf16)

    rows = pl.BlockSpec((STEP, f), lambda m: (m, 2))
    whole = pl.BlockSpec((half, f), lambda m: (0, 2))
    part = pl.BlockSpec((STEP, half), lambda m: (m, 0))
    return call(
        body,
        "feed_output",
        (shape_of(count, half),) * 2,
        flops=2 * BLOCKS * count * width * f,
        moved=2 * BLOCKS * (count + width) * f + 6 * count * width,
        tie=tie,
        n_in=13,
        grid=(count // STEP,),
        in_specs=[pl.BlockSpec((STEP, width), lambda m: (m, 0))] + [rows] * 4 + [whole] * 8,
        out_specs=(part, part),
    )(hidden, *acts, *owns, *others, *tie)


def keep_and_send(place, total, keep, send):
    width = keep.shape[0] // 2
    for j in range(4):
        target = keep if j < 2 else send
        rows = pl.ds(pl.multiple_of(quarter_of(place, j) * width, width), width)
        target[(j % 2) * width : (j % 2 + 1) * width, :] = total[rows, :].astype(bf16)


def feed_weights(place, normed_t, low_t, acts, received, tie):
    width, count = normed_t.shape
    half, lanes = received.shape
    f = lanes // 3
    step = f

    def body(place, normed_t, low_t, acts, received, keep, send, total):
        def put(left):
            total[...] = dot(left[...], acts[...]) + received[...].astype(f32)

        is_down = pl.program_id(0) >= 2 * f // step

        @pl.when(jnp.logical_not(is_down))
        def _():
            put(normed_t)

        @pl.when(is_down)
        def _():
            put(low_t)

        keep_and_send(place, total, keep, send)

    left = pl.BlockSpec((half, count), lambda j, place: (0, 0))
    part = pl.BlockSpec((half // 2, step), lambda j, place: (0, j))
    return call(
        body,
        "feed_weights",
        (shape_of(half // 2, lanes),) * 2,
        flops=6 * count * half * f,
        moved=2 * (2 * half * count + count * lanes + 2 * half * lanes),
        tie=tie,
        n_in=5,
        grid_spec=scalar_grid(
            (lanes // step,),
            [
                left,
                left,
                pl.BlockSpec((count, step), lambda j, place: (0, j)),
                pl.BlockSpec((half, step), lambda j, place: (0, j)),
            ],
            [part, part],
            [pltpu.VMEM((half, step), f32)],
        ),
    )(place, normed_t, low_t, acts, received, *tie)


def hidden_backward(hidden, grad_normed, grad_out, gain):
    width = hidden.shape[1]
    rstd = lax.rsqrt(jnp.sum(hidden * hidden, axis=1, keepdims=True) / width + eps)
    scaled = grad_normed * gain
    mean = jnp.sum(scaled * hidden, axis=1, keepdims=True) / width
    grad = grad_out + (rstd * scaled - hidden * (rstd * rstd * rstd) * mean)
    return grad, grad_normed * hidden * rstd


def first_rows(hidden, grad_normed, low, gate_c, gain, halves):
    width = hidden.shape[1]
    n = width // BLOCKS
    half = width // 2

    def body(hidden, grad_normed, low, gate_c, gain, *refs):
        grad, _ = hidden_backward(hidden[...], grad_normed[...], low[...].astype(f32), gain[...])
        grad_o = grad.astype(bf16)
        for s in range(BLOCKS):
            value = dot(grad_o[:, :half], refs[0][s]) + dot(grad_o[:, half:], refs[1][s])
            lanes = slice(s * n, (s + 1) * n)
            refs[-1][:, lanes] = (value * gate_c[:, lanes].astype(f32))[:8]

    few = pl.BlockSpec((HALO, width), lambda i: (0, 0))
    return call(
        body,
        "first_rows",
        shape_of(8, width, dtype=f32),
        grid=(1,),
        in_specs=[few] * 4
        + [pl.BlockSpec((1, width), lambda i: (0, 0))]
        + [pl.BlockSpec((BLOCKS, half, n), lambda i: (0, 0, 3))] * 2,
        out_specs=pl.BlockSpec((8, width), lambda i: (0, 0)),
    )(hidden, grad_normed, low, gate_c, gain, *halves)


def mix_backward(
    place, hidden, grad_normed, low, tokens, theirs, saved, later, taps, gain_one, gain_two, halves, tie
):
    count, width = hidden.shape
    half = width // 2
    n = width // BLOCKS
    tiles = count // STEP

    def body(place, *refs):
        hidden, grad_normed, low, mine, other = refs[:5]
        gate_b, gate_c, value_part, conv, later, taps, gain_one, gain_two = refs[5:13]
        sources = refs[13:15]
        grad_own, grad_other, grads, turned, sums = refs[15:20]
        inward, outward, extended, sems = refs[20:]
        step = pl.program_id(0)
        tile = tiles - 1 - step

        @pl.when(step == 0)
        def _():
            copies = mix_copies(sources, inward, outward, sems)
            for copy in copies:
                copy.start()
            sums[...] = jnp.zeros_like(sums)
            extended[STEP:, :] = later[...]
            for copy in copies:
                copy.wait()

        @pl.when(step > 0)
        def _():
            extended[STEP:, :] = extended[:8, :]

        grad, gain_terms = hidden_backward(
            hidden[...], grad_normed[...], low[...].astype(f32), gain_two[...]
        )
        sums[1:2, :] += jnp.sum(gain_terms, axis=0, keepdims=True)
        grad_o = grad.astype(bf16)
        turned[...] = grad.T.astype(bf16)
        grad_carried = dot(grad_o, outward[...])
        extended[:STEP, :] = grad_carried * gate_c[...].astype(f32)
        grad_c = (grad_carried * conv[...].astype(f32)).astype(bf16)
        left_gate, right_gate = gate_b[...].astype(f32), value_part[...].astype(f32)
        product = left_gate * right_gate
        grad_product = jnp.zeros((STEP, width), f32)
        for lag in range(KCONV):
            slot, start = slots(place, tile * STEP + lag, STEP)
            keep = (slot - lag >= start).astype(f32)
            masked = keep * extended[lag : lag + STEP, :]
            grad_product = grad_product + taps[lag : lag + 1, :] * masked
            sums[2 + lag : 3 + lag, :] += jnp.sum(masked * product, axis=0, keepdims=True)
        grad_b = (grad_product * right_gate).astype(bf16)
        grad_v = (grad_product * left_gate).astype(bf16)
        for s in range(BLOCKS):
            lanes = slice(s * n, (s + 1) * n)
            at = s * 3 * n
            grads[:, at : at + n] = grad_b[:, lanes]
            grads[:, at + n : at + 2 * n] = grad_c[:, lanes]
            grads[:, at + 2 * n : at + 3 * n] = grad_v[:, lanes]
        grad_first = dot_nt(grads[...], inward[...])
        left, right = mine[...].astype(f32), other[...].astype(f32)
        rstd = inverse_rms(left, right)
        scaled = grad_first * gain_one[...]
        mean = (
            jnp.sum(scaled[:, :half] * left, axis=1, keepdims=True)
            + jnp.sum(scaled[:, half:] * right, axis=1, keepdims=True)
        ) / width
        for i, (value, target) in enumerate(((left, grad_own), (right, grad_other))):
            lanes = slice(i * half, (i + 1) * half)
            sums[0:1, lanes] += jnp.sum(grad_first[:, lanes] * value * rstd, axis=0, keepdims=True)
            target[...] = (
                grad[:, lanes] + (rstd * scaled[:, lanes] - value * (rstd * rstd * rstd) * mean)
            ).astype(bf16)

    def tile_of(m):
        return tiles - 1 - m

    rows = pl.BlockSpec((STEP, width), lambda m, place: (tile_of(m), 0))
    one = pl.BlockSpec((1, width), lambda m, place: (0, 0))
    eight = pl.BlockSpec((8, width), lambda m, place: (0, 0))
    narrow = pl.BlockSpec((STEP, half), lambda m, place: (tile_of(m), 0))
    return call(
        body,
        "mix_backward",
        (
            shape_of(count, half),
            shape_of(count, half),
            shape_of(count, 3 * width),
            shape_of(width, count),
            shape_of(8, width, dtype=f32),
        ),
        flops=8 * count * width * width,
        moved=44 * count * width,
        tie=tie,
        n_in=16,
        grid_spec=scalar_grid(
            (tiles,),
            [
                rows,
                rows,
                rows,
                pl.BlockSpec(
                    (STEP, half), lambda m, place: (place[1] * tiles + tile_of(m), 0)
                ),
                narrow,
                rows,
                rows,
                rows,
                rows,
                eight,
                pl.BlockSpec((KCONV, width), lambda m, place: (0, 0)),
                one,
                one,
            ]
            + [HERE] * 2,
            [
                narrow,
                narrow,
                pl.BlockSpec((STEP, 3 * width), lambda m, place: (tile_of(m), 0)),
                pl.BlockSpec((width, STEP), lambda m, place: (0, tile_of(m))),
                eight,
            ],
            [
                pltpu.VMEM((width, 3 * width), bf16),
                pltpu.VMEM((width, width), bf16),
                pltpu.VMEM((STEP + 8, width), f32),
                pltpu.SemaphoreType.DMA((4 * BLOCKS,)),
            ],
        ),
    )(
        place,
        hidden,
        grad_normed,
        low,
        tokens,
        theirs,
        *saved,
        later,
        taps,
        gain_one,
        gain_two,
        *halves,
        *tie,
    )


def mix_weights(place, normed_t, grad_t, grads, carried, received, tie):
    width, count = normed_t.shape
    half = width // 2
    n = width // BLOCKS
    side = 1 if received is None else 0

    def body(place, normed_t, grad_t, grads, carried, *refs):
        inward = dot(normed_t[...], grads[...])
        outward = dot(grad_t[...], carried[...])
        if received is None:
            out = refs[0]
            out[:, : 3 * n] = inward.astype(bf16)
            out[:, 3 * n :] = outward.astype(bf16)
        else:
            received_part, keep, send, total = refs
            total[:, : 3 * n] = inward + received_part[:, : 3 * n].astype(f32)
            total[:, 3 * n :] = outward + received_part[:, 3 * n :].astype(f32)
            keep_and_send(place, total, keep, send)

    left = pl.BlockSpec((half, count), lambda s, place: (side, 0))
    part = pl.BlockSpec((half, 4 * n), lambda s, place: (0, s))
    small = pl.BlockSpec((half // 2, 4 * n), lambda s, place: (0, s))
    more = [] if received is None else [received]
    return call(
        body,
        "mix_weights",
        (shape_of(half // 2, 4 * width),) * 2 if more else shape_of(half, 4 * width),
        flops=8 * count * half * width,
        moved=2 * (2 * half * count + (count + half) * 4 * width),
        tie=tie,
        n_in=5 + len(more),
        grid_spec=scalar_grid(
            (BLOCKS,),
            [
                left,
                left,
                pl.BlockSpec((count, 3 * n), lambda s, place: (0, s)),
                pl.BlockSpec((count, n), lambda s, place: (0, s)),
            ]
            + [part] * len(more),
            [small, small] if more else part,
            [pltpu.VMEM((half, 4 * n), f32)] if more else [],
        ),
    )(place, normed_t, grad_t, grads, carried, *more, *tie)


def after(value, *earlier):
    return lax.optimization_barrier((value, *earlier))[0]


def swap_cores(value):
    return lax.ppermute(value, "col", [(0, 1), (1, 0)])


def across_first(value):
    return lax.ppermute(
        value, ("dp", "col"), [(2 * p + c, 2 * (p ^ (1 << c)) + c) for p in range(4) for c in range(2)]
    )


def across_second(value):
    return lax.ppermute(
        value, ("dp", "col"), [(2 * p + c, 2 * (p ^ (2 >> c)) + c) for p in range(4) for c in range(2)]
    )


def along_row(value, steps):
    return lax.ppermute(value, "row", [(i, (i + steps) % BLOCKS) for i in range(BLOCKS)])


def quarters(part):
    across = across_first(part)
    return (part, across, across_second(part), across_second(across))


def add(*parts):
    return sum(part.astype(f32) for part in parts).astype(bf16)


def upper(value):
    return value[: value.shape[0] // 2]


def lower(value):
    return value[value.shape[0] // 2 :]


def block_of(value, b, axis=0):
    width = value.shape[axis] // BLOCKS
    return lax.dynamic_slice_in_dim(value, b * width, width, axis)


def later_rows(value):
    pairs = [(i, i - 1) for i in range(1, 2 * BLOCKS)]
    value = lax.ppermute(value, ("row", "col"), pairs)
    parts = jnp.split(value, BLOCKS, axis=1)
    order = [OFFSETS.index(offset % BLOCKS - 1) for offset in OFFSETS]
    moved = jnp.concatenate([parts[i] for i in order], axis=1)
    return jnp.where(lax.axis_index("col") == 1, moved, value)


def shards(
    tokens,
    cotangent,
    seq_lens,
    norm1_gain,
    in_weight,
    conv_weight,
    out_weight,
    norm2_gain,
    gate_up_weight,
    down_weight,
):
    dp, row, core = lax.axis_index("dp"), lax.axis_index("row"), lax.axis_index("col")
    count, half = tokens.shape[0] // 2, tokens.shape[1]
    position = ((dp * BLOCKS + row) * 2 + core) * count
    lengths = lax.dynamic_slice_in_dim(seq_lens, position // ROW_LEN, 1, 0)[0]
    place = jnp.stack(
        [dp, core, position % ROW_LEN, lengths[0], lengths[0] + lengths[1]]
    ).astype(jnp.int32)

    def of_the_other(value):
        return lax.dynamic_slice_in_dim(value, (1 - core) * count, count, 0)

    mix_first = pack(in_weight, out_weight, place, 1, conv_weight)
    mix_quarters = [along_row(mix_first, -offset) for offset in OFFSETS[1:]]
    own_gains = jnp.pad(jnp.stack([norm1_gain, norm2_gain]), ((0, HALO - 2), (0, 0)))
    mix_own = pack(in_weight, out_weight, place, 4, tie=[mix_first])
    feed_own = pack(gate_up_weight, down_weight, place, 4, tie=[mix_own])
    before = lax.ppermute(
        after(tokens[2 * count - HALO :], mix_own), "row", [(i, i + 1) for i in range(BLOCKS - 1)]
    )
    joined = join_rows(mix_quarters, [mix_own, feed_own])
    theirs = swap_cores(outgoing(place, tokens, cotangent, before, own_gains, [joined]))
    feed_first = pack(gate_up_weight, down_weight, place, 1, tie=[joined])
    gains = jnp.concatenate([own_gains[:2], theirs[2 * count + HALO :][:2]], axis=1).astype(f32)
    gain_one, gain_two = gains[:1], gains[1:]
    normed, normed_t, low, low_t = prepare(
        place, tokens, theirs, before, cotangent, gain_one, [joined]
    )
    width = half // 4
    taps = jnp.concatenate(
        [conv_weight] + [part[width : width + KCONV, : conv_weight.shape[1]] for part in mix_quarters],
        axis=1,
    ).astype(f32)
    quarter_one = along_row(feed_first, -OFFSETS[1])
    mix_half = mix_assemble(mix_own, quarters(joined), place, [normed, quarter_one])
    mix_halves = [mix_half, swap_cores(mix_half)]
    half_one = lax.all_gather(after(quarter_one, mix_half), "dp", axis=0, tiled=True)

    *saved, hidden, carried, normed_two, normed_two_t = mix_forward(
        place, normed, mix_halves, tokens, theirs, taps, gain_two, []
    )
    feed_halves, others = [feed_own], [swap_cores(feed_own)]
    activations, from_them = [], []

    def gathered(k, last, here):
        part = along_row(after(feed_first, last), -OFFSETS[k])
        return lax.all_gather(after(part, here), "dp", axis=0, tiled=True)

    def have(half):
        feed_halves.append(half)
        others.append(swap_cores(half))

    def activate(grad, tie):
        k = len(activations)
        grad, acts, for_them = feed(
            normed_two, low, normed_two_t, low_t, feed_halves[k], others[k], grad, tie
        )
        activations.append(acts)
        from_them.append(swap_cores(for_them))
        return grad, for_them

    def weights_of(k, tie):
        keep, send = feed_weights(place, normed_two_t, low_t, activations[k], from_them[k], tie)
        return keep, across_second(send)

    grad_normed_two, done = activate(None, [])
    half_two = gathered(2, mix_half, done)
    have(after(half_one, done))
    grad_normed_two, last = activate(grad_normed_two, [])
    half_three = gathered(3, done, last)
    done = last
    keep, send = weights_of(0, [done])
    have(after(half_two, keep))
    grad_normed_two, done = activate(grad_normed_two, [keep])
    zero = (keep, send)
    keep, send = weights_of(1, [done, send])
    one = (keep, send)
    keep, send = weights_of(2, [keep])
    two = (keep, send)
    have(after(half_three, one[0]))
    grad_normed_two, done = activate(grad_normed_two, [keep])
    one_low, two_low = add(*map(lower, one)), add(*map(lower, two))
    one_across, two_across = across_first(one_low), across_first(two_low)
    first = first_rows(hidden, grad_normed_two, low, saved[1], gain_two, mix_halves)
    later = later_rows(first)
    keep, send = weights_of(3, [first, one_low, two_low])
    one = add(*map(upper, one), one_across)
    two = add(*map(upper, two), two_across)
    zero_across = across_first(after(add(*map(lower, zero)), keep))

    grad_own, grad_other, grads, grad_t, sums = mix_backward(
        place,
        hidden,
        grad_normed_two,
        low,
        tokens,
        theirs,
        saved,
        later,
        taps,
        gain_one,
        gain_two,
        mix_halves,
        [keep, one, two],
    )
    three = (keep, send)
    three_low = add(*map(lower, three))
    one, two = along_row(one, OFFSETS[1]), along_row(two, OFFSETS[2])
    where = jnp.array([OFFSETS.index(offset) for offset in (0, 1, 2, -1)], jnp.int32)
    own_taps = jnp.concatenate(
        [block_of(sums[2:], where[(b - row) % BLOCKS], 1) for b in range(BLOCKS)], axis=1
    )
    packed_sums = jnp.concatenate([sums[:2], own_taps], axis=0)
    every = lax.all_gather(packed_sums, ("dp", "row", "col"), axis=0)

    for_them = mix_weights(place, normed_t, grad_t, grads, carried, None, [one, three_low, packed_sums])
    received = swap_cores(for_them)
    three = add(*map(upper, three), across_first(three_low))
    grad_theirs = swap_cores(grad_other)
    input_back = join_tokens(grad_own, after(grad_theirs, for_them), place)
    keep, send = mix_weights(
        place, normed_t, grad_t, grads, carried, received, [three, two, input_back]
    )
    send = across_second(send)
    three = along_row(three, OFFSETS[3])
    own_out, other_out = feed_output(hidden, activations, feed_halves, others, [keep])
    send = after(send, own_out)
    other_out = swap_cores(other_out)
    mix_low = add(lower(keep), lower(send))
    mix_across = across_first(mix_low)
    three = after(three, mix_low)
    feed_sum = quarters(add(*map(upper, zero), zero_across, one, two, three))
    mix_quarters = jnp.split(add(upper(keep), upper(send), mix_across), BLOCKS, axis=1)
    mix_quarters = [along_row(part, OFFSETS[k]) if k else part for k, part in enumerate(mix_quarters)]
    mix_sum = quarters(add(*mix_quarters))
    output_back = join_tokens(own_out, other_out, place)
    gate_up_grad, down_grad = unpack(feed_sum, 2, place)
    in_grad, out_grad = unpack(mix_sum, 3, place)
    every = after(every, gate_up_grad)
    sums = jnp.sum(every.reshape(16, 2, *packed_sums.shape), axis=0)
    mine, other = sums[core], sums[1 - core]
    gain_grads = mine[:2, :half] + other[:2, half:]
    taps_grad = block_of(mine[2 : 2 + KCONV] + other[2 : 2 + KCONV], row, 1)
    return (
        output_back,
        input_back,
        gain_grads[0],
        in_grad,
        taps_grad,
        out_grad,
        gain_grads[1],
        gate_up_grad,
        down_grad,
    )


def from_behind(value, axis, steps):
    count = lax.axis_size(axis)
    leading, last = (max(0, -steps), min(count, count - steps))
    return lax.ppermute(value, axis, [(source, source + steps) for source in range(leading, last)])


def token_index(count, extra):
    flat_rank = (
        lax.axis_index("dp") * lax.axis_size("row") + lax.axis_index("row")
    ) * lax.axis_size("col") + lax.axis_index("col")
    return flat_rank * count + jnp.arange(count + extra, dtype=jnp.int32)


def flat_slot_masks(seq_lens, count, extra):
    position = token_index(count, extra)
    packed = position // ROW_LEN
    place = position - packed * ROW_LEN
    table = (packed[:, None] == jnp.arange(seq_lens.shape[0], dtype=jnp.int32)[None, :]).astype(
        jnp.int32
    )
    first = jnp.sum(table * seq_lens[None, :, 0], axis=1)
    second = jnp.sum(table * seq_lens[None, :, 1], axis=1)
    start = jnp.where(place < first, 0, first)
    valid_slot = (place < first + second).astype(jnp.float32)
    keep_masks = jnp.stack([(place - lag >= start).astype(jnp.float32) for lag in range(KCONV)])
    return (valid_slot[:count], keep_masks)


def collect(
    norm1_gain, in_weight, conv_weight, out_weight, norm2_gain, gate_up_weight, down_weight
):
    in_rows, conv_full, out_rows, gate_rows, down_rows = (
        lax.all_gather(in_weight, "row", axis=2, tiled=True),
        lax.all_gather(conv_weight, "row", axis=1, tiled=True),
        lax.all_gather(out_weight, "row", axis=0, tiled=True),
        lax.all_gather(gate_up_weight, "row", axis=2, tiled=True),
        lax.all_gather(down_weight, "row", axis=0, tiled=True),
    )
    gain_first, in_full, out_full, gain_second, gate_full, down_full = (
        lax.all_gather(norm1_gain, "col", axis=0, tiled=True),
        lax.all_gather(in_rows, "col", axis=1, tiled=True),
        lax.all_gather(out_rows, "col", axis=1, tiled=True),
        lax.all_gather(norm2_gain, "col", axis=0, tiled=True),
        lax.all_gather(gate_rows, "col", axis=1, tiled=True),
        lax.all_gather(down_rows, "col", axis=1, tiled=True),
    )
    return (gain_first, in_full, conv_full, out_full, gain_second, gate_full, down_full)


def flat_norm_backward(values, rstd, gain, grad_normed):
    scaled = grad_normed * gain
    gain_grad = jnp.sum(grad_normed * values * rstd, axis=0)
    grad_values = rstd * scaled - values * (rstd * rstd * rstd) * jnp.mean(
        scaled * values, axis=1, keepdims=True
    )
    return (grad_values, gain_grad)


def project(left, right):
    return jnp.dot(left, right, preferred_element_type=jnp.float32)


def weight_grad(left, right):
    return jnp.einsum("td,te->de", left, right, preferred_element_type=jnp.float32)


def back_project(grad, matrix):
    return jnp.einsum("te,de->td", grad, matrix, preferred_element_type=jnp.float32)


def flat_shards(
    tokens,
    cotangent,
    seq_lens,
    norm1_gain,
    in_weight,
    conv_weight,
    out_weight,
    norm2_gain,
    gate_up_weight,
    down_weight,
):
    own_tokens, own_cotangent = (
        lax.all_to_all(tokens, "col", split_axis=0, concat_axis=1, tiled=True),
        lax.all_to_all(cotangent, "col", split_axis=0, concat_axis=1, tiled=True),
    )
    gain_first, in_full, conv_full, out_full, gain_second, gate_full, down_full = collect(
        norm1_gain, in_weight, conv_weight, out_weight, norm2_gain, gate_up_weight, down_weight
    )
    count, width = own_tokens.shape
    reach = KCONV - 1
    valid_slot, keep_masks = flat_slot_masks(seq_lens, count, reach)
    conv_taps = conv_full.astype(jnp.float32)
    gain_one_f = gain_first.astype(jnp.float32)
    gain_two_f = gain_second.astype(jnp.float32)
    inputs = own_tokens.astype(jnp.float32)
    rstd_first = lax.rsqrt(jnp.mean(inputs * inputs, axis=1, keepdims=True) + eps)
    normed = (inputs * rstd_first * gain_one_f).astype(jnp.bfloat16)
    gate_b = project(normed, in_full[0])
    gate_c = project(normed, in_full[1])
    value_part = project(normed, in_full[2])
    product = gate_b * value_part
    earlier = from_behind(product[count - reach :], ("row", "col"), 1)
    extended = jnp.concatenate([earlier, product], axis=0)
    conv = jnp.zeros((count, width), jnp.float32)
    for lag in range(KCONV):
        conv = (
            conv
            + conv_taps[lag]
            * keep_masks[lag, :count, None]
            * extended[reach - lag : reach - lag + count]
        )
    carried = (gate_c * conv).astype(jnp.bfloat16)
    hidden = inputs + project(carried, out_full)
    rstd_second = lax.rsqrt(jnp.mean(hidden * hidden, axis=1, keepdims=True) + eps)
    normed_two = (hidden * rstd_second * gain_two_f).astype(jnp.bfloat16)
    gate = project(normed_two, gate_full[0])
    up_part = project(normed_two, gate_full[1])
    sigmoid_gate = jax.nn.sigmoid(gate)
    silu_gate = gate * sigmoid_gate
    active = (silu_gate * up_part).astype(jnp.bfloat16)
    output = hidden + project(active, down_full)
    grad_out = own_cotangent.astype(jnp.float32) * valid_slot[:, None]
    grad_low = grad_out.astype(jnp.bfloat16)
    down_grad = weight_grad(active, grad_low)
    grad_active = back_project(grad_low, down_full)
    grad_gate = (grad_active * up_part * sigmoid_gate * (1.0 + gate * (1.0 - sigmoid_gate))).astype(
        jnp.bfloat16
    )
    grad_up = (grad_active * silu_gate).astype(jnp.bfloat16)
    gate_grad = jnp.stack([weight_grad(normed_two, grad_gate), weight_grad(normed_two, grad_up)])
    grad_normed_two = back_project(grad_gate, gate_full[0]) + back_project(grad_up, gate_full[1])
    grad_second, gain_second_part = flat_norm_backward(hidden, rstd_second, gain_two_f, grad_normed_two)
    grad_hidden = grad_out + grad_second
    grad_o = grad_hidden.astype(jnp.bfloat16)
    out_grad = weight_grad(carried, grad_o)
    grad_carried = back_project(grad_o, out_full)
    grad_gate_c = (grad_carried * conv).astype(jnp.bfloat16)
    grad_conv = grad_carried * gate_c
    later = from_behind(grad_conv[:reach], ("row", "col"), -1)
    grad_extended = jnp.concatenate([grad_conv, later], axis=0)
    grad_product = jnp.zeros((count, width), jnp.float32)
    conv_rows = []
    for lag in range(KCONV):
        masked = keep_masks[lag, :, None] * grad_extended
        grad_product = grad_product + conv_taps[lag] * masked[lag : lag + count]
        conv_rows.append(
            jnp.sum(masked[:count] * extended[reach - lag : reach - lag + count], axis=0)
        )
    conv_grad = jnp.stack(conv_rows)
    grad_gate_b = (grad_product * value_part).astype(jnp.bfloat16)
    grad_value = (grad_product * gate_b).astype(jnp.bfloat16)
    in_grad = jnp.stack(
        [
            weight_grad(normed, grad_gate_b),
            weight_grad(normed, grad_gate_c),
            weight_grad(normed, grad_value),
        ]
    )
    grad_normed = (
        back_project(grad_gate_b, in_full[0])
        + back_project(grad_gate_c, in_full[1])
        + back_project(grad_value, in_full[2])
    )
    grad_first, gain_first_part = flat_norm_backward(inputs, rstd_first, gain_one_f, grad_normed)
    input_grad = (grad_hidden + grad_first).astype(jnp.bfloat16)
    output_back, input_back = (
        lax.all_to_all(output.astype(jnp.bfloat16), "col", split_axis=1, concat_axis=0, tiled=True),
        lax.all_to_all(input_grad, "col", split_axis=1, concat_axis=0, tiled=True),
    )
    in_cols, out_cols, gate_cols, down_cols = (
        lax.psum_scatter(in_grad, "col", scatter_dimension=1, tiled=True),
        lax.psum_scatter(out_grad, "col", scatter_dimension=1, tiled=True),
        lax.psum_scatter(gate_grad, "col", scatter_dimension=1, tiled=True),
        lax.psum_scatter(down_grad, "col", scatter_dimension=1, tiled=True),
    )
    in_part, out_part, gate_part, down_part = (
        lax.psum_scatter(in_cols, "row", scatter_dimension=2, tiled=True),
        lax.psum_scatter(out_cols, "row", scatter_dimension=0, tiled=True),
        lax.psum_scatter(gate_cols, "row", scatter_dimension=2, tiled=True),
        lax.psum_scatter(down_cols, "row", scatter_dimension=0, tiled=True),
    )
    in_sum, out_sum, gate_sum, down_sum = lax.psum((in_part, out_part, gate_part, down_part), "dp")
    gain_one_sum, gain_two_sum, conv_sum = lax.psum(
        (gain_first_part, gain_second_part, conv_grad), ("dp", "row", "col")
    )
    col_width = width // lax.axis_size("col")
    row_width = width // lax.axis_size("row")
    gain_first_grad = lax.dynamic_slice_in_dim(
        gain_one_sum, lax.axis_index("col") * col_width, col_width
    )
    gain_second_grad = lax.dynamic_slice_in_dim(
        gain_two_sum, lax.axis_index("col") * col_width, col_width
    )
    conv_weight_grad = lax.dynamic_slice_in_dim(
        conv_sum, lax.axis_index("row") * row_width, row_width, axis=1
    )
    return (
        output_back,
        input_back,
        gain_first_grad,
        in_sum,
        conv_weight_grad,
        out_sum,
        gain_second_grad,
        gate_sum,
        down_sum,
    )


def solution(mesh):
    ring = mesh.shape["dp"] == 4 and mesh.shape["row"] == BLOCKS and mesh.shape["col"] == 2
    return jax.shard_map(
        shards if ring else flat_shards,
        mesh=mesh,
        in_specs=(
            P(("dp", "row"), "col"),
            P(("dp", "row"), "col"),
            P(),
            P("col"),
            P(None, "col", "row"),
            P(None, "row"),
            P("row", "col"),
            P("col"),
            P(None, "col", "row"),
            P("row", "col"),
        ),
        out_specs=(
            P(("dp", "row"), "col"),
            P(("dp", "row"), "col"),
            P("col"),
            P(None, "col", "row"),
            P(None, "row"),
            P("row", "col"),
            P("col"),
            P(None, "col", "row"),
            P("row", "col"),
        ),
        check_vma=False,
    )
```

```python
import functools

import jax
import jax.numpy as jnp
from jax import lax
from jax.experimental import pallas as pl
from jax.experimental.pallas import tpu as pltpu
from jax.sharding import PartitionSpec as P

KCONV = 3
ROW_LEN = 8192
BLOCKS = 4
OFFSETS = (0, -1, 1, 2)
HALO = 16
STEP = 256
WIDE = 512


eps = 1e-05
bf16 = jnp.bfloat16
f32 = jnp.float32
VMEM_LIMIT = 64000 * 1024
HERE = pl.BlockSpec(memory_space=pl.ANY)
SCALARS = pl.BlockSpec(memory_space=pltpu.SMEM)


def dot(left, right):
    return jnp.dot(left, right, preferred_element_type=f32)


def dot_nt(left, right):
    return lax.dot_general(left, right, (((1,), (1,)), ((), ())), preferred_element_type=f32)


def shape_of(*dims, dtype=bf16):
    return jax.ShapeDtypeStruct(dims, dtype)


def call(body, name, out_shape, flops=0, moved=0, tie=(), n_in=None, **kwargs):
    if tie:
        inner, at = body, n_in

        def body(*refs):
            inner(*refs[:at], *refs[at + len(tie) :])

        if "grid_spec" in kwargs:
            spec = kwargs["grid_spec"]
            kwargs["grid_spec"] = pltpu.PrefetchScalarGridSpec(
                num_scalar_prefetch=1,
                grid=spec.grid,
                in_specs=list(spec.in_specs) + [HERE] * len(tie),
                out_specs=spec.out_specs,
                scratch_shapes=spec.scratch_shapes,
            )
        else:
            kwargs["in_specs"] = list(kwargs["in_specs"]) + [HERE] * len(tie)
    return pl.pallas_call(
        body,
        out_shape=out_shape,
        name=name,
        compiler_params=pltpu.CompilerParams(vmem_limit_bytes=VMEM_LIMIT),
        cost_estimate=pl.CostEstimate(flops=flops, bytes_accessed=moved, transcendentals=0),
        **kwargs,
    )


def scalar_grid(grid, in_specs, out_specs, scratch_shapes=()):
    return pltpu.PrefetchScalarGridSpec(
        num_scalar_prefetch=1,
        grid=grid,
        in_specs=in_specs,
        out_specs=out_specs,
        scratch_shapes=scratch_shapes,
    )


def quarter_of(place, j):
    dp, core = place[0], place[1]
    low, high = j % 2, j // 2
    mask = jnp.where(core == 0, 2 * high + low, 2 * low + high)
    return jnp.bitwise_xor(dp, mask)


def join_tokens(mine, theirs, place):
    count, half = mine.shape

    def body(place, mine, theirs, out):
        own = pl.program_id(0) == place[1]

        @pl.when(own)
        def _():
            out[...] = mine[...]

        @pl.when(jnp.logical_not(own))
        def _():
            out[...] = theirs[...]

    kept = pl.BlockSpec((count, half), lambda h, place: (0, 0))
    return call(
        body,
        "join_tokens",
        shape_of(2 * count, half),
        grid_spec=scalar_grid(
            (2,), [kept, kept], pl.BlockSpec((count, half), lambda h, place: (h, 0))
        ),
    )(place, mine, theirs)


def outgoing(place, tokens, cotangent, before, gains, tie):
    count, half = tokens.shape[0] // 2, tokens.shape[1]
    rows = 2 * count + 2 * HALO

    def body(place, tokens, cotangent, between, before, gains, out):
        out[:count] = tokens[...]
        out[count : 2 * count] = cotangent[...]

        @pl.when(place[1] == 0)
        def _():
            out[2 * count : 2 * count + HALO] = between[...]

        @pl.when(place[1] == 1)
        def _():
            out[2 * count : 2 * count + HALO] = before[...]

        out[2 * count + HALO :] = gains[...]

    theirs = pl.BlockSpec((count, half), lambda i, place: (1 - place[1], 0))
    few = pl.BlockSpec((HALO, half), lambda i, place: (0, 0))
    return call(
        body,
        "outgoing",
        shape_of(rows, half),
        tie=tie,
        n_in=6,
        grid_spec=scalar_grid(
            (1,),
            [theirs, theirs, pl.BlockSpec((HALO, half), lambda i, place: (count // HALO - 1, 0)), few, few],
            pl.BlockSpec((rows, half), lambda i, place: (0, 0)),
        ),
    )(place, tokens, cotangent, tokens, before, gains, *tie)


def pack(stack, turned, place, quarters, rows=None, tie=()):
    k, half, n = stack.shape
    width = half // 4
    lanes = (k + 1) * n
    below = [] if rows is None else [rows]

    def body(place, stack, turned, *refs):
        out = refs[-1]
        for i in range(k):
            out[:width, i * n : (i + 1) * n] = stack[i]
        out[:width, k * n :] = turned[...].astype(f32).T.astype(out.dtype)
        if below:
            out[width:, :] = jnp.zeros((HALO, lanes), out.dtype)
            out[width : width + KCONV, :n] = refs[0][...]

    def source(j, place):
        return place[0] if quarters == 1 else j

    return call(
        body,
        "pack",
        shape_of(quarters * width + HALO * len(below), lanes),
        tie=tie,
        n_in=3 + len(below),
        grid_spec=scalar_grid(
            (quarters,),
            [
                pl.BlockSpec((k, width, n), lambda j, place: (0, source(j, place), 0)),
                pl.BlockSpec((n, width), lambda j, place: (0, source(j, place))),
            ]
            + [pl.BlockSpec((KCONV, n), lambda j, place: (0, 0))] * len(below),
            pl.BlockSpec((width + HALO * len(below), lanes), lambda j, place: (j, 0)),
        ),
    )(place, stack, turned, *below, *tie)


def join_rows(parts, tie):
    rows, lanes = parts[0].shape

    def body(*refs):
        for i in range(len(parts)):
            refs[-1][i * rows : (i + 1) * rows] = refs[i][...]

    whole = pl.BlockSpec(memory_space=pltpu.VMEM)
    return call(
        body,
        "join_rows",
        shape_of(len(parts) * rows, lanes),
        tie=tie,
        n_in=len(parts),
        in_specs=[whole] * len(parts),
        out_specs=whole,
    )(*parts, *tie)


def mix_assemble(own, pieces, place, tie):
    half, lanes = own.shape
    width = half // 4
    stride = width + HALO

    def body(place, own, *refs):
        out = refs[-1]
        out[0] = own[...]
        for s in range(1, BLOCKS):
            for j in range(4):
                rows = pl.ds(pl.multiple_of(quarter_of(place, j) * width, width), width)
                out[s, rows, :] = refs[j][(s - 1) * stride : (s - 1) * stride + width, :]

    whole = pl.BlockSpec(memory_space=pltpu.VMEM)
    return call(
        body,
        "mix_assemble",
        shape_of(BLOCKS, half, lanes),
        tie=tie,
        n_in=6,
        in_specs=[SCALARS] + [whole] * 5,
        out_specs=whole,
    )(place, own, *pieces, *tie)


def unpack(pieces, k, place):
    width, lanes = pieces[0].shape
    half, n = 4 * width, lanes // (k + 1)

    def body(place, *refs):
        stack, turned = refs[4:]
        for j in range(4):

            @pl.when(pl.program_id(0) == j)
            def _(piece=refs[j]):
                for i in range(k):
                    stack[i] = piece[:, i * n : (i + 1) * n].astype(f32)
                turned[...] = piece[:, k * n :].astype(f32).T

    whole = pl.BlockSpec((width, lanes), lambda j, place: (0, 0))
    return call(
        body,
        "unpack",
        (shape_of(k, half, n, dtype=f32), shape_of(n, half, dtype=f32)),
        grid_spec=scalar_grid(
            (4,),
            [whole] * 4,
            [
                pl.BlockSpec((k, width, n), lambda j, place: (0, quarter_of(place, j), 0)),
                pl.BlockSpec((n, width), lambda j, place: (0, quarter_of(place, j))),
            ],
        ),
    )(place, *pieces)


def rows_of(i, step=STEP):
    return pl.ds(pl.multiple_of(i * step, step), step)


def slots(place, start, count):
    slot = place[2] + start + lax.broadcasted_iota(jnp.int32, (count, 1), 0)
    return slot, jnp.where(slot < place[3], 0, place[3])


def inverse_rms(*parts):
    width = sum(part.shape[1] for part in parts)
    total = sum(jnp.sum(part * part, axis=1, keepdims=True) for part in parts)
    return lax.rsqrt(total / width + eps)


def prepare(place, tokens, theirs, before, cotangent, gain, tie):
    count, half = tokens.shape[0] // 2, tokens.shape[1]
    width = 2 * half

    def body(
        place, own, other, before, between, halo_other, cot, cot_other, gain, normed, normed_t, low, low_t
    ):
        def norm(left, right):
            left, right = left.astype(f32), right.astype(f32)
            rstd = inverse_rms(left, right)
            return (
                (left * rstd * gain[:, :half]).astype(bf16),
                (right * rstd * gain[:, half:]).astype(bf16),
            )

        halo = jnp.where(place[1] == 0, before[...].astype(f32), between[...].astype(f32))

        @pl.when(pl.program_id(0) == 0)
        def _():
            left, right = norm(halo, halo_other[...])
            normed[:HALO, :half] = left
            normed[:HALO, half:] = right

        tile = pl.program_id(0)
        here = pl.ds(pl.multiple_of(HALO + tile * STEP, HALO), STEP)
        for i, value in enumerate(norm(own[...], other[...])):
            lanes = slice(i * half, (i + 1) * half)
            normed[here, lanes] = value
            normed_t[lanes, :] = value.astype(f32).T.astype(bf16)
        slot, _ = slots(place, tile * STEP, STEP)
        valid = (slot < place[4]).astype(f32)
        for i, value in enumerate((cot[...], cot_other[...])):
            lanes = slice(i * half, (i + 1) * half)
            value = value.astype(f32) * valid
            low[:, lanes] = value.astype(bf16)
            low_t[lanes, :] = value.T.astype(bf16)

    tiles = count // STEP
    mine = pl.BlockSpec((STEP, half), lambda m, place: (place[1] * tiles + m, 0))

    def received(first):
        return pl.BlockSpec((STEP, half), lambda m, place: (first + m, 0))

    def few(block):
        return pl.BlockSpec((HALO, half), lambda m, place: (block, 0))

    turned = pl.BlockSpec((width, STEP), lambda m, place: (0, m))
    return call(
        body,
        "prepare",
        (
            shape_of(HALO + count, width),
            shape_of(width, count),
            shape_of(count, width),
            shape_of(width, count),
        ),
        moved=16 * count * width,
        tie=tie,
        n_in=9,
        grid_spec=scalar_grid(
            (tiles,),
            [
                mine,
                received(0),
                few(0),
                few(count // HALO - 1),
                few(2 * count // HALO),
                mine,
                received(tiles),
                pl.BlockSpec((1, width), lambda m, place: (0, 0)),
            ],
            [
                pl.BlockSpec((HALO + count, width), lambda m, place: (0, 0)),
                turned,
                pl.BlockSpec((STEP, width), lambda m, place: (m, 0)),
                turned,
            ],
        ),
    )(place, tokens, theirs, before, tokens, theirs, cotangent, theirs, gain, *tie)


def mix_copies(sources, inward, outward, sems):
    copies = []
    for s in range(BLOCKS):
        for side in range(2):
            source = sources[side].at[s]
            half, lanes = source.shape
            n = lanes // 4
            rows = pl.ds(side * half, half)
            at = 4 * s + 2 * side
            copies.append(
                pltpu.make_async_copy(
                    source.at[:, pl.ds(0, 3 * n)],
                    inward.at[rows, pl.ds(s * 3 * n, 3 * n)],
                    sems.at[at],
                )
            )
            copies.append(
                pltpu.make_async_copy(
                    source.at[:, pl.ds(3 * n, n)],
                    outward.at[rows, pl.ds(s * n, n)],
                    sems.at[at + 1],
                )
            )
    return copies


def mix_forward(place, normed, halves, tokens, theirs, taps, gain, tie):
    count, half = tokens.shape[0] // 2, tokens.shape[1]
    width = 2 * half
    n = width // BLOCKS
    part = (HALO + count) // 5
    kept = 4

    def body(place, *refs):
        normed_hbm, sources, refs = refs[0], refs[1:3], refs[3:]
        tokens_hbm, theirs_hbm, taps, gain = refs[:4]
        results, hidden_hbm, carried_hbm, normed2_hbm, turned_hbm = (
            refs[4:8],
            refs[8],
            refs[9],
            refs[10],
            refs[11],
        )
        normed, inward, outward, mine, other, mixed, product, carried, hidden, normed2, turned = refs[
            12:23
        ]
        saved = refs[23:27]
        in_sems, weight_sems, saved_sems, out_sems = refs[27:]
        loads = [
            pltpu.make_async_copy(normed_hbm, normed, in_sems.at[0]),
            pltpu.make_async_copy(
                tokens_hbm.at[pl.ds(pl.multiple_of(place[1] * count, count), count)],
                mine,
                in_sems.at[1],
            ),
            pltpu.make_async_copy(theirs_hbm.at[pl.ds(0, count)], other, in_sems.at[2]),
        ]
        weights = mix_copies(sources, inward, outward, weight_sems)
        loads[0].start()
        for copy in weights:
            copy.start()
        loads[1].start()
        loads[2].start()
        loads[0].wait()
        pending = []
        for s in range(BLOCKS):
            for copy in weights[4 * s : 4 * s + 4]:
                copy.wait()

            def project(i, carry, s=s):
                rows = rows_of(i, part)
                value = dot(normed[rows, :], inward[:, s * 3 * n : (s + 1) * 3 * n])
                mixed[rows, :] = value
                product[rows, :] = value[:, :n] * value[:, 2 * n :]
                return carry

            lax.fori_loop(0, 5, project, 0)
            lanes = slice(s * n, (s + 1) * n)
            for m in range(count // STEP):
                first = HALO + m * STEP
                rows = slice(m * STEP, (m + 1) * STEP)
                slot, start = slots(place, m * STEP, STEP)
                conv = jnp.zeros((STEP, n), f32)
                for lag in range(KCONV):
                    keep = (slot - lag >= start).astype(f32)
                    conv = conv + taps[lag : lag + 1, lanes] * (
                        keep * product[first - lag : first - lag + STEP, :]
                    )
                inside = mixed[first : first + STEP, :]
                carried[rows, lanes] = (inside[:, n : 2 * n] * conv).astype(bf16)
                for i, value in enumerate((inside[:, :n], inside[:, n : 2 * n], inside[:, 2 * n :], conv)):
                    saved[i][rows, lanes] = value.astype(bf16)
            for i in range(kept):
                copy = pltpu.make_async_copy(
                    saved[i].at[:, pl.ds(s * n, n)],
                    results[i].at[:, pl.ds(s * n, n)],
                    saved_sems.at[kept * s + i],
                )
                copy.start()
                pending.append(copy)
        copy = pltpu.make_async_copy(carried, carried_hbm, in_sems.at[3])
        copy.start()
        pending.append(copy)
        loads[1].wait()
        loads[2].wait()
        for m in range(count // STEP):
            rows = slice(m * STEP, (m + 1) * STEP)
            term = dot_nt(carried[rows, :], outward[...])
            left = mine[rows, :].astype(f32) + term[:, :half]
            right = other[rows, :].astype(f32) + term[:, half:]
            rstd = inverse_rms(left, right)
            for i, value in enumerate((left, right)):
                lanes = slice(i * half, (i + 1) * half)
                hidden[rows, lanes] = value
                value = value * rstd * gain[:, lanes]
                normed2[rows, lanes] = value.astype(bf16)
                turned[lanes, rows] = value.T.astype(bf16)
            for i, (source, target, by) in enumerate(
                (
                    (hidden, hidden_hbm, 0),
                    (normed2, normed2_hbm, 0),
                    (turned, turned_hbm, 1),
                )
            ):
                here = pl.ds(m * STEP, STEP)
                source, target = (
                    (source.at[:, here], target.at[:, here])
                    if by
                    else (source.at[here], target.at[here])
                )
                copy = pltpu.make_async_copy(source, target, out_sems.at[3 * m + i])
                copy.start()
                pending.append(copy)
        for copy in pending:
            copy.wait()

    tiles = count // STEP
    wide = shape_of(count, width, dtype=f32)
    flat = shape_of(count, width)
    whole = pl.BlockSpec(memory_space=pltpu.VMEM)
    return call(
        body,
        "mix_forward",
        (flat, flat, flat, flat, wide, flat, flat, shape_of(width, count)),
        flops=8 * count * width * width,
        moved=30 * count * width + 8 * width * width,
        tie=tie,
        n_in=8,
        in_specs=[SCALARS] + [HERE] * 5 + [whole] * 2,
        out_specs=(HERE,) * 8,
        scratch_shapes=[
            pltpu.VMEM((HALO + count, width), bf16),
            pltpu.VMEM((width, 3 * width), bf16),
            pltpu.VMEM((width, width), bf16),
            pltpu.VMEM((count, half), bf16),
            pltpu.VMEM((count, half), bf16),
            pltpu.VMEM((HALO + count, 3 * n), f32),
            pltpu.VMEM((HALO + count, n), f32),
            pltpu.VMEM((count, width), bf16),
            pltpu.VMEM((count, width), f32),
            pltpu.VMEM((count, width), bf16),
            pltpu.VMEM((width, count), bf16),
        ]
        + [pltpu.VMEM((count, width), bf16)] * kept
        + [
            pltpu.SemaphoreType.DMA((4,)),
            pltpu.SemaphoreType.DMA((4 * BLOCKS,)),
            pltpu.SemaphoreType.DMA((kept * BLOCKS,)),
            pltpu.SemaphoreType.DMA((3 * tiles,)),
        ],
    )(place, normed, *halves, tokens, theirs, taps, gain, *tie)


def feed_body(
    lanes,
    started,
    normed_hbm,
    low_hbm,
    normed_t_hbm,
    low_t_hbm,
    own_hbm,
    other_hbm,
    grad_in,
    grad_hbm,
    acts_hbm,
    theirs_hbm,
    normed,
    low,
    normed_t,
    low_t,
    weights,
    grad,
    acts,
    theirs,
    in_sems,
    grad_sems,
    acts_sems,
    their_sems,
):
    f = lanes // 3
    count, width = normed.shape
    half = width // 2
    loads = [
        pltpu.make_async_copy(source, target, in_sems.at[i])
        for i, (source, target) in enumerate(
            (
                (normed_hbm, normed),
                (own_hbm, weights.at[pl.ds(0, half)]),
                (other_hbm, weights.at[pl.ds(half, half)]),
                (low_hbm, low),
                (normed_t_hbm.at[pl.ds(half, half)], normed_t),
                (low_t_hbm.at[pl.ds(half, half)], low_t),
            )
        )
    ]
    if started:
        loads.append(pltpu.make_async_copy(grad_in, grad, in_sems.at[6]))
    for load in loads[:4]:
        load.start()
    for load in loads[:4]:
        load.wait()
    for load in loads[4:]:
        load.start()

    def acts_copy(i):
        rows = rows_of(i, WIDE)
        return pltpu.make_async_copy(acts.at[rows], acts_hbm.at[rows], acts_sems.at[i])

    def activations(i, carry):
        rows = rows_of(i, WIDE)
        for start in range(0, f, 256):
            stop = min(start + 256, f)
            gate_lanes = slice(start, stop)
            up_lanes = slice(f + start, f + stop)
            down_lanes = slice(2 * f + start, 2 * f + stop)
            gate = dot(normed[rows, :], weights[:, gate_lanes])
            up_part = dot(normed[rows, :], weights[:, up_lanes])
            grad_active = dot(low[rows, :], weights[:, down_lanes])
            sigmoid_gate = jax.nn.sigmoid(gate)
            silu_gate = gate * sigmoid_gate
            acts[rows, gate_lanes] = (
                grad_active * up_part * sigmoid_gate * (1.0 + gate * (1.0 - sigmoid_gate))
            ).astype(bf16)
            acts[rows, up_lanes] = (grad_active * silu_gate).astype(bf16)
            acts[rows, down_lanes] = (silu_gate * up_part).astype(bf16)
        acts_copy(i).start()
        return carry

    lax.fori_loop(0, count // WIDE, activations, 0)
    loads[4].wait()
    loads[5].wait()

    def their_copy(i):
        rows = rows_of(i, WIDE)
        return pltpu.make_async_copy(theirs.at[rows], theirs_hbm.at[rows], their_sems.at[i])

    def outer(i, carry):
        rows = rows_of(i, WIDE)
        theirs[rows, : 2 * f] = dot(normed_t[rows, :], acts[:, : 2 * f]).astype(bf16)
        theirs[rows, 2 * f :] = dot(low_t[rows, :], acts[:, 2 * f :]).astype(bf16)
        their_copy(i).start()
        return carry

    lax.fori_loop(0, half // WIDE, outer, 0)
    if started:
        loads[6].wait()

    def grad_copy(i):
        rows = rows_of(i, WIDE)
        return pltpu.make_async_copy(grad.at[rows], grad_hbm.at[rows], grad_sems.at[i])

    def inner(i, carry):
        rows = rows_of(i, WIDE)
        term = dot_nt(acts[rows, : 2 * f], weights[:, : 2 * f])
        grad[rows, :] = grad[rows, :] + term if started else term
        grad_copy(i).start()
        return carry

    lax.fori_loop(0, count // WIDE, inner, 0)
    for i in range(half // WIDE):
        their_copy(i).wait()
    for i in range(count // WIDE):
        acts_copy(i).wait()
        grad_copy(i).wait()


def feed(normed, low, normed_t, low_t, own, other, grad, tie):
    count, width = normed.shape
    half, lanes = own.shape
    f = lanes // 3
    started = grad is not None
    tiles = count // WIDE
    before = [grad] if started else []
    body = functools.partial(feed_body, lanes, started)
    if not started:
        inner = body

        def body(*refs):
            inner(*refs[:6], None, *refs[6:])

    return call(
        body,
        "feed",
        (shape_of(count, width, dtype=f32), shape_of(count, lanes), shape_of(half, lanes)),
        flops=13 * count * width * f,
        moved=2 * (4 * count * width + 3 * half * lanes + count * lanes) + 8 * count * width,
        tie=tie,
        n_in=6 + len(before),
        in_specs=[HERE] * (6 + len(before)),
        out_specs=(HERE,) * 3,
        scratch_shapes=[
            pltpu.VMEM((count, width), bf16),
            pltpu.VMEM((count, width), bf16),
            pltpu.VMEM((half, count), bf16),
            pltpu.VMEM((half, count), bf16),
            pltpu.VMEM((width, lanes), bf16),
            pltpu.VMEM((count, width), f32),
            pltpu.VMEM((count, lanes), bf16),
            pltpu.VMEM((half, lanes), bf16),
            pltpu.SemaphoreType.DMA((7,)),
            pltpu.SemaphoreType.DMA((tiles,)),
            pltpu.SemaphoreType.DMA((tiles,)),
            pltpu.SemaphoreType.DMA((half // WIDE,)),
        ],
    )(normed, low, normed_t, low_t, own, other, *before, *tie)


def feed_output(hidden, acts, owns, others, tie):
    count, width = hidden.shape
    half, lanes = owns[0].shape
    f = lanes // 3

    def body(hidden, *refs):
        acts, owns, others, outs = refs[:4], refs[4:8], refs[8:12], refs[12:]
        for side, weights in enumerate((owns, others)):
            total = hidden[:, side * half : (side + 1) * half]
            for k in range(BLOCKS):
                total = total + dot_nt(acts[k][...], weights[k][...])
            outs[side][...] = total.astype(bf16)

    rows = pl.BlockSpec((STEP, f), lambda m: (m, 2))
    whole = pl.BlockSpec((half, f), lambda m: (0, 2))
    part = pl.BlockSpec((STEP, half), lambda m: (m, 0))
    return call(
        body,
        "feed_output",
        (shape_of(count, half),) * 2,
        flops=2 * BLOCKS * count * width * f,
        moved=2 * BLOCKS * (count + width) * f + 6 * count * width,
        tie=tie,
        n_in=13,
        grid=(count // STEP,),
        in_specs=[pl.BlockSpec((STEP, width), lambda m: (m, 0))] + [rows] * 4 + [whole] * 8,
        out_specs=(part, part),
    )(hidden, *acts, *owns, *others, *tie)


def keep_and_send(place, total, keep, send):
    width = keep.shape[0] // 2
    for j in range(4):
        target = keep if j < 2 else send
        rows = pl.ds(pl.multiple_of(quarter_of(place, j) * width, width), width)
        target[(j % 2) * width : (j % 2 + 1) * width, :] = total[rows, :].astype(bf16)


def feed_weights(place, normed_t, low_t, acts, received, tie):
    width, count = normed_t.shape
    half, lanes = received.shape
    f = lanes // 3
    step = f

    def body(place, normed_t, low_t, acts, received, keep, send, total):
        def put(left):
            total[...] = dot(left[...], acts[...]) + received[...].astype(f32)

        is_down = pl.program_id(0) >= 2 * f // step

        @pl.when(jnp.logical_not(is_down))
        def _():
            put(normed_t)

        @pl.when(is_down)
        def _():
            put(low_t)

        keep_and_send(place, total, keep, send)

    left = pl.BlockSpec((half, count), lambda j, place: (0, 0))
    part = pl.BlockSpec((half // 2, step), lambda j, place: (0, j))
    return call(
        body,
        "feed_weights",
        (shape_of(half // 2, lanes),) * 2,
        flops=6 * count * half * f,
        moved=2 * (2 * half * count + count * lanes + 2 * half * lanes),
        tie=tie,
        n_in=5,
        grid_spec=scalar_grid(
            (lanes // step,),
            [
                left,
                left,
                pl.BlockSpec((count, step), lambda j, place: (0, j)),
                pl.BlockSpec((half, step), lambda j, place: (0, j)),
            ],
            [part, part],
            [pltpu.VMEM((half, step), f32)],
        ),
    )(place, normed_t, low_t, acts, received, *tie)


def hidden_backward(hidden, grad_normed, grad_out, gain):
    width = hidden.shape[1]
    rstd = lax.rsqrt(jnp.sum(hidden * hidden, axis=1, keepdims=True) / width + eps)
    scaled = grad_normed * gain
    mean = jnp.sum(scaled * hidden, axis=1, keepdims=True) / width
    grad = grad_out + (rstd * scaled - hidden * (rstd * rstd * rstd) * mean)
    return grad, grad_normed * hidden * rstd


def first_rows(hidden, grad_normed, low, gate_c, gain, halves):
    width = hidden.shape[1]
    n = width // BLOCKS
    half = width // 2

    def body(hidden, grad_normed, low, gate_c, gain, *refs):
        grad, _ = hidden_backward(hidden[...], grad_normed[...], low[...].astype(f32), gain[...])
        grad_o = grad.astype(bf16)
        for s in range(BLOCKS):
            value = dot(grad_o[:, :half], refs[0][s]) + dot(grad_o[:, half:], refs[1][s])
            lanes = slice(s * n, (s + 1) * n)
            refs[-1][:, lanes] = (value * gate_c[:, lanes].astype(f32))[:8]

    few = pl.BlockSpec((HALO, width), lambda i: (0, 0))
    return call(
        body,
        "first_rows",
        shape_of(8, width, dtype=f32),
        grid=(1,),
        in_specs=[few] * 4
        + [pl.BlockSpec((1, width), lambda i: (0, 0))]
        + [pl.BlockSpec((BLOCKS, half, n), lambda i: (0, 0, 3))] * 2,
        out_specs=pl.BlockSpec((8, width), lambda i: (0, 0)),
    )(hidden, grad_normed, low, gate_c, gain, *halves)


def mix_backward(
    place, hidden, grad_normed, low, tokens, theirs, saved, later, taps, gain_one, gain_two, halves, tie
):
    count, width = hidden.shape
    half = width // 2
    n = width // BLOCKS
    tiles = count // STEP

    def body(place, *refs):
        hidden, grad_normed, low, mine, other = refs[:5]
        gate_b, gate_c, value_part, conv, later, taps, gain_one, gain_two = refs[5:13]
        sources = refs[13:15]
        grad_own, grad_other, grads, turned, sums = refs[15:20]
        inward, outward, extended, sems = refs[20:]
        step = pl.program_id(0)
        tile = tiles - 1 - step

        @pl.when(step == 0)
        def _():
            copies = mix_copies(sources, inward, outward, sems)
            for copy in copies:
                copy.start()
            sums[...] = jnp.zeros_like(sums)
            extended[STEP:, :] = later[...]
            for copy in copies:
                copy.wait()

        @pl.when(step > 0)
        def _():
            extended[STEP:, :] = extended[:8, :]

        grad, gain_terms = hidden_backward(
            hidden[...], grad_normed[...], low[...].astype(f32), gain_two[...]
        )
        sums[1:2, :] += jnp.sum(gain_terms, axis=0, keepdims=True)
        grad_o = grad.astype(bf16)
        turned[...] = grad.T.astype(bf16)
        grad_carried = dot(grad_o, outward[...])
        extended[:STEP, :] = grad_carried * gate_c[...].astype(f32)
        grad_c = (grad_carried * conv[...].astype(f32)).astype(bf16)
        left_gate, right_gate = gate_b[...].astype(f32), value_part[...].astype(f32)
        product = left_gate * right_gate
        grad_product = jnp.zeros((STEP, width), f32)
        for lag in range(KCONV):
            slot, start = slots(place, tile * STEP + lag, STEP)
            keep = (slot - lag >= start).astype(f32)
            masked = keep * extended[lag : lag + STEP, :]
            grad_product = grad_product + taps[lag : lag + 1, :] * masked
            sums[2 + lag : 3 + lag, :] += jnp.sum(masked * product, axis=0, keepdims=True)
        grad_b = (grad_product * right_gate).astype(bf16)
        grad_v = (grad_product * left_gate).astype(bf16)
        for s in range(BLOCKS):
            lanes = slice(s * n, (s + 1) * n)
            at = s * 3 * n
            grads[:, at : at + n] = grad_b[:, lanes]
            grads[:, at + n : at + 2 * n] = grad_c[:, lanes]
            grads[:, at + 2 * n : at + 3 * n] = grad_v[:, lanes]
        grad_first = dot_nt(grads[...], inward[...])
        left, right = mine[...].astype(f32), other[...].astype(f32)
        rstd = inverse_rms(left, right)
        scaled = grad_first * gain_one[...]
        mean = (
            jnp.sum(scaled[:, :half] * left, axis=1, keepdims=True)
            + jnp.sum(scaled[:, half:] * right, axis=1, keepdims=True)
        ) / width
        for i, (value, target) in enumerate(((left, grad_own), (right, grad_other))):
            lanes = slice(i * half, (i + 1) * half)
            sums[0:1, lanes] += jnp.sum(grad_first[:, lanes] * value * rstd, axis=0, keepdims=True)
            target[...] = (
                grad[:, lanes] + (rstd * scaled[:, lanes] - value * (rstd * rstd * rstd) * mean)
            ).astype(bf16)

    def tile_of(m):
        return tiles - 1 - m

    rows = pl.BlockSpec((STEP, width), lambda m, place: (tile_of(m), 0))
    one = pl.BlockSpec((1, width), lambda m, place: (0, 0))
    eight = pl.BlockSpec((8, width), lambda m, place: (0, 0))
    narrow = pl.BlockSpec((STEP, half), lambda m, place: (tile_of(m), 0))
    return call(
        body,
        "mix_backward",
        (
            shape_of(count, half),
            shape_of(count, half),
            shape_of(count, 3 * width),
            shape_of(width, count),
            shape_of(8, width, dtype=f32),
        ),
        flops=8 * count * width * width,
        moved=44 * count * width,
        tie=tie,
        n_in=16,
        grid_spec=scalar_grid(
            (tiles,),
            [
                rows,
                rows,
                rows,
                pl.BlockSpec(
                    (STEP, half), lambda m, place: (place[1] * tiles + tile_of(m), 0)
                ),
                narrow,
                rows,
                rows,
                rows,
                rows,
                eight,
                pl.BlockSpec((KCONV, width), lambda m, place: (0, 0)),
                one,
                one,
            ]
            + [HERE] * 2,
            [
                narrow,
                narrow,
                pl.BlockSpec((STEP, 3 * width), lambda m, place: (tile_of(m), 0)),
                pl.BlockSpec((width, STEP), lambda m, place: (0, tile_of(m))),
                eight,
            ],
            [
                pltpu.VMEM((width, 3 * width), bf16),
                pltpu.VMEM((width, width), bf16),
                pltpu.VMEM((STEP + 8, width), f32),
                pltpu.SemaphoreType.DMA((4 * BLOCKS,)),
            ],
        ),
    )(
        place,
        hidden,
        grad_normed,
        low,
        tokens,
        theirs,
        *saved,
        later,
        taps,
        gain_one,
        gain_two,
        *halves,
        *tie,
    )


def mix_weights(place, normed_t, grad_t, grads, carried, received, tie):
    width, count = normed_t.shape
    half = width // 2
    n = width // BLOCKS
    side = 1 if received is None else 0

    def body(place, normed_t, grad_t, grads, carried, *refs):
        inward = dot(normed_t[...], grads[...])
        outward = dot(grad_t[...], carried[...])
        if received is None:
            out = refs[0]
            out[:, : 3 * n] = inward.astype(bf16)
            out[:, 3 * n :] = outward.astype(bf16)
        else:
            received_part, keep, send, total = refs
            total[:, : 3 * n] = inward + received_part[:, : 3 * n].astype(f32)
            total[:, 3 * n :] = outward + received_part[:, 3 * n :].astype(f32)
            keep_and_send(place, total, keep, send)

    left = pl.BlockSpec((half, count), lambda s, place: (side, 0))
    part = pl.BlockSpec((half, 4 * n), lambda s, place: (0, s))
    small = pl.BlockSpec((half // 2, 4 * n), lambda s, place: (0, s))
    more = [] if received is None else [received]
    return call(
        body,
        "mix_weights",
        (shape_of(half // 2, 4 * width),) * 2 if more else shape_of(half, 4 * width),
        flops=8 * count * half * width,
        moved=2 * (2 * half * count + (count + half) * 4 * width),
        tie=tie,
        n_in=5 + len(more),
        grid_spec=scalar_grid(
            (BLOCKS,),
            [
                left,
                left,
                pl.BlockSpec((count, 3 * n), lambda s, place: (0, s)),
                pl.BlockSpec((count, n), lambda s, place: (0, s)),
            ]
            + [part] * len(more),
            [small, small] if more else part,
            [pltpu.VMEM((half, 4 * n), f32)] if more else [],
        ),
    )(place, normed_t, grad_t, grads, carried, *more, *tie)


def after(value, *earlier):
    return lax.optimization_barrier((value, *earlier))[0]


def swap_cores(value):
    return lax.ppermute(value, "col", [(0, 1), (1, 0)])


def across_first(value):
    return lax.ppermute(
        value, ("dp", "col"), [(2 * p + c, 2 * (p ^ (1 << c)) + c) for p in range(4) for c in range(2)]
    )


def across_second(value):
    return lax.ppermute(
        value, ("dp", "col"), [(2 * p + c, 2 * (p ^ (2 >> c)) + c) for p in range(4) for c in range(2)]
    )


def along_row(value, steps):
    return lax.ppermute(value, "row", [(i, (i + steps) % BLOCKS) for i in range(BLOCKS)])


def quarters(part):
    across = across_first(part)
    return (part, across, across_second(part), across_second(across))


def add(*parts):
    return sum(part.astype(f32) for part in parts).astype(bf16)


def upper(value):
    return value[: value.shape[0] // 2]


def lower(value):
    return value[value.shape[0] // 2 :]


def block_of(value, b, axis=0):
    width = value.shape[axis] // BLOCKS
    return lax.dynamic_slice_in_dim(value, b * width, width, axis)


def later_rows(value):
    pairs = [(i, i - 1) for i in range(1, 2 * BLOCKS)]
    value = lax.ppermute(value, ("row", "col"), pairs)
    parts = jnp.split(value, BLOCKS, axis=1)
    order = [OFFSETS.index(offset % BLOCKS - 1) for offset in OFFSETS]
    moved = jnp.concatenate([parts[i] for i in order], axis=1)
    return jnp.where(lax.axis_index("col") == 1, moved, value)


def shards(
    tokens,
    cotangent,
    seq_lens,
    norm1_gain,
    in_weight,
    conv_weight,
    out_weight,
    norm2_gain,
    gate_up_weight,
    down_weight,
):
    dp, row, core = lax.axis_index("dp"), lax.axis_index("row"), lax.axis_index("col")
    count, half = tokens.shape[0] // 2, tokens.shape[1]
    position = ((dp * BLOCKS + row) * 2 + core) * count
    lengths = lax.dynamic_slice_in_dim(seq_lens, position // ROW_LEN, 1, 0)[0]
    place = jnp.stack(
        [dp, core, position % ROW_LEN, lengths[0], lengths[0] + lengths[1]]
    ).astype(jnp.int32)

    def of_the_other(value):
        return lax.dynamic_slice_in_dim(value, (1 - core) * count, count, 0)

    mix_first = pack(in_weight, out_weight, place, 1, conv_weight)
    mix_quarters = [along_row(mix_first, -offset) for offset in OFFSETS[1:]]
    own_gains = jnp.pad(jnp.stack([norm1_gain, norm2_gain]), ((0, HALO - 2), (0, 0)))
    mix_own = pack(in_weight, out_weight, place, 4, tie=[mix_first])
    feed_own = pack(gate_up_weight, down_weight, place, 4, tie=[mix_own])
    before = lax.ppermute(
        after(tokens[2 * count - HALO :], mix_own), "row", [(i, i + 1) for i in range(BLOCKS - 1)]
    )
    joined = join_rows(mix_quarters, [mix_own, feed_own])
    theirs = swap_cores(outgoing(place, tokens, cotangent, before, own_gains, [joined]))
    feed_first = pack(gate_up_weight, down_weight, place, 1, tie=[joined])
    gains = jnp.concatenate([own_gains[:2], theirs[2 * count + HALO :][:2]], axis=1).astype(f32)
    gain_one, gain_two = gains[:1], gains[1:]
    normed, normed_t, low, low_t = prepare(
        place, tokens, theirs, before, cotangent, gain_one, [joined]
    )
    width = half // 4
    taps = jnp.concatenate(
        [conv_weight] + [part[width : width + KCONV, : conv_weight.shape[1]] for part in mix_quarters],
        axis=1,
    ).astype(f32)
    quarter_one = along_row(feed_first, -OFFSETS[1])
    mix_half = mix_assemble(mix_own, quarters(joined), place, [normed, quarter_one])
    mix_halves = [mix_half, swap_cores(mix_half)]
    half_one = lax.all_gather(after(quarter_one, mix_half), "dp", axis=0, tiled=True)

    *saved, hidden, carried, normed_two, normed_two_t = mix_forward(
        place, normed, mix_halves, tokens, theirs, taps, gain_two, []
    )
    feed_halves, others = [feed_own], [swap_cores(feed_own)]
    activations, from_them = [], []

    def gathered(k, last, here):
        part = along_row(after(feed_first, last), -OFFSETS[k])
        return lax.all_gather(after(part, here), "dp", axis=0, tiled=True)

    def have(half):
        feed_halves.append(half)
        others.append(swap_cores(half))

    def activate(grad, tie):
        k = len(activations)
        grad, acts, for_them = feed(
            normed_two, low, normed_two_t, low_t, feed_halves[k], others[k], grad, tie
        )
        activations.append(acts)
        from_them.append(swap_cores(for_them))
        return grad, for_them

    def weights_of(k, tie):
        keep, send = feed_weights(place, normed_two_t, low_t, activations[k], from_them[k], tie)
        return keep, across_second(send)

    grad_normed_two, done = activate(None, [])
    half_two = gathered(2, mix_half, done)
    have(after(half_one, done))
    grad_normed_two, last = activate(grad_normed_two, [])
    half_three = gathered(3, done, last)
    done = last
    keep, send = weights_of(0, [done])
    have(after(half_two, keep))
    grad_normed_two, done = activate(grad_normed_two, [keep])
    zero = (keep, send)
    keep, send = weights_of(1, [done, send])
    one = (keep, send)
    keep, send = weights_of(2, [keep])
    two = (keep, send)
    have(after(half_three, one[0]))
    grad_normed_two, done = activate(grad_normed_two, [keep])
    one_low, two_low = add(*map(lower, one)), add(*map(lower, two))
    one_across, two_across = across_first(one_low), across_first(two_low)
    first = first_rows(hidden, grad_normed_two, low, saved[1], gain_two, mix_halves)
    later = later_rows(first)
    keep, send = weights_of(3, [first, one_low, two_low])
    one = add(*map(upper, one), one_across)
    two = add(*map(upper, two), two_across)
    zero_across = across_first(after(add(*map(lower, zero)), keep))

    grad_own, grad_other, grads, grad_t, sums = mix_backward(
        place,
        hidden,
        grad_normed_two,
        low,
        tokens,
        theirs,
        saved,
        later,
        taps,
        gain_one,
        gain_two,
        mix_halves,
        [keep, one, two],
    )
    three = (keep, send)
    three_low = add(*map(lower, three))
    one, two = along_row(one, OFFSETS[1]), along_row(two, OFFSETS[2])
    where = jnp.array([OFFSETS.index(offset) for offset in (0, 1, 2, -1)], jnp.int32)
    own_taps = jnp.concatenate(
        [block_of(sums[2:], where[(b - row) % BLOCKS], 1) for b in range(BLOCKS)], axis=1
    )
    packed_sums = jnp.concatenate([sums[:2], own_taps], axis=0)
    every = lax.all_gather(packed_sums, ("dp", "row", "col"), axis=0)

    for_them = mix_weights(place, normed_t, grad_t, grads, carried, None, [one, three_low, packed_sums])
    received = swap_cores(for_them)
    three = add(*map(upper, three), across_first(three_low))
    grad_theirs = swap_cores(grad_other)
    input_back = join_tokens(grad_own, after(grad_theirs, for_them), place)
    keep, send = mix_weights(
        place, normed_t, grad_t, grads, carried, received, [three, two, input_back]
    )
    send = across_second(send)
    three = along_row(three, OFFSETS[3])
    own_out, other_out = feed_output(hidden, activations, feed_halves, others, [keep])
    send = after(send, own_out)
    other_out = swap_cores(other_out)
    mix_low = add(lower(keep), lower(send))
    mix_across = across_first(mix_low)
    three = after(three, mix_low)
    feed_sum = quarters(add(*map(upper, zero), zero_across, one, two, three))
    mix_quarters = jnp.split(add(upper(keep), upper(send), mix_across), BLOCKS, axis=1)
    mix_quarters = [along_row(part, OFFSETS[k]) if k else part for k, part in enumerate(mix_quarters)]
    mix_sum = quarters(add(*mix_quarters))
    output_back = join_tokens(own_out, other_out, place)
    gate_up_grad, down_grad = unpack(feed_sum, 2, place)
    in_grad, out_grad = unpack(mix_sum, 3, place)
    every = after(every, gate_up_grad)
    sums = jnp.sum(every.reshape(16, 2, *packed_sums.shape), axis=0)
    mine, other = sums[core], sums[1 - core]
    gain_grads = mine[:2, :half] + other[:2, half:]
    taps_grad = block_of(mine[2 : 2 + KCONV] + other[2 : 2 + KCONV], row, 1)
    return (
        output_back,
        input_back,
        gain_grads[0],
        in_grad,
        taps_grad,
        out_grad,
        gain_grads[1],
        gate_up_grad,
        down_grad,
    )


def from_behind(value, axis, steps):
    count = lax.axis_size(axis)
    leading, last = (max(0, -steps), min(count, count - steps))
    return lax.ppermute(value, axis, [(source, source + steps) for source in range(leading, last)])


def token_index(count, extra):
    flat_rank = (
        lax.axis_index("dp") * lax.axis_size("row") + lax.axis_index("row")
    ) * lax.axis_size("col") + lax.axis_index("col")
    return flat_rank * count + jnp.arange(count + extra, dtype=jnp.int32)


def flat_slot_masks(seq_lens, count, extra):
    position = token_index(count, extra)
    packed = position // ROW_LEN
    place = position - packed * ROW_LEN
    table = (packed[:, None] == jnp.arange(seq_lens.shape[0], dtype=jnp.int32)[None, :]).astype(
        jnp.int32
    )
    first = jnp.sum(table * seq_lens[None, :, 0], axis=1)
    second = jnp.sum(table * seq_lens[None, :, 1], axis=1)
    start = jnp.where(place < first, 0, first)
    valid_slot = (place < first + second).astype(jnp.float32)
    keep_masks = jnp.stack([(place - lag >= start).astype(jnp.float32) for lag in range(KCONV)])
    return (valid_slot[:count], keep_masks)


def collect(
    norm1_gain, in_weight, conv_weight, out_weight, norm2_gain, gate_up_weight, down_weight
):
    in_rows, conv_full, out_rows, gate_rows, down_rows = (
        lax.all_gather(in_weight, "row", axis=2, tiled=True),
        lax.all_gather(conv_weight, "row", axis=1, tiled=True),
        lax.all_gather(out_weight, "row", axis=0, tiled=True),
        lax.all_gather(gate_up_weight, "row", axis=2, tiled=True),
        lax.all_gather(down_weight, "row", axis=0, tiled=True),
    )
    gain_first, in_full, out_full, gain_second, gate_full, down_full = (
        lax.all_gather(norm1_gain, "col", axis=0, tiled=True),
        lax.all_gather(in_rows, "col", axis=1, tiled=True),
        lax.all_gather(out_rows, "col", axis=1, tiled=True),
        lax.all_gather(norm2_gain, "col", axis=0, tiled=True),
        lax.all_gather(gate_rows, "col", axis=1, tiled=True),
        lax.all_gather(down_rows, "col", axis=1, tiled=True),
    )
    return (gain_first, in_full, conv_full, out_full, gain_second, gate_full, down_full)


def flat_norm_backward(values, rstd, gain, grad_normed):
    scaled = grad_normed * gain
    gain_grad = jnp.sum(grad_normed * values * rstd, axis=0)
    grad_values = rstd * scaled - values * (rstd * rstd * rstd) * jnp.mean(
        scaled * values, axis=1, keepdims=True
    )
    return (grad_values, gain_grad)


def project(left, right):
    return jnp.dot(left, right, preferred_element_type=jnp.float32)


def weight_grad(left, right):
    return jnp.einsum("td,te->de", left, right, preferred_element_type=jnp.float32)


def back_project(grad, matrix):
    return jnp.einsum("te,de->td", grad, matrix, preferred_element_type=jnp.float32)


def flat_shards(
    tokens,
    cotangent,
    seq_lens,
    norm1_gain,
    in_weight,
    conv_weight,
    out_weight,
    norm2_gain,
    gate_up_weight,
    down_weight,
):
    own_tokens, own_cotangent = (
        lax.all_to_all(tokens, "col", split_axis=0, concat_axis=1, tiled=True),
        lax.all_to_all(cotangent, "col", split_axis=0, concat_axis=1, tiled=True),
    )
    gain_first, in_full, conv_full, out_full, gain_second, gate_full, down_full = collect(
        norm1_gain, in_weight, conv_weight, out_weight, norm2_gain, gate_up_weight, down_weight
    )
    count, width = own_tokens.shape
    reach = KCONV - 1
    valid_slot, keep_masks = flat_slot_masks(seq_lens, count, reach)
    conv_taps = conv_full.astype(jnp.float32)
    gain_one_f = gain_first.astype(jnp.float32)
    gain_two_f = gain_second.astype(jnp.float32)
    inputs = own_tokens.astype(jnp.float32)
    rstd_first = lax.rsqrt(jnp.mean(inputs * inputs, axis=1, keepdims=True) + eps)
    normed = (inputs * rstd_first * gain_one_f).astype(jnp.bfloat16)
    gate_b = project(normed, in_full[0])
    gate_c = project(normed, in_full[1])
    value_part = project(normed, in_full[2])
    product = gate_b * value_part
    earlier = from_behind(product[count - reach :], ("row", "col"), 1)
    extended = jnp.concatenate([earlier, product], axis=0)
    conv = jnp.zeros((count, width), jnp.float32)
    for lag in range(KCONV):
        conv = (
            conv
            + conv_taps[lag]
            * keep_masks[lag, :count, None]
            * extended[reach - lag : reach - lag + count]
        )
    carried = (gate_c * conv).astype(jnp.bfloat16)
    hidden = inputs + project(carried, out_full)
    rstd_second = lax.rsqrt(jnp.mean(hidden * hidden, axis=1, keepdims=True) + eps)
    normed_two = (hidden * rstd_second * gain_two_f).astype(jnp.bfloat16)
    gate = project(normed_two, gate_full[0])
    up_part = project(normed_two, gate_full[1])
    sigmoid_gate = jax.nn.sigmoid(gate)
    silu_gate = gate * sigmoid_gate
    active = (silu_gate * up_part).astype(jnp.bfloat16)
    output = hidden + project(active, down_full)
    grad_out = own_cotangent.astype(jnp.float32) * valid_slot[:, None]
    grad_low = grad_out.astype(jnp.bfloat16)
    down_grad = weight_grad(active, grad_low)
    grad_active = back_project(grad_low, down_full)
    grad_gate = (grad_active * up_part * sigmoid_gate * (1.0 + gate * (1.0 - sigmoid_gate))).astype(
        jnp.bfloat16
    )
    grad_up = (grad_active * silu_gate).astype(jnp.bfloat16)
    gate_grad = jnp.stack([weight_grad(normed_two, grad_gate), weight_grad(normed_two, grad_up)])
    grad_normed_two = back_project(grad_gate, gate_full[0]) + back_project(grad_up, gate_full[1])
    grad_second, gain_second_part = flat_norm_backward(hidden, rstd_second, gain_two_f, grad_normed_two)
    grad_hidden = grad_out + grad_second
    grad_o = grad_hidden.astype(jnp.bfloat16)
    out_grad = weight_grad(carried, grad_o)
    grad_carried = back_project(grad_o, out_full)
    grad_gate_c = (grad_carried * conv).astype(jnp.bfloat16)
    grad_conv = grad_carried * gate_c
    later = from_behind(grad_conv[:reach], ("row", "col"), -1)
    grad_extended = jnp.concatenate([grad_conv, later], axis=0)
    grad_product = jnp.zeros((count, width), jnp.float32)
    conv_rows = []
    for lag in range(KCONV):
        masked = keep_masks[lag, :, None] * grad_extended
        grad_product = grad_product + conv_taps[lag] * masked[lag : lag + count]
        conv_rows.append(
            jnp.sum(masked[:count] * extended[reach - lag : reach - lag + count], axis=0)
        )
    conv_grad = jnp.stack(conv_rows)
    grad_gate_b = (grad_product * value_part).astype(jnp.bfloat16)
    grad_value = (grad_product * gate_b).astype(jnp.bfloat16)
    in_grad = jnp.stack(
        [
            weight_grad(normed, grad_gate_b),
            weight_grad(normed, grad_gate_c),
            weight_grad(normed, grad_value),
        ]
    )
    grad_normed = (
        back_project(grad_gate_b, in_full[0])
        + back_project(grad_gate_c, in_full[1])
        + back_project(grad_value, in_full[2])
    )
    grad_first, gain_first_part = flat_norm_backward(inputs, rstd_first, gain_one_f, grad_normed)
    input_grad = (grad_hidden + grad_first).astype(jnp.bfloat16)
    output_back, input_back = (
        lax.all_to_all(output.astype(jnp.bfloat16), "col", split_axis=1, concat_axis=0, tiled=True),
        lax.all_to_all(input_grad, "col", split_axis=1, concat_axis=0, tiled=True),
    )
    in_cols, out_cols, gate_cols, down_cols = (
        lax.psum_scatter(in_grad, "col", scatter_dimension=1, tiled=True),
        lax.psum_scatter(out_grad, "col", scatter_dimension=1, tiled=True),
        lax.psum_scatter(gate_grad, "col", scatter_dimension=1, tiled=True),
        lax.psum_scatter(down_grad, "col", scatter_dimension=1, tiled=True),
    )
    in_part, out_part, gate_part, down_part = (
        lax.psum_scatter(in_cols, "row", scatter_dimension=2, tiled=True),
        lax.psum_scatter(out_cols, "row", scatter_dimension=0, tiled=True),
        lax.psum_scatter(gate_cols, "row", scatter_dimension=2, tiled=True),
        lax.psum_scatter(down_cols, "row", scatter_dimension=0, tiled=True),
    )
    in_sum, out_sum, gate_sum, down_sum = lax.psum((in_part, out_part, gate_part, down_part), "dp")
    gain_one_sum, gain_two_sum, conv_sum = lax.psum(
        (gain_first_part, gain_second_part, conv_grad), ("dp", "row", "col")
    )
    col_width = width // lax.axis_size("col")
    row_width = width // lax.axis_size("row")
    gain_first_grad = lax.dynamic_slice_in_dim(
        gain_one_sum, lax.axis_index("col") * col_width, col_width
    )
    gain_second_grad = lax.dynamic_slice_in_dim(
        gain_two_sum, lax.axis_index("col") * col_width, col_width
    )
    conv_weight_grad = lax.dynamic_slice_in_dim(
        conv_sum, lax.axis_index("row") * row_width, row_width, axis=1
    )
    return (
        output_back,
        input_back,
        gain_first_grad,
        in_sum,
        conv_weight_grad,
        out_sum,
        gain_second_grad,
        gate_sum,
        down_sum,
    )


def solution(mesh):
    ring = mesh.shape["dp"] == 4 and mesh.shape["row"] == BLOCKS and mesh.shape["col"] == 2
    return jax.shard_map(
        shards if ring else flat_shards,
        mesh=mesh,
        in_specs=(
            P(("dp", "row"), "col"),
            P(("dp", "row"), "col"),
            P(),
            P("col"),
            P(None, "col", "row"),
            P(None, "row"),
            P("row", "col"),
            P("col"),
            P(None, "col", "row"),
            P("row", "col"),
        ),
        out_specs=(
            P(("dp", "row"), "col"),
            P(("dp", "row"), "col"),
            P("col"),
            P(None, "col", "row"),
            P(None, "row"),
            P("row", "col"),
            P("col"),
            P(None, "col", "row"),
            P("row", "col"),
        ),
        check_vma=False,
    )
```

```python
import functools

import jax
import jax.numpy as jnp
from jax import lax
from jax.experimental import pallas as pl
from jax.experimental.pallas import tpu as pltpu
from jax.sharding import PartitionSpec as P

KCONV = 3
ROW_LEN = 8192
BLOCKS = 4
OFFSETS = (0, -1, 1, 2)
HALO = 16
STEP = 256


eps = 1e-05
bf16 = jnp.bfloat16
f32 = jnp.float32
VMEM_LIMIT = 64000 * 1024
HERE = pl.BlockSpec(memory_space=pl.ANY)
SCALARS = pl.BlockSpec(memory_space=pltpu.SMEM)


def dot(left, right):
    return jnp.dot(left, right, preferred_element_type=f32)


def dot_nt(left, right):
    return lax.dot_general(left, right, (((1,), (1,)), ((), ())), preferred_element_type=f32)


def shape_of(*dims, dtype=bf16):
    return jax.ShapeDtypeStruct(dims, dtype)


def call(body, name, out_shape, flops=0, moved=0, tie=(), n_in=None, **kwargs):
    if tie:
        inner, at = body, n_in

        def body(*refs):
            inner(*refs[:at], *refs[at + len(tie) :])

        if "grid_spec" in kwargs:
            spec = kwargs["grid_spec"]
            kwargs["grid_spec"] = pltpu.PrefetchScalarGridSpec(
                num_scalar_prefetch=1,
                grid=spec.grid,
                in_specs=list(spec.in_specs) + [HERE] * len(tie),
                out_specs=spec.out_specs,
                scratch_shapes=spec.scratch_shapes,
            )
        else:
            kwargs["in_specs"] = list(kwargs["in_specs"]) + [HERE] * len(tie)
    return pl.pallas_call(
        body,
        out_shape=out_shape,
        name=name,
        compiler_params=pltpu.CompilerParams(vmem_limit_bytes=VMEM_LIMIT),
        cost_estimate=pl.CostEstimate(flops=flops, bytes_accessed=moved, transcendentals=0),
        **kwargs,
    )


def scalar_grid(grid, in_specs, out_specs, scratch_shapes=()):
    return pltpu.PrefetchScalarGridSpec(
        num_scalar_prefetch=1,
        grid=grid,
        in_specs=in_specs,
        out_specs=out_specs,
        scratch_shapes=scratch_shapes,
    )


def quarter_of(place, j):
    dp, core = place[0], place[1]
    low, high = j % 2, j // 2
    mask = jnp.where(core == 0, 2 * high + low, 2 * low + high)
    return jnp.bitwise_xor(dp, mask)


def join_tokens(mine, theirs, place):
    count, half = mine.shape

    def body(place, mine, theirs, out):
        own = pl.program_id(0) == place[1]

        @pl.when(own)
        def _():
            out[...] = mine[...]

        @pl.when(jnp.logical_not(own))
        def _():
            out[...] = theirs[...]

    kept = pl.BlockSpec((count, half), lambda h, place: (0, 0))
    return call(
        body,
        "join_tokens",
        shape_of(2 * count, half),
        grid_spec=scalar_grid(
            (2,), [kept, kept], pl.BlockSpec((count, half), lambda h, place: (h, 0))
        ),
    )(place, mine, theirs)


def outgoing(place, tokens, cotangent, before, gains, tie):
    count, half = tokens.shape[0] // 2, tokens.shape[1]
    rows = 2 * count + 2 * HALO

    def body(place, tokens, cotangent, between, before, gains, out):
        out[:count] = tokens[...]
        out[count : 2 * count] = cotangent[...]

        @pl.when(place[1] == 0)
        def _():
            out[2 * count : 2 * count + HALO] = between[...]

        @pl.when(place[1] == 1)
        def _():
            out[2 * count : 2 * count + HALO] = before[...]

        out[2 * count + HALO :] = gains[...]

    theirs = pl.BlockSpec((count, half), lambda i, place: (1 - place[1], 0))
    few = pl.BlockSpec((HALO, half), lambda i, place: (0, 0))
    return call(
        body,
        "outgoing",
        shape_of(rows, half),
        tie=tie,
        n_in=6,
        grid_spec=scalar_grid(
            (1,),
            [theirs, theirs, pl.BlockSpec((HALO, half), lambda i, place: (count // HALO - 1, 0)), few, few],
            pl.BlockSpec((rows, half), lambda i, place: (0, 0)),
        ),
    )(place, tokens, cotangent, tokens, before, gains, *tie)


def pack(stack, turned, place, quarters, rows=None, tie=()):
    k, half, n = stack.shape
    width = half // 4
    lanes = (k + 1) * n
    below = [] if rows is None else [rows]

    def body(place, stack, turned, *refs):
        out = refs[-1]
        for i in range(k):
            out[:width, i * n : (i + 1) * n] = stack[i]
        out[:width, k * n :] = turned[...].astype(f32).T.astype(out.dtype)
        if below:
            out[width:, :] = jnp.zeros((HALO, lanes), out.dtype)
            out[width : width + KCONV, :n] = refs[0][...]

    def source(j, place):
        return place[0] if quarters == 1 else j

    return call(
        body,
        "pack",
        shape_of(quarters * width + HALO * len(below), lanes),
        tie=tie,
        n_in=3 + len(below),
        grid_spec=scalar_grid(
            (quarters,),
            [
                pl.BlockSpec((k, width, n), lambda j, place: (0, source(j, place), 0)),
                pl.BlockSpec((n, width), lambda j, place: (0, source(j, place))),
            ]
            + [pl.BlockSpec((KCONV, n), lambda j, place: (0, 0))] * len(below),
            pl.BlockSpec((width + HALO * len(below), lanes), lambda j, place: (j, 0)),
        ),
    )(place, stack, turned, *below, *tie)


def join_rows(parts, tie):
    rows, lanes = parts[0].shape

    def body(*refs):
        for i in range(len(parts)):
            refs[-1][i * rows : (i + 1) * rows] = refs[i][...]

    whole = pl.BlockSpec(memory_space=pltpu.VMEM)
    return call(
        body,
        "join_rows",
        shape_of(len(parts) * rows, lanes),
        tie=tie,
        n_in=len(parts),
        in_specs=[whole] * len(parts),
        out_specs=whole,
    )(*parts, *tie)


def mix_assemble(own, pieces, place, tie):
    half, lanes = own.shape
    width = half // 4
    stride = width + HALO

    def body(place, own, *refs):
        out = refs[-1]
        out[0] = own[...]
        for s in range(1, BLOCKS):
            for j in range(4):
                rows = pl.ds(pl.multiple_of(quarter_of(place, j) * width, width), width)
                out[s, rows, :] = refs[j][(s - 1) * stride : (s - 1) * stride + width, :]

    whole = pl.BlockSpec(memory_space=pltpu.VMEM)
    return call(
        body,
        "mix_assemble",
        shape_of(BLOCKS, half, lanes),
        tie=tie,
        n_in=6,
        in_specs=[SCALARS] + [whole] * 5,
        out_specs=whole,
    )(place, own, *pieces, *tie)


def unpack(pieces, k, place):
    width, lanes = pieces[0].shape
    half, n = 4 * width, lanes // (k + 1)

    def body(place, *refs):
        stack, turned = refs[4:]
        for j in range(4):

            @pl.when(pl.program_id(0) == j)
            def _(piece=refs[j]):
                for i in range(k):
                    stack[i] = piece[:, i * n : (i + 1) * n].astype(f32)
                turned[...] = piece[:, k * n :].astype(f32).T

    whole = pl.BlockSpec((width, lanes), lambda j, place: (0, 0))
    return call(
        body,
        "unpack",
        (shape_of(k, half, n, dtype=f32), shape_of(n, half, dtype=f32)),
        grid_spec=scalar_grid(
            (4,),
            [whole] * 4,
            [
                pl.BlockSpec((k, width, n), lambda j, place: (0, quarter_of(place, j), 0)),
                pl.BlockSpec((n, width), lambda j, place: (0, quarter_of(place, j))),
            ],
        ),
    )(place, *pieces)


def rows_of(i, step=STEP):
    return pl.ds(pl.multiple_of(i * step, step), step)


def slots(place, start, count):
    slot = place[2] + start + lax.broadcasted_iota(jnp.int32, (count, 1), 0)
    return slot, jnp.where(slot < place[3], 0, place[3])


def inverse_rms(*parts):
    width = sum(part.shape[1] for part in parts)
    total = sum(jnp.sum(part * part, axis=1, keepdims=True) for part in parts)
    return lax.rsqrt(total / width + eps)


def prepare(place, tokens, theirs, before, cotangent, gain, tie):
    count, half = tokens.shape[0] // 2, tokens.shape[1]
    width = 2 * half

    def body(
        place, own, other, before, between, halo_other, cot, cot_other, gain, normed, normed_t, low, low_t
    ):
        def norm(left, right):
            left, right = left.astype(f32), right.astype(f32)
            rstd = inverse_rms(left, right)
            return (
                (left * rstd * gain[:, :half]).astype(bf16),
                (right * rstd * gain[:, half:]).astype(bf16),
            )

        halo = jnp.where(place[1] == 0, before[...].astype(f32), between[...].astype(f32))

        @pl.when(pl.program_id(0) == 0)
        def _():
            left, right = norm(halo, halo_other[...])
            normed[:HALO, :half] = left
            normed[:HALO, half:] = right

        tile = pl.program_id(0)
        here = pl.ds(pl.multiple_of(HALO + tile * STEP, HALO), STEP)
        for i, value in enumerate(norm(own[...], other[...])):
            lanes = slice(i * half, (i + 1) * half)
            normed[here, lanes] = value
            normed_t[lanes, :] = value.astype(f32).T.astype(bf16)
        slot, _ = slots(place, tile * STEP, STEP)
        valid = (slot < place[4]).astype(f32)
        for i, value in enumerate((cot[...], cot_other[...])):
            lanes = slice(i * half, (i + 1) * half)
            value = value.astype(f32) * valid
            low[:, lanes] = value.astype(bf16)
            low_t[lanes, :] = value.T.astype(bf16)

    tiles = count // STEP
    mine = pl.BlockSpec((STEP, half), lambda m, place: (place[1] * tiles + m, 0))

    def received(first):
        return pl.BlockSpec((STEP, half), lambda m, place: (first + m, 0))

    def few(block):
        return pl.BlockSpec((HALO, half), lambda m, place: (block, 0))

    turned = pl.BlockSpec((width, STEP), lambda m, place: (0, m))
    return call(
        body,
        "prepare",
        (
            shape_of(HALO + count, width),
            shape_of(width, count),
            shape_of(count, width),
            shape_of(width, count),
        ),
        moved=16 * count * width,
        tie=tie,
        n_in=9,
        grid_spec=scalar_grid(
            (tiles,),
            [
                mine,
                received(0),
                few(0),
                few(count // HALO - 1),
                few(2 * count // HALO),
                mine,
                received(tiles),
                pl.BlockSpec((1, width), lambda m, place: (0, 0)),
            ],
            [
                pl.BlockSpec((HALO + count, width), lambda m, place: (0, 0)),
                turned,
                pl.BlockSpec((STEP, width), lambda m, place: (m, 0)),
                turned,
            ],
        ),
    )(place, tokens, theirs, before, tokens, theirs, cotangent, theirs, gain, *tie)


def mix_copies(sources, inward, outward, sems):
    copies = []
    for s in range(BLOCKS):
        for side in range(2):
            source = sources[side].at[s]
            half, lanes = source.shape
            n = lanes // 4
            rows = pl.ds(side * half, half)
            at = 4 * s + 2 * side
            copies.append(
                pltpu.make_async_copy(
                    source.at[:, pl.ds(0, 3 * n)],
                    inward.at[rows, pl.ds(s * 3 * n, 3 * n)],
                    sems.at[at],
                )
            )
            copies.append(
                pltpu.make_async_copy(
                    source.at[:, pl.ds(3 * n, n)],
                    outward.at[rows, pl.ds(s * n, n)],
                    sems.at[at + 1],
                )
            )
    return copies


def mix_forward(place, normed, halves, tokens, theirs, taps, gain, tie):
    count, half = tokens.shape[0] // 2, tokens.shape[1]
    width = 2 * half
    n = width // BLOCKS
    part = (HALO + count) // 5
    kept = 4

    def body(place, *refs):
        normed_hbm, sources, refs = refs[0], refs[1:3], refs[3:]
        tokens_hbm, theirs_hbm, taps, gain = refs[:4]
        results, hidden_hbm, carried_hbm, normed2_hbm, turned_hbm = (
            refs[4:8],
            refs[8],
            refs[9],
            refs[10],
            refs[11],
        )
        normed, inward, outward, mine, other, mixed, product, carried, hidden, normed2, turned = refs[
            12:23
        ]
        saved = refs[23:27]
        in_sems, weight_sems, saved_sems, out_sems = refs[27:]
        loads = [
            pltpu.make_async_copy(normed_hbm, normed, in_sems.at[0]),
            pltpu.make_async_copy(
                tokens_hbm.at[pl.ds(pl.multiple_of(place[1] * count, count), count)],
                mine,
                in_sems.at[1],
            ),
            pltpu.make_async_copy(theirs_hbm.at[pl.ds(0, count)], other, in_sems.at[2]),
        ]
        weights = mix_copies(sources, inward, outward, weight_sems)
        loads[0].start()
        for copy in weights:
            copy.start()
        loads[1].start()
        loads[2].start()
        loads[0].wait()
        pending = []
        for s in range(BLOCKS):
            for copy in weights[4 * s : 4 * s + 4]:
                copy.wait()

            def project(i, carry, s=s):
                rows = rows_of(i, part)
                value = dot(normed[rows, :], inward[:, s * 3 * n : (s + 1) * 3 * n])
                mixed[rows, :] = value
                product[rows, :] = value[:, :n] * value[:, 2 * n :]
                return carry

            lax.fori_loop(0, 5, project, 0)
            lanes = slice(s * n, (s + 1) * n)
            for m in range(count // STEP):
                first = HALO + m * STEP
                rows = slice(m * STEP, (m + 1) * STEP)
                slot, start = slots(place, m * STEP, STEP)
                conv = jnp.zeros((STEP, n), f32)
                for lag in range(KCONV):
                    keep = (slot - lag >= start).astype(f32)
                    conv = conv + taps[lag : lag + 1, lanes] * (
                        keep * product[first - lag : first - lag + STEP, :]
                    )
                inside = mixed[first : first + STEP, :]
                carried[rows, lanes] = (inside[:, n : 2 * n] * conv).astype(bf16)
                for i, value in enumerate((inside[:, :n], inside[:, n : 2 * n], inside[:, 2 * n :], conv)):
                    saved[i][rows, lanes] = value.astype(bf16)
            for i in range(kept):
                copy = pltpu.make_async_copy(
                    saved[i].at[:, pl.ds(s * n, n)],
                    results[i].at[:, pl.ds(s * n, n)],
                    saved_sems.at[kept * s + i],
                )
                copy.start()
                pending.append(copy)
        copy = pltpu.make_async_copy(carried, carried_hbm, in_sems.at[3])
        copy.start()
        pending.append(copy)
        loads[1].wait()
        loads[2].wait()
        for m in range(count // STEP):
            rows = slice(m * STEP, (m + 1) * STEP)
            term = dot_nt(carried[rows, :], outward[...])
            left = mine[rows, :].astype(f32) + term[:, :half]
            right = other[rows, :].astype(f32) + term[:, half:]
            rstd = inverse_rms(left, right)
            for i, value in enumerate((left, right)):
                lanes = slice(i * half, (i + 1) * half)
                hidden[rows, lanes] = value
                value = value * rstd * gain[:, lanes]
                normed2[rows, lanes] = value.astype(bf16)
                turned[lanes, rows] = value.T.astype(bf16)
            for i, (source, target, by) in enumerate(
                (
                    (hidden, hidden_hbm, 0),
                    (normed2, normed2_hbm, 0),
                    (turned, turned_hbm, 1),
                )
            ):
                here = pl.ds(m * STEP, STEP)
                source, target = (
                    (source.at[:, here], target.at[:, here])
                    if by
                    else (source.at[here], target.at[here])
                )
                copy = pltpu.make_async_copy(source, target, out_sems.at[3 * m + i])
                copy.start()
                pending.append(copy)
        for copy in pending:
            copy.wait()

    tiles = count // STEP
    wide = shape_of(count, width, dtype=f32)
    flat = shape_of(count, width)
    whole = pl.BlockSpec(memory_space=pltpu.VMEM)
    return call(
        body,
        "mix_forward",
        (flat, flat, flat, flat, wide, flat, flat, shape_of(width, count)),
        flops=8 * count * width * width,
        moved=30 * count * width + 8 * width * width,
        tie=tie,
        n_in=8,
        in_specs=[SCALARS] + [HERE] * 5 + [whole] * 2,
        out_specs=(HERE,) * 8,
        scratch_shapes=[
            pltpu.VMEM((HALO + count, width), bf16),
            pltpu.VMEM((width, 3 * width), bf16),
            pltpu.VMEM((width, width), bf16),
            pltpu.VMEM((count, half), bf16),
            pltpu.VMEM((count, half), bf16),
            pltpu.VMEM((HALO + count, 3 * n), f32),
            pltpu.VMEM((HALO + count, n), f32),
            pltpu.VMEM((count, width), bf16),
            pltpu.VMEM((count, width), f32),
            pltpu.VMEM((count, width), bf16),
            pltpu.VMEM((width, count), bf16),
        ]
        + [pltpu.VMEM((count, width), bf16)] * kept
        + [
            pltpu.SemaphoreType.DMA((4,)),
            pltpu.SemaphoreType.DMA((4 * BLOCKS,)),
            pltpu.SemaphoreType.DMA((kept * BLOCKS,)),
            pltpu.SemaphoreType.DMA((3 * tiles,)),
        ],
    )(place, normed, *halves, tokens, theirs, taps, gain, *tie)


def feed_body(
    lanes,
    started,
    normed_hbm,
    low_hbm,
    normed_t_hbm,
    low_t_hbm,
    own_hbm,
    other_hbm,
    grad_in,
    grad_hbm,
    acts_hbm,
    theirs_hbm,
    normed,
    low,
    normed_t,
    low_t,
    weights,
    grad,
    acts,
    theirs,
    in_sems,
    grad_sems,
    acts_sems,
    their_sems,
):
    f = lanes // 3
    count, width = normed.shape
    half = width // 2
    loads = [
        pltpu.make_async_copy(source, target, in_sems.at[i])
        for i, (source, target) in enumerate(
            (
                (normed_hbm, normed),
                (own_hbm, weights.at[pl.ds(0, half)]),
                (other_hbm, weights.at[pl.ds(half, half)]),
                (low_hbm, low),
                (normed_t_hbm.at[pl.ds(half, half)], normed_t),
                (low_t_hbm.at[pl.ds(half, half)], low_t),
            )
        )
    ]
    if started:
        loads.append(pltpu.make_async_copy(grad_in, grad, in_sems.at[6]))
    for load in loads[:4]:
        load.start()
    for load in loads[:4]:
        load.wait()
    for load in loads[4:]:
        load.start()

    def acts_copy(i):
        rows = rows_of(i)
        return pltpu.make_async_copy(acts.at[rows], acts_hbm.at[rows], acts_sems.at[i])

    def activations(i, carry):
        rows = rows_of(i)
        for start in range(0, f, 256):
            stop = min(start + 256, f)
            gate_lanes = slice(start, stop)
            up_lanes = slice(f + start, f + stop)
            down_lanes = slice(2 * f + start, 2 * f + stop)
            gate = dot(normed[rows, :], weights[:, gate_lanes])
            up_part = dot(normed[rows, :], weights[:, up_lanes])
            grad_active = dot(low[rows, :], weights[:, down_lanes])
            sigmoid_gate = jax.nn.sigmoid(gate)
            silu_gate = gate * sigmoid_gate
            acts[rows, gate_lanes] = (
                grad_active * up_part * sigmoid_gate * (1.0 + gate * (1.0 - sigmoid_gate))
            ).astype(bf16)
            acts[rows, up_lanes] = (grad_active * silu_gate).astype(bf16)
            acts[rows, down_lanes] = (silu_gate * up_part).astype(bf16)
        acts_copy(i).start()
        return carry

    lax.fori_loop(0, count // STEP, activations, 0)
    loads[4].wait()
    loads[5].wait()

    def their_copy(i):
        rows = rows_of(i)
        return pltpu.make_async_copy(theirs.at[rows], theirs_hbm.at[rows], their_sems.at[i])

    def outer(i, carry):
        rows = rows_of(i)
        theirs[rows, : 2 * f] = dot(normed_t[rows, :], acts[:, : 2 * f]).astype(bf16)
        theirs[rows, 2 * f :] = dot(low_t[rows, :], acts[:, 2 * f :]).astype(bf16)
        their_copy(i).start()
        return carry

    lax.fori_loop(0, half // STEP, outer, 0)
    if started:
        loads[6].wait()

    def grad_copy(i):
        rows = rows_of(i)
        return pltpu.make_async_copy(grad.at[rows], grad_hbm.at[rows], grad_sems.at[i])

    def inner(i, carry):
        rows = rows_of(i)
        term = dot_nt(acts[rows, : 2 * f], weights[:, : 2 * f])
        grad[rows, :] = grad[rows, :] + term if started else term
        grad_copy(i).start()
        return carry

    lax.fori_loop(0, count // STEP, inner, 0)
    for i in range(half // STEP):
        their_copy(i).wait()
    for i in range(count // STEP):
        acts_copy(i).wait()
        grad_copy(i).wait()


def feed(normed, low, normed_t, low_t, own, other, grad, tie):
    count, width = normed.shape
    half, lanes = own.shape
    f = lanes // 3
    started = grad is not None
    tiles = count // STEP
    before = [grad] if started else []
    body = functools.partial(feed_body, lanes, started)
    if not started:
        inner = body

        def body(*refs):
            inner(*refs[:6], None, *refs[6:])

    return call(
        body,
        "feed",
        (shape_of(count, width, dtype=f32), shape_of(count, lanes), shape_of(half, lanes)),
        flops=13 * count * width * f,
        moved=2 * (4 * count * width + 3 * half * lanes + count * lanes) + 8 * count * width,
        tie=tie,
        n_in=6 + len(before),
        in_specs=[HERE] * (6 + len(before)),
        out_specs=(HERE,) * 3,
        scratch_shapes=[
            pltpu.VMEM((count, width), bf16),
            pltpu.VMEM((count, width), bf16),
            pltpu.VMEM((half, count), bf16),
            pltpu.VMEM((half, count), bf16),
            pltpu.VMEM((width, lanes), bf16),
            pltpu.VMEM((count, width), f32),
            pltpu.VMEM((count, lanes), bf16),
            pltpu.VMEM((half, lanes), bf16),
            pltpu.SemaphoreType.DMA((7,)),
            pltpu.SemaphoreType.DMA((tiles,)),
            pltpu.SemaphoreType.DMA((tiles,)),
            pltpu.SemaphoreType.DMA((half // STEP,)),
        ],
    )(normed, low, normed_t, low_t, own, other, *before, *tie)


def feed_output(hidden, acts, owns, others, tie):
    count, width = hidden.shape
    half, lanes = owns[0].shape
    f = lanes // 3

    def body(hidden, *refs):
        acts, owns, others, outs = refs[:4], refs[4:8], refs[8:12], refs[12:]
        for side, weights in enumerate((owns, others)):
            total = hidden[:, side * half : (side + 1) * half]
            for k in range(BLOCKS):
                total = total + dot_nt(acts[k][...], weights[k][...])
            outs[side][...] = total.astype(bf16)

    rows = pl.BlockSpec((STEP, f), lambda m: (m, 2))
    whole = pl.BlockSpec((half, f), lambda m: (0, 2))
    part = pl.BlockSpec((STEP, half), lambda m: (m, 0))
    return call(
        body,
        "feed_output",
        (shape_of(count, half),) * 2,
        flops=2 * BLOCKS * count * width * f,
        moved=2 * BLOCKS * (count + width) * f + 6 * count * width,
        tie=tie,
        n_in=13,
        grid=(count // STEP,),
        in_specs=[pl.BlockSpec((STEP, width), lambda m: (m, 0))] + [rows] * 4 + [whole] * 8,
        out_specs=(part, part),
    )(hidden, *acts, *owns, *others, *tie)


def keep_and_send(place, total, keep, send):
    width = keep.shape[0] // 2
    for j in range(4):
        target = keep if j < 2 else send
        rows = pl.ds(pl.multiple_of(quarter_of(place, j) * width, width), width)
        target[(j % 2) * width : (j % 2 + 1) * width, :] = total[rows, :].astype(bf16)


def feed_weights(place, normed_t, low_t, acts, received, tie):
    width, count = normed_t.shape
    half, lanes = received.shape
    f = lanes // 3
    step = f

    def body(place, normed_t, low_t, acts, received, keep, send, total):
        def put(left):
            total[...] = dot(left[...], acts[...]) + received[...].astype(f32)

        is_down = pl.program_id(0) >= 2 * f // step

        @pl.when(jnp.logical_not(is_down))
        def _():
            put(normed_t)

        @pl.when(is_down)
        def _():
            put(low_t)

        keep_and_send(place, total, keep, send)

    left = pl.BlockSpec((half, count), lambda j, place: (0, 0))
    part = pl.BlockSpec((half // 2, step), lambda j, place: (0, j))
    return call(
        body,
        "feed_weights",
        (shape_of(half // 2, lanes),) * 2,
        flops=6 * count * half * f,
        moved=2 * (2 * half * count + count * lanes + 2 * half * lanes),
        tie=tie,
        n_in=5,
        grid_spec=scalar_grid(
            (lanes // step,),
            [
                left,
                left,
                pl.BlockSpec((count, step), lambda j, place: (0, j)),
                pl.BlockSpec((half, step), lambda j, place: (0, j)),
            ],
            [part, part],
            [pltpu.VMEM((half, step), f32)],
        ),
    )(place, normed_t, low_t, acts, received, *tie)


def hidden_backward(hidden, grad_normed, grad_out, gain):
    width = hidden.shape[1]
    rstd = lax.rsqrt(jnp.sum(hidden * hidden, axis=1, keepdims=True) / width + eps)
    scaled = grad_normed * gain
    mean = jnp.sum(scaled * hidden, axis=1, keepdims=True) / width
    grad = grad_out + (rstd * scaled - hidden * (rstd * rstd * rstd) * mean)
    return grad, grad_normed * hidden * rstd


def first_rows(hidden, grad_normed, low, gate_c, gain, halves):
    width = hidden.shape[1]
    n = width // BLOCKS
    half = width // 2

    def body(hidden, grad_normed, low, gate_c, gain, *refs):
        grad, _ = hidden_backward(hidden[...], grad_normed[...], low[...].astype(f32), gain[...])
        grad_o = grad.astype(bf16)
        for s in range(BLOCKS):
            value = dot(grad_o[:, :half], refs[0][s]) + dot(grad_o[:, half:], refs[1][s])
            lanes = slice(s * n, (s + 1) * n)
            refs[-1][:, lanes] = (value * gate_c[:, lanes].astype(f32))[:8]

    few = pl.BlockSpec((HALO, width), lambda i: (0, 0))
    return call(
        body,
        "first_rows",
        shape_of(8, width, dtype=f32),
        grid=(1,),
        in_specs=[few] * 4
        + [pl.BlockSpec((1, width), lambda i: (0, 0))]
        + [pl.BlockSpec((BLOCKS, half, n), lambda i: (0, 0, 3))] * 2,
        out_specs=pl.BlockSpec((8, width), lambda i: (0, 0)),
    )(hidden, grad_normed, low, gate_c, gain, *halves)


def mix_backward(
    place, hidden, grad_normed, low, tokens, theirs, saved, later, taps, gain_one, gain_two, halves, tie
):
    count, width = hidden.shape
    half = width // 2
    n = width // BLOCKS
    tiles = count // STEP

    def body(place, *refs):
        hidden, grad_normed, low, mine, other = refs[:5]
        gate_b, gate_c, value_part, conv, later, taps, gain_one, gain_two = refs[5:13]
        sources = refs[13:15]
        grad_own, grad_other, grads, turned, sums = refs[15:20]
        inward, outward, extended, sems = refs[20:]
        step = pl.program_id(0)
        tile = tiles - 1 - step

        @pl.when(step == 0)
        def _():
            copies = mix_copies(sources, inward, outward, sems)
            for copy in copies:
                copy.start()
            sums[...] = jnp.zeros_like(sums)
            extended[STEP:, :] = later[...]
            for copy in copies:
                copy.wait()

        @pl.when(step > 0)
        def _():
            extended[STEP:, :] = extended[:8, :]

        grad, gain_terms = hidden_backward(
            hidden[...], grad_normed[...], low[...].astype(f32), gain_two[...]
        )
        sums[1:2, :] += jnp.sum(gain_terms, axis=0, keepdims=True)
        grad_o = grad.astype(bf16)
        turned[...] = grad.T.astype(bf16)
        grad_carried = dot(grad_o, outward[...])
        extended[:STEP, :] = grad_carried * gate_c[...].astype(f32)
        grad_c = (grad_carried * conv[...].astype(f32)).astype(bf16)
        left_gate, right_gate = gate_b[...].astype(f32), value_part[...].astype(f32)
        product = left_gate * right_gate
        grad_product = jnp.zeros((STEP, width), f32)
        for lag in range(KCONV):
            slot, start = slots(place, tile * STEP + lag, STEP)
            keep = (slot - lag >= start).astype(f32)
            masked = keep * extended[lag : lag + STEP, :]
            grad_product = grad_product + taps[lag : lag + 1, :] * masked
            sums[2 + lag : 3 + lag, :] += jnp.sum(masked * product, axis=0, keepdims=True)
        grad_b = (grad_product * right_gate).astype(bf16)
        grad_v = (grad_product * left_gate).astype(bf16)
        for s in range(BLOCKS):
            lanes = slice(s * n, (s + 1) * n)
            at = s * 3 * n
            grads[:, at : at + n] = grad_b[:, lanes]
            grads[:, at + n : at + 2 * n] = grad_c[:, lanes]
            grads[:, at + 2 * n : at + 3 * n] = grad_v[:, lanes]
        grad_first = dot_nt(grads[...], inward[...])
        left, right = mine[...].astype(f32), other[...].astype(f32)
        rstd = inverse_rms(left, right)
        scaled = grad_first * gain_one[...]
        mean = (
            jnp.sum(scaled[:, :half] * left, axis=1, keepdims=True)
            + jnp.sum(scaled[:, half:] * right, axis=1, keepdims=True)
        ) / width
        for i, (value, target) in enumerate(((left, grad_own), (right, grad_other))):
            lanes = slice(i * half, (i + 1) * half)
            sums[0:1, lanes] += jnp.sum(grad_first[:, lanes] * value * rstd, axis=0, keepdims=True)
            target[...] = (
                grad[:, lanes] + (rstd * scaled[:, lanes] - value * (rstd * rstd * rstd) * mean)
            ).astype(bf16)

    def tile_of(m):
        return tiles - 1 - m

    rows = pl.BlockSpec((STEP, width), lambda m, place: (tile_of(m), 0))
    one = pl.BlockSpec((1, width), lambda m, place: (0, 0))
    eight = pl.BlockSpec((8, width), lambda m, place: (0, 0))
    narrow = pl.BlockSpec((STEP, half), lambda m, place: (tile_of(m), 0))
    return call(
        body,
        "mix_backward",
        (
            shape_of(count, half),
            shape_of(count, half),
            shape_of(count, 3 * width),
            shape_of(width, count),
            shape_of(8, width, dtype=f32),
        ),
        flops=8 * count * width * width,
        moved=44 * count * width,
        tie=tie,
        n_in=16,
        grid_spec=scalar_grid(
            (tiles,),
            [
                rows,
                rows,
                rows,
                pl.BlockSpec(
                    (STEP, half), lambda m, place: (place[1] * tiles + tile_of(m), 0)
                ),
                narrow,
                rows,
                rows,
                rows,
                rows,
                eight,
                pl.BlockSpec((KCONV, width), lambda m, place: (0, 0)),
                one,
                one,
            ]
            + [HERE] * 2,
            [
                narrow,
                narrow,
                pl.BlockSpec((STEP, 3 * width), lambda m, place: (tile_of(m), 0)),
                pl.BlockSpec((width, STEP), lambda m, place: (0, tile_of(m))),
                eight,
            ],
            [
                pltpu.VMEM((width, 3 * width), bf16),
                pltpu.VMEM((width, width), bf16),
                pltpu.VMEM((STEP + 8, width), f32),
                pltpu.SemaphoreType.DMA((4 * BLOCKS,)),
            ],
        ),
    )(
        place,
        hidden,
        grad_normed,
        low,
        tokens,
        theirs,
        *saved,
        later,
        taps,
        gain_one,
        gain_two,
        *halves,
        *tie,
    )


def mix_weights(place, normed_t, grad_t, grads, carried, received, tie):
    width, count = normed_t.shape
    half = width // 2
    n = width // BLOCKS
    side = 1 if received is None else 0

    def body(place, normed_t, grad_t, grads, carried, *refs):
        inward = dot(normed_t[...], grads[...])
        outward = dot(grad_t[...], carried[...])
        if received is None:
            out = refs[0]
            out[:, : 3 * n] = inward.astype(bf16)
            out[:, 3 * n :] = outward.astype(bf16)
        else:
            received_part, keep, send, total = refs
            total[:, : 3 * n] = inward + received_part[:, : 3 * n].astype(f32)
            total[:, 3 * n :] = outward + received_part[:, 3 * n :].astype(f32)
            keep_and_send(place, total, keep, send)

    left = pl.BlockSpec((half, count), lambda s, place: (side, 0))
    part = pl.BlockSpec((half, 4 * n), lambda s, place: (0, s))
    small = pl.BlockSpec((half // 2, 4 * n), lambda s, place: (0, s))
    more = [] if received is None else [received]
    return call(
        body,
        "mix_weights",
        (shape_of(half // 2, 4 * width),) * 2 if more else shape_of(half, 4 * width),
        flops=8 * count * half * width,
        moved=2 * (2 * half * count + (count + half) * 4 * width),
        tie=tie,
        n_in=5 + len(more),
        grid_spec=scalar_grid(
            (BLOCKS,),
            [
                left,
                left,
                pl.BlockSpec((count, 3 * n), lambda s, place: (0, s)),
                pl.BlockSpec((count, n), lambda s, place: (0, s)),
            ]
            + [part] * len(more),
            [small, small] if more else part,
            [pltpu.VMEM((half, 4 * n), f32)] if more else [],
        ),
    )(place, normed_t, grad_t, grads, carried, *more, *tie)


def after(value, *earlier):
    return lax.optimization_barrier((value, *earlier))[0]


def swap_cores(value):
    return lax.ppermute(value, "col", [(0, 1), (1, 0)])


def across_first(value):
    return lax.ppermute(
        value, ("dp", "col"), [(2 * p + c, 2 * (p ^ (1 << c)) + c) for p in range(4) for c in range(2)]
    )


def across_second(value):
    return lax.ppermute(
        value, ("dp", "col"), [(2 * p + c, 2 * (p ^ (2 >> c)) + c) for p in range(4) for c in range(2)]
    )


def along_row(value, steps):
    return lax.ppermute(value, "row", [(i, (i + steps) % BLOCKS) for i in range(BLOCKS)])


def quarters(part):
    across = across_first(part)
    return (part, across, across_second(part), across_second(across))


def add(*parts):
    return sum(part.astype(f32) for part in parts).astype(bf16)


def upper(value):
    return value[: value.shape[0] // 2]


def lower(value):
    return value[value.shape[0] // 2 :]


def block_of(value, b, axis=0):
    width = value.shape[axis] // BLOCKS
    return lax.dynamic_slice_in_dim(value, b * width, width, axis)


def later_rows(value):
    pairs = [(i, i - 1) for i in range(1, 2 * BLOCKS)]
    value = lax.ppermute(value, ("row", "col"), pairs)
    parts = jnp.split(value, BLOCKS, axis=1)
    order = [OFFSETS.index(offset % BLOCKS - 1) for offset in OFFSETS]
    moved = jnp.concatenate([parts[i] for i in order], axis=1)
    return jnp.where(lax.axis_index("col") == 1, moved, value)


def shards(
    tokens,
    cotangent,
    seq_lens,
    norm1_gain,
    in_weight,
    conv_weight,
    out_weight,
    norm2_gain,
    gate_up_weight,
    down_weight,
):
    dp, row, core = lax.axis_index("dp"), lax.axis_index("row"), lax.axis_index("col")
    count, half = tokens.shape[0] // 2, tokens.shape[1]
    position = ((dp * BLOCKS + row) * 2 + core) * count
    lengths = lax.dynamic_slice_in_dim(seq_lens, position // ROW_LEN, 1, 0)[0]
    place = jnp.stack(
        [dp, core, position % ROW_LEN, lengths[0], lengths[0] + lengths[1]]
    ).astype(jnp.int32)

    def of_the_other(value):
        return lax.dynamic_slice_in_dim(value, (1 - core) * count, count, 0)

    mix_first = pack(in_weight, out_weight, place, 1, conv_weight)
    mix_quarters = [along_row(mix_first, -offset) for offset in OFFSETS[1:]]
    own_gains = jnp.pad(jnp.stack([norm1_gain, norm2_gain]), ((0, HALO - 2), (0, 0)))
    mix_own = pack(in_weight, out_weight, place, 4, tie=[mix_first])
    feed_own = pack(gate_up_weight, down_weight, place, 4, tie=[mix_own])
    before = lax.ppermute(
        after(tokens[2 * count - HALO :], mix_own), "row", [(i, i + 1) for i in range(BLOCKS - 1)]
    )
    joined = join_rows(mix_quarters, [mix_own, feed_own])
    theirs = swap_cores(outgoing(place, tokens, cotangent, before, own_gains, [joined]))
    feed_first = pack(gate_up_weight, down_weight, place, 1, tie=[joined])
    gains = jnp.concatenate([own_gains[:2], theirs[2 * count + HALO :][:2]], axis=1).astype(f32)
    gain_one, gain_two = gains[:1], gains[1:]
    normed, normed_t, low, low_t = prepare(
        place, tokens, theirs, before, cotangent, gain_one, [joined]
    )
    width = half // 4
    taps = jnp.concatenate(
        [conv_weight] + [part[width : width + KCONV, : conv_weight.shape[1]] for part in mix_quarters],
        axis=1,
    ).astype(f32)
    quarter_one = along_row(feed_first, -OFFSETS[1])
    mix_half = mix_assemble(mix_own, quarters(joined), place, [normed, quarter_one])
    mix_halves = [mix_half, swap_cores(mix_half)]
    half_one = lax.all_gather(after(quarter_one, mix_half), "dp", axis=0, tiled=True)

    *saved, hidden, carried, normed_two, normed_two_t = mix_forward(
        place, normed, mix_halves, tokens, theirs, taps, gain_two, []
    )
    feed_halves, others = [feed_own], [swap_cores(feed_own)]
    activations, from_them = [], []

    def gathered(k, last, here):
        part = along_row(after(feed_first, last), -OFFSETS[k])
        return lax.all_gather(after(part, here), "dp", axis=0, tiled=True)

    def have(half):
        feed_halves.append(half)
        others.append(swap_cores(half))

    def activate(grad, tie):
        k = len(activations)
        grad, acts, for_them = feed(
            normed_two, low, normed_two_t, low_t, feed_halves[k], others[k], grad, tie
        )
        activations.append(acts)
        from_them.append(swap_cores(for_them))
        return grad, for_them

    def weights_of(k, tie):
        keep, send = feed_weights(place, normed_two_t, low_t, activations[k], from_them[k], tie)
        return keep, across_second(send)

    grad_normed_two, done = activate(None, [])
    half_two = gathered(2, mix_half, done)
    have(after(half_one, done))
    grad_normed_two, last = activate(grad_normed_two, [])
    half_three = gathered(3, done, last)
    done = last
    keep, send = weights_of(0, [done])
    have(after(half_two, keep))
    grad_normed_two, done = activate(grad_normed_two, [keep])
    zero = (keep, send)
    keep, send = weights_of(1, [done, send])
    one = (keep, send)
    keep, send = weights_of(2, [keep])
    two = (keep, send)
    have(after(half_three, one[0]))
    grad_normed_two, done = activate(grad_normed_two, [keep])
    one_low, two_low = add(*map(lower, one)), add(*map(lower, two))
    one_across, two_across = across_first(one_low), across_first(two_low)
    first = first_rows(hidden, grad_normed_two, low, saved[1], gain_two, mix_halves)
    later = later_rows(first)
    keep, send = weights_of(3, [first, one_low, two_low])
    one = add(*map(upper, one), one_across)
    two = add(*map(upper, two), two_across)
    zero_across = across_first(after(add(*map(lower, zero)), keep))

    grad_own, grad_other, grads, grad_t, sums = mix_backward(
        place,
        hidden,
        grad_normed_two,
        low,
        tokens,
        theirs,
        saved,
        later,
        taps,
        gain_one,
        gain_two,
        mix_halves,
        [keep, one, two],
    )
    three = (keep, send)
    three_low = add(*map(lower, three))
    one, two = along_row(one, OFFSETS[1]), along_row(two, OFFSETS[2])
    where = jnp.array([OFFSETS.index(offset) for offset in (0, 1, 2, -1)], jnp.int32)
    own_taps = jnp.concatenate(
        [block_of(sums[2:], where[(b - row) % BLOCKS], 1) for b in range(BLOCKS)], axis=1
    )
    packed_sums = jnp.concatenate([sums[:2], own_taps], axis=0)
    every = lax.all_gather(packed_sums, ("dp", "row", "col"), axis=0)

    for_them = mix_weights(place, normed_t, grad_t, grads, carried, None, [one, three_low, packed_sums])
    received = swap_cores(for_them)
    three = add(*map(upper, three), across_first(three_low))
    grad_theirs = swap_cores(grad_other)
    input_back = join_tokens(grad_own, after(grad_theirs, for_them), place)
    keep, send = mix_weights(
        place, normed_t, grad_t, grads, carried, received, [three, two, input_back]
    )
    send = across_second(send)
    three = along_row(three, OFFSETS[3])
    own_out, other_out = feed_output(hidden, activations, feed_halves, others, [keep])
    send = after(send, own_out)
    other_out = swap_cores(other_out)
    mix_low = add(lower(keep), lower(send))
    mix_across = across_first(mix_low)
    three = after(three, mix_low)
    feed_sum = quarters(add(*map(upper, zero), zero_across, one, two, three))
    mix_quarters = jnp.split(add(upper(keep), upper(send), mix_across), BLOCKS, axis=1)
    mix_quarters = [along_row(part, OFFSETS[k]) if k else part for k, part in enumerate(mix_quarters)]
    mix_sum = quarters(add(*mix_quarters))
    output_back = join_tokens(own_out, other_out, place)
    gate_up_grad, down_grad = unpack(feed_sum, 2, place)
    in_grad, out_grad = unpack(mix_sum, 3, place)
    every = after(every, mix_sum[0])
    sums = jnp.sum(every.reshape(16, 2, *packed_sums.shape), axis=0)
    mine, other = sums[core], sums[1 - core]
    gain_grads = mine[:2, :half] + other[:2, half:]
    taps_grad = block_of(mine[2 : 2 + KCONV] + other[2 : 2 + KCONV], row, 1)
    return (
        output_back,
        input_back,
        gain_grads[0],
        in_grad,
        taps_grad,
        out_grad,
        gain_grads[1],
        gate_up_grad,
        down_grad,
    )


def from_behind(value, axis, steps):
    count = lax.axis_size(axis)
    leading, last = (max(0, -steps), min(count, count - steps))
    return lax.ppermute(value, axis, [(source, source + steps) for source in range(leading, last)])


def token_index(count, extra):
    flat_rank = (
        lax.axis_index("dp") * lax.axis_size("row") + lax.axis_index("row")
    ) * lax.axis_size("col") + lax.axis_index("col")
    return flat_rank * count + jnp.arange(count + extra, dtype=jnp.int32)


def flat_slot_masks(seq_lens, count, extra):
    position = token_index(count, extra)
    packed = position // ROW_LEN
    place = position - packed * ROW_LEN
    table = (packed[:, None] == jnp.arange(seq_lens.shape[0], dtype=jnp.int32)[None, :]).astype(
        jnp.int32
    )
    first = jnp.sum(table * seq_lens[None, :, 0], axis=1)
    second = jnp.sum(table * seq_lens[None, :, 1], axis=1)
    start = jnp.where(place < first, 0, first)
    valid_slot = (place < first + second).astype(jnp.float32)
    keep_masks = jnp.stack([(place - lag >= start).astype(jnp.float32) for lag in range(KCONV)])
    return (valid_slot[:count], keep_masks)


def collect(
    norm1_gain, in_weight, conv_weight, out_weight, norm2_gain, gate_up_weight, down_weight
):
    in_rows, conv_full, out_rows, gate_rows, down_rows = (
        lax.all_gather(in_weight, "row", axis=2, tiled=True),
        lax.all_gather(conv_weight, "row", axis=1, tiled=True),
        lax.all_gather(out_weight, "row", axis=0, tiled=True),
        lax.all_gather(gate_up_weight, "row", axis=2, tiled=True),
        lax.all_gather(down_weight, "row", axis=0, tiled=True),
    )
    gain_first, in_full, out_full, gain_second, gate_full, down_full = (
        lax.all_gather(norm1_gain, "col", axis=0, tiled=True),
        lax.all_gather(in_rows, "col", axis=1, tiled=True),
        lax.all_gather(out_rows, "col", axis=1, tiled=True),
        lax.all_gather(norm2_gain, "col", axis=0, tiled=True),
        lax.all_gather(gate_rows, "col", axis=1, tiled=True),
        lax.all_gather(down_rows, "col", axis=1, tiled=True),
    )
    return (gain_first, in_full, conv_full, out_full, gain_second, gate_full, down_full)


def flat_norm_backward(values, rstd, gain, grad_normed):
    scaled = grad_normed * gain
    gain_grad = jnp.sum(grad_normed * values * rstd, axis=0)
    grad_values = rstd * scaled - values * (rstd * rstd * rstd) * jnp.mean(
        scaled * values, axis=1, keepdims=True
    )
    return (grad_values, gain_grad)


def project(left, right):
    return jnp.dot(left, right, preferred_element_type=jnp.float32)


def weight_grad(left, right):
    return jnp.einsum("td,te->de", left, right, preferred_element_type=jnp.float32)


def back_project(grad, matrix):
    return jnp.einsum("te,de->td", grad, matrix, preferred_element_type=jnp.float32)


def flat_shards(
    tokens,
    cotangent,
    seq_lens,
    norm1_gain,
    in_weight,
    conv_weight,
    out_weight,
    norm2_gain,
    gate_up_weight,
    down_weight,
):
    own_tokens, own_cotangent = (
        lax.all_to_all(tokens, "col", split_axis=0, concat_axis=1, tiled=True),
        lax.all_to_all(cotangent, "col", split_axis=0, concat_axis=1, tiled=True),
    )
    gain_first, in_full, conv_full, out_full, gain_second, gate_full, down_full = collect(
        norm1_gain, in_weight, conv_weight, out_weight, norm2_gain, gate_up_weight, down_weight
    )
    count, width = own_tokens.shape
    reach = KCONV - 1
    valid_slot, keep_masks = flat_slot_masks(seq_lens, count, reach)
    conv_taps = conv_full.astype(jnp.float32)
    gain_one_f = gain_first.astype(jnp.float32)
    gain_two_f = gain_second.astype(jnp.float32)
    inputs = own_tokens.astype(jnp.float32)
    rstd_first = lax.rsqrt(jnp.mean(inputs * inputs, axis=1, keepdims=True) + eps)
    normed = (inputs * rstd_first * gain_one_f).astype(jnp.bfloat16)
    gate_b = project(normed, in_full[0])
    gate_c = project(normed, in_full[1])
    value_part = project(normed, in_full[2])
    product = gate_b * value_part
    earlier = from_behind(product[count - reach :], ("row", "col"), 1)
    extended = jnp.concatenate([earlier, product], axis=0)
    conv = jnp.zeros((count, width), jnp.float32)
    for lag in range(KCONV):
        conv = (
            conv
            + conv_taps[lag]
            * keep_masks[lag, :count, None]
            * extended[reach - lag : reach - lag + count]
        )
    carried = (gate_c * conv).astype(jnp.bfloat16)
    hidden = inputs + project(carried, out_full)
    rstd_second = lax.rsqrt(jnp.mean(hidden * hidden, axis=1, keepdims=True) + eps)
    normed_two = (hidden * rstd_second * gain_two_f).astype(jnp.bfloat16)
    gate = project(normed_two, gate_full[0])
    up_part = project(normed_two, gate_full[1])
    sigmoid_gate = jax.nn.sigmoid(gate)
    silu_gate = gate * sigmoid_gate
    active = (silu_gate * up_part).astype(jnp.bfloat16)
    output = hidden + project(active, down_full)
    grad_out = own_cotangent.astype(jnp.float32) * valid_slot[:, None]
    grad_low = grad_out.astype(jnp.bfloat16)
    down_grad = weight_grad(active, grad_low)
    grad_active = back_project(grad_low, down_full)
    grad_gate = (grad_active * up_part * sigmoid_gate * (1.0 + gate * (1.0 - sigmoid_gate))).astype(
        jnp.bfloat16
    )
    grad_up = (grad_active * silu_gate).astype(jnp.bfloat16)
    gate_grad = jnp.stack([weight_grad(normed_two, grad_gate), weight_grad(normed_two, grad_up)])
    grad_normed_two = back_project(grad_gate, gate_full[0]) + back_project(grad_up, gate_full[1])
    grad_second, gain_second_part = flat_norm_backward(hidden, rstd_second, gain_two_f, grad_normed_two)
    grad_hidden = grad_out + grad_second
    grad_o = grad_hidden.astype(jnp.bfloat16)
    out_grad = weight_grad(carried, grad_o)
    grad_carried = back_project(grad_o, out_full)
    grad_gate_c = (grad_carried * conv).astype(jnp.bfloat16)
    grad_conv = grad_carried * gate_c
    later = from_behind(grad_conv[:reach], ("row", "col"), -1)
    grad_extended = jnp.concatenate([grad_conv, later], axis=0)
    grad_product = jnp.zeros((count, width), jnp.float32)
    conv_rows = []
    for lag in range(KCONV):
        masked = keep_masks[lag, :, None] * grad_extended
        grad_product = grad_product + conv_taps[lag] * masked[lag : lag + count]
        conv_rows.append(
            jnp.sum(masked[:count] * extended[reach - lag : reach - lag + count], axis=0)
        )
    conv_grad = jnp.stack(conv_rows)
    grad_gate_b = (grad_product * value_part).astype(jnp.bfloat16)
    grad_value = (grad_product * gate_b).astype(jnp.bfloat16)
    in_grad = jnp.stack(
        [
            weight_grad(normed, grad_gate_b),
            weight_grad(normed, grad_gate_c),
            weight_grad(normed, grad_value),
        ]
    )
    grad_normed = (
        back_project(grad_gate_b, in_full[0])
        + back_project(grad_gate_c, in_full[1])
        + back_project(grad_value, in_full[2])
    )
    grad_first, gain_first_part = flat_norm_backward(inputs, rstd_first, gain_one_f, grad_normed)
    input_grad = (grad_hidden + grad_first).astype(jnp.bfloat16)
    output_back, input_back = (
        lax.all_to_all(output.astype(jnp.bfloat16), "col", split_axis=1, concat_axis=0, tiled=True),
        lax.all_to_all(input_grad, "col", split_axis=1, concat_axis=0, tiled=True),
    )
    in_cols, out_cols, gate_cols, down_cols = (
        lax.psum_scatter(in_grad, "col", scatter_dimension=1, tiled=True),
        lax.psum_scatter(out_grad, "col", scatter_dimension=1, tiled=True),
        lax.psum_scatter(gate_grad, "col", scatter_dimension=1, tiled=True),
        lax.psum_scatter(down_grad, "col", scatter_dimension=1, tiled=True),
    )
    in_part, out_part, gate_part, down_part = (
        lax.psum_scatter(in_cols, "row", scatter_dimension=2, tiled=True),
        lax.psum_scatter(out_cols, "row", scatter_dimension=0, tiled=True),
        lax.psum_scatter(gate_cols, "row", scatter_dimension=2, tiled=True),
        lax.psum_scatter(down_cols, "row", scatter_dimension=0, tiled=True),
    )
    in_sum, out_sum, gate_sum, down_sum = lax.psum((in_part, out_part, gate_part, down_part), "dp")
    gain_one_sum, gain_two_sum, conv_sum = lax.psum(
        (gain_first_part, gain_second_part, conv_grad), ("dp", "row", "col")
    )
    col_width = width // lax.axis_size("col")
    row_width = width // lax.axis_size("row")
    gain_first_grad = lax.dynamic_slice_in_dim(
        gain_one_sum, lax.axis_index("col") * col_width, col_width
    )
    gain_second_grad = lax.dynamic_slice_in_dim(
        gain_two_sum, lax.axis_index("col") * col_width, col_width
    )
    conv_weight_grad = lax.dynamic_slice_in_dim(
        conv_sum, lax.axis_index("row") * row_width, row_width, axis=1
    )
    return (
        output_back,
        input_back,
        gain_first_grad,
        in_sum,
        conv_weight_grad,
        out_sum,
        gain_second_grad,
        gate_sum,
        down_sum,
    )


def solution(mesh):
    ring = mesh.shape["dp"] == 4 and mesh.shape["row"] == BLOCKS and mesh.shape["col"] == 2
    return jax.shard_map(
        shards if ring else flat_shards,
        mesh=mesh,
        in_specs=(
            P(("dp", "row"), "col"),
            P(("dp", "row"), "col"),
            P(),
            P("col"),
            P(None, "col", "row"),
            P(None, "row"),
            P("row", "col"),
            P("col"),
            P(None, "col", "row"),
            P("row", "col"),
        ),
        out_specs=(
            P(("dp", "row"), "col"),
            P(("dp", "row"), "col"),
            P("col"),
            P(None, "col", "row"),
            P(None, "row"),
            P("row", "col"),
            P("col"),
            P(None, "col", "row"),
            P("row", "col"),
        ),
        check_vma=False,
    )
```
